256 devices in a mesh: field: 8 (over x, core), row: 32 (over z, y).
Axes of the slice: x: 4, y: 4, z: 8, core: 2. Of those that a mesh axis runs over, the one named last changes fastest.
Arguments:
- row_owner: int32 [8192, 32, 1], P('row'), may hold values from 0 to 31; in each aligned block of 8192 rows (0 to 8191, 8192 to 16383, ..., all dimensions but the last counted through in order) at most 512 rows name the same one
- row_slot: int32 [8192, 32], P('row'), may hold values from 0 to 1023
- feature_table: bfloat16 [32768, 2048], P('row', 'field'), may hold values from -2 to 2
- w_first: bfloat16 [32, 32, 2048], replicated, may hold values from -0.25 to 0.25
- w_hidden: bfloat16 [2, 2048, 2048], P(None, 'field'), may hold values from -0.1875 to 0.1875
- w_out: bfloat16 [2048], replicated, may hold values from -0.1875 to 0.1875
Outputs:
- logits: float32 [8192], P('row')
The draws below stay inside these ranges and needn't reach their ends.
Inputs may be any that keep to these rules, and one draw needn't show every extreme that they name: `row_owner`: in the 8192 lookups of one device's samples (aligned blocks of samples), no owner is named more than 512 times, a bound that some block reaches.
All inputs are finite; a program needn't handle non-finite values.
Results may differ from the reference program's by a relative error of at most 0.0086.
Values may be sent and summed in bfloat16 or wider, within the bound.
No kernel may reach another device: no remote copies, remote signals or barrier semaphores. Data moves between devices by JAX's collectives and lax.ppermute only.
A program may use at most 128 MiB of HBM per device.

```python
import math
import jax
import jax.numpy as jnp
import numpy as np
from jax import lax

F = 32
K = 64
H = 2048
LAYERS = 2
B_DEV = 256
ROWS_DEV = 1024
SAMPLES = 8192
ROWS = 32768
CAP = 512
N_ROW = 32


def place_ends(result, own_key, least, largest):
    spot = [jax.random.randint(jax.random.fold_in(own_key, axis), (), 0, length) for axis, length in enumerate(result.shape)]
    longest = result.shape.index(max(result.shape))
    beside = spot[:longest] + [(spot[longest] + 1) % result.shape[longest]] + spot[longest + 1:]
    return result.at[tuple(spot)].set(least).at[tuple(beside)].set(largest)


def steps_of(rng, shape, split, smallest, top_value):
    level = 1.0
    for dim, parts in split:
        steps = jax.random.uniform(jax.random.fold_in(jax.random.fold_in(rng, 6), dim), (parts,), jnp.float32, smallest / len(split), top_value / len(split))
        level = level * jnp.repeat(jnp.exp(steps), shape[dim] // parts).reshape((-1,) + (1,) * (len(shape) - 1 - dim))
    return level


def shared_out(stream_key, own, number, rows, amount, top, limit, lean):
    order = jax.random.permutation(stream_key, amount)
    crowded, common = shares(amount, rows * top, limit, lean, True), shares(amount, rows * top, limit, lean, False)
    places = jnp.arange(amount)

    def named(sizes, offset_by):
        used = int((sizes > 0).sum())
        fixed = max(1, used // 4)
        shifted = fixed + (places - fixed + offset_by * (used - fixed)) % max(1, amount - fixed)
        return jnp.zeros((amount,), jnp.int32).at[order[jnp.where(places < fixed, places, shifted)]].set(jnp.asarray(sizes, jnp.int32))

    sizes = jnp.where(number % 4 == 0, named(crowded, number // 4), named(common, number - number // 4 - 1))
    mixed = jax.random.permutation(jax.random.fold_in(own, 3), amount)
    donor, taker = mixed[0:amount // 2 * 2:2], mixed[1:amount // 2 * 2:2]
    slack = jnp.minimum(sizes[donor] - 1, limit - sizes[taker]) // 2
    slack = jnp.where((donor == order[0]) | (taker == order[0]) | (sizes[taker] == 0), 0, jnp.maximum(slack, 0))
    shifted = jax.random.randint(jax.random.fold_in(own, 4), (amount // 2,), 0, 1 << 20) % (slack + 1)
    sizes = sizes.at[donor].add(-shifted).at[taker].add(shifted)
    members = jnp.searchsorted(jnp.cumsum(sizes), jnp.arange(rows * top), side="right").astype(jnp.int32)
    table = members.reshape(top, rows).T
    table = table[jax.random.permutation(jax.random.fold_in(own, 1), rows)]
    offset_by = jax.random.randint(jax.random.fold_in(own, 2), (rows, 1), 0, top)
    return jnp.take_along_axis(table, (jnp.arange(top)[None, :] + offset_by) % top, axis=1)


def shares(amount, total, most, lean, full):
    weights = [(1 << 20) // math.isqrt(rank ** lean) + 1 for rank in range(1, amount + 1)]
    largest = most if full else min(most, max(-(-total // amount), total * weights[0] // sum(weights)))
    least = 1 if total - largest >= amount - 1 else 0
    counts, rest = [largest] + [least] * (amount - 1), total - largest - least * (amount - 1)
    while rest > 0:
        movable = [i for i in range(1, amount) if counts[i] < largest] or [i for i in range(1, amount) if counts[i] < most]
        pool, budget = sum([weights[i] for i in movable]), rest
        for i in movable:
            more = min(most - counts[i], max(1, budget * weights[i] // pool), rest)
            counts[i] = counts[i] + more
            rest = rest - more
    return np.array(counts)


def centred(key, shape, spread, reach, pieces=(), dtype=jnp.bfloat16):
    values = spread * jax.random.normal(key, shape, jnp.float32)
    if pieces:
        values = values * steps_of(key, shape, pieces, -0.22, 0.18)
    return jnp.clip(values, -reach, reach).astype(dtype)


def setup_inputs(seed: int = 0) -> dict:
    key_list = jax.random.split(jax.random.key(seed), 7)
    row_owner_keys = jax.random.split(jax.random.fold_in(key_list[0], 1), SAMPLES * F // (B_DEV * F))
    row_owner_turns = jax.random.permutation(jax.random.fold_in(key_list[0], 3), SAMPLES * F // (B_DEV * F))
    row_owner = jax.vmap(lambda own, number: shared_out(jax.random.fold_in(key_list[0], 2), own, number, B_DEV * F, N_ROW, 1, CAP, 1))(row_owner_keys, row_owner_turns).reshape((SAMPLES, F, 1))
    row_slot = place_ends(jax.random.randint(key_list[1], (SAMPLES, F), 0, ROWS_DEV), jax.random.fold_in(key_list[1], 1), 0, ROWS_DEV - 1).astype(jnp.int32)
    feature_table = centred(key_list[2], (ROWS, F * K), 0.35, 2.0, ((0, 32), (1, 8)))
    w_first = centred(key_list[3], (F, F, H), (F * (F - 1) // 2) ** -0.5, 0.25)
    w_hidden = centred(key_list[4], (LAYERS, H, H), (H // 2) ** -0.5, 0.1875, ((1, 8),))
    w_out = centred(key_list[5], (H,), (H // 2) ** -0.5, 0.1875)
    return dict(row_owner=row_owner, row_slot=row_slot, feature_table=feature_table, w_first=w_first, w_hidden=w_hidden, w_out=w_out)


def reference(row_owner, row_slot, feature_table, w_first, w_hidden, w_out):
    row_ids = (row_owner[:, :, 0] * ROWS_DEV + row_slot).astype(jnp.int32)
    upper_pairs = jnp.arange(F)[:, None] < jnp.arange(F)[None, :]

    def score_block(block_ids):
        gathered = jnp.take(feature_table, block_ids.reshape(-1), axis=0).astype(jnp.float32)
        vectors = gathered.reshape(block_ids.shape[0], F, F, K)
        pair_dots = jnp.einsum("bijk,bjik->bij", vectors, vectors, precision=lax.Precision.HIGHEST).astype(jnp.bfloat16)
        pair_dots = jnp.where(upper_pairs[None], pair_dots, jnp.zeros_like(pair_dots))
        hidden = jnp.dot(pair_dots.reshape(-1, F * F), w_first.reshape(F * F, H), preferred_element_type=jnp.float32)
        hidden = jax.nn.relu(hidden).astype(jnp.bfloat16)
        for depth in range(LAYERS):
            hidden = jax.nn.relu(jnp.dot(hidden, w_hidden[depth], preferred_element_type=jnp.float32)).astype(jnp.bfloat16)
        return jnp.dot(hidden, w_out, preferred_element_type=jnp.float32)

    blocks = row_ids.reshape(N_ROW, B_DEV, F)
    return lax.map(score_block, blocks).reshape(-1)
```

```python
import functools

import jax
import jax.numpy as jnp
from jax import lax
from jax.experimental import pallas as pl
from jax.experimental.pallas import tpu as pltpu
from jax.sharding import PartitionSpec as P

F = 32
K = 64
H = 2048
NZ = 8
NY = 4
GROUPS = 8
PER = 4
HALF = 128

DIRECTIONS = ((1, 0), (-1, 0), (0, 1), (0, -1))
SPREAD = (
    ((2, (0, 0), (0, 1)), (0, (0, 0), (1, 0)), (3, (0, 0), (0, 3)), (1, (0, 0), (7, 0))),
    ((1, (0, 1), (7, 1)), (0, (1, 0), (2, 0)), (3, (1, 0), (1, 3)), (2, (1, 0), (1, 1))),
    ((0, (2, 0), (3, 0)), (3, (7, 0), (7, 3)), (1, (7, 0), (6, 0)), (2, (0, 1), (0, 2))),
    ((2, (7, 1), (7, 2)), (1, (7, 1), (6, 1)), (0, (1, 3), (2, 3)), (3, (1, 3), (1, 2))),
    ((0, (3, 0), (4, 0)), (3, (6, 0), (6, 3)), (2, (3, 0), (3, 1)), (1, (6, 0), (5, 0))),
    ((3, (2, 3), (2, 2)), (1, (6, 1), (5, 1)), (2, (6, 1), (6, 2)), (0, (2, 3), (3, 3))),
    ((1, (3, 1), (2, 1)), (2, (3, 1), (3, 2)), (0, (3, 1), (4, 1)), (3, (4, 0), (4, 3))),
    ((2, (5, 1), (5, 2)), (3, (5, 0), (5, 3)), (0, (3, 2), (4, 2))),
)


def step_pairs(direction):
    dz, dy = direction
    return [
        (z * NY + y, ((z + dz) % NZ) * NY + (y + dy) % NY) for z in range(NZ) for y in range(NY)
    ]


def spread_shard(own):
    pieces = {(0, 0): own}
    for step in SPREAD:
        for way, source, target in step:
            pieces[target] = lax.ppermute(pieces[source], "row", step_pairs(DIRECTIONS[way]))
    return [pieces[(dz, dy)] for dz in range(NZ) for dy in range(NY)]


def gather_kernel(count, rows, index, *refs):
    pieces, out, table, sems = refs[:-3], refs[-3], refs[-2], refs[-1]
    copies = [
        pltpu.make_async_copy(piece, table.at[pl.ds(n * rows, rows)], sems.at[n])
        for n, piece in enumerate(pieces)
    ]
    for copy in copies:
        copy.start()
    for copy in copies:
        copy.wait()
    unroll = 32

    def some(i, carry):
        first = i * unroll
        for u in range(unroll):
            out[first + u] = table[index[first + u]]
        return carry

    lax.fori_loop(0, count // unroll, some, 0)


def gather_rows(index, pieces, name):
    count = index.shape[0]
    rows = pieces[0].shape[0]
    total = rows * len(pieces)
    return pl.pallas_call(
        functools.partial(gather_kernel, count, rows),
        out_shape=jax.ShapeDtypeStruct((count, 2, 128), jnp.bfloat16),
        grid_spec=pltpu.PrefetchScalarGridSpec(
            num_scalar_prefetch=1,
            grid=(),
            in_specs=[pl.BlockSpec(memory_space=pl.ANY)] * len(pieces),
            out_specs=pl.BlockSpec(memory_space=pltpu.VMEM),
            scratch_shapes=[
                pltpu.VMEM((total, 2, 128), jnp.bfloat16),
                pltpu.SemaphoreType.DMA((len(pieces),)),
            ],
        ),
        compiler_params=pltpu.CompilerParams(vmem_limit_bytes=30 << 20),
        cost_estimate=pl.CostEstimate(flops=0, bytes_accessed=total * 512, transcendentals=0),
        name=name,
    )(index, *pieces)


def pair_kernel(me_ref, local_ref, other_ref, out_ref, sums_ref):
    me = me_ref[0]
    rows = 2 * HALF
    lane = lax.broadcasted_iota(jnp.int32, (rows, 128), 1)
    block = lane // 32
    unit = lane // 16
    inner = lane % 16
    depth = lax.broadcasted_iota(jnp.int32, (512, 128), 0)
    column = lax.broadcasted_iota(jnp.int32, (512, 128), 1)
    turn = depth // 128
    second = (depth % 128) // 32
    place = ((second + turn) % PER) * PER + second
    collect = jnp.where(column % 16 == place, 1.0, 0.0).astype(jnp.bfloat16)

    def choose(tiles, offsets):
        value = tiles[offsets[3]]
        for b in (2, 1, 0):
            value = jnp.where(block == b, tiles[offsets[b]], value)
        return value

    def products(first, second):
        high, low = [], []
        for d in range(PER):
            left = choose(first, [(b + d) % PER for b in range(PER)])
            right = choose(second, [(b - d) % PER for b in range(PER)])
            if d:
                right = pltpu.roll(right, 128 - 32 * d, 1)
            value = left * right
            rounded = value.astype(jnp.bfloat16)
            high.append(rounded)
            low.append((value - rounded.astype(jnp.float32)).astype(jnp.bfloat16))
        high = jnp.concatenate(high, axis=1)
        low = jnp.concatenate(low, axis=1)
        return jnp.dot(high, collect, preferred_element_type=jnp.float32) + jnp.dot(
            low, collect, preferred_element_type=jnp.float32
        )

    def tiles(ref, a):
        return [ref[a, n].astype(jnp.float32) for n in range(PER)]

    total = jnp.zeros((rows, 128), jnp.float32)
    for a in range(GROUPS):
        dots = products(tiles(local_ref, a), tiles(other_ref, a))
        total = total + jnp.where(unit == a, dots, 0.0)
    own_first = tiles(other_ref, me)
    own_second = tiles(local_ref, me)
    first_dots = products(own_first, own_first)
    second_dots = products(own_second, own_second)
    i, j = inner // PER, inner % PER
    zero = jnp.zeros_like(total)
    sums_ref[0] = jnp.where(
        unit < me, total, jnp.where((unit == me) & (i < j), first_dots, zero)
    )
    sums_ref[1] = jnp.where(
        unit > me, total, jnp.where((unit == me) & (i > j), second_dots, zero)
    )
    for half in range(2):
        value = sums_ref[half, pl.ds(0, HALF, stride=2), :] + sums_ref[
            half, pl.ds(1, HALF, stride=2), :
        ]
        out_ref[pl.ds(half * HALF, HALF), :] = value.astype(jnp.bfloat16)


def pair_products(me, local, other):
    return pl.pallas_call(
        pair_kernel,
        out_shape=jax.ShapeDtypeStruct((2 * HALF, 128), jnp.bfloat16),
        grid_spec=pltpu.PrefetchScalarGridSpec(
            num_scalar_prefetch=1,
            grid=(),
            in_specs=[pl.BlockSpec(memory_space=pltpu.VMEM)] * 2,
            out_specs=pl.BlockSpec(memory_space=pltpu.VMEM),
            scratch_shapes=[pltpu.VMEM((2, 2 * HALF, 128), jnp.float32)],
        ),
        compiler_params=pltpu.CompilerParams(vmem_limit_bytes=30 << 20),
        name="pair_products",
    )(me, local, other)


def body(row_owner, row_slot, feature_table, w_first, w_hidden, w_out):
    samples = row_slot.shape[0]
    rows = feature_table.shape[0]
    me = lax.axis_index("field")
    mine = lax.axis_index("row")

    source = jnp.arange(2 * 128, dtype=jnp.int32)
    wanted = (source % 128) // 32 * K + source // 128 * 32 + source % 32
    reorder = (source[:, None] == wanted[None, :]).astype(jnp.bfloat16)
    packed = jnp.dot(feature_table, reorder, preferred_element_type=jnp.float32)
    packed = packed.astype(jnp.bfloat16).reshape(rows, 2, 128)
    pieces = spread_shard(packed)

    full_hidden = lax.all_gather(w_hidden, "field", axis=1, tiled=True)

    owner = row_owner[:, :, 0]
    piece = (mine // NY - owner // NY) % NZ * NY + (mine % NY - owner % NY) % NY
    ids = (piece * rows + row_slot).T.reshape(GROUPS, PER, 2, HALF)
    early = (me <= jnp.arange(GROUPS, dtype=jnp.int32))[:, None, None]
    send_ids = jnp.where(early, ids[:, :, 0], ids[:, :, 1]).reshape(-1)
    local_ids = jnp.where(early, ids[:, :, 1], ids[:, :, 0]).reshape(-1)

    col = jnp.arange(F * F, dtype=jnp.int32)
    b, a, i, j = col // 128, col // 16 % 8, col // 4 % 4, col % 4
    forward = (a * PER + i) * F + b * PER + j
    backward = (b * PER + j) * F + a * PER + i
    rows_of = jnp.where(me < GROUPS // 2, forward, backward)
    first_order = (rows_of[:, None] == col[None, :]).astype(jnp.bfloat16)
    first = jnp.dot(
        first_order, w_first.reshape(F * F, H), preferred_element_type=jnp.float32
    ).astype(jnp.bfloat16)

    sent = gather_rows(send_ids, pieces, "gather_sent")
    other = lax.all_to_all(
        sent.reshape(GROUPS, PER * HALF, 2, 128), "field", split_axis=0, concat_axis=0, tiled=True
    )
    local = gather_rows(local_ids, pieces, "gather_local")
    dots = pair_products(
        me.reshape(1),
        local.reshape(GROUPS, PER, 2 * HALF, 128),
        other.reshape(GROUPS, PER, 2 * HALF, 128),
    )
    block = samples // GROUPS
    own_dots = lax.all_to_all(
        dots.reshape(GROUPS, block, 128), "field", split_axis=0, concat_axis=0, tiled=True
    )
    hidden = jnp.dot(
        own_dots.transpose(1, 0, 2).reshape(block, F * F), first, preferred_element_type=jnp.float32
    )
    hidden = jax.nn.relu(hidden).astype(jnp.bfloat16)
    for depth in range(w_hidden.shape[0]):
        hidden = jax.nn.relu(
            jnp.dot(hidden, full_hidden[depth], preferred_element_type=jnp.float32)
        ).astype(jnp.bfloat16)
    logits = jnp.dot(hidden, w_out, preferred_element_type=jnp.float32)
    everyone = lax.all_to_all(
        jnp.broadcast_to(logits[None], (GROUPS, block)),
        "field",
        split_axis=0,
        concat_axis=0,
        tiled=True,
    )
    return everyone.reshape(samples)


def solution(mesh):
    placed = (
        P("row", None, None),
        P("row", None),
        P("row", "field"),
        P(),
        P(None, "field", None),
        P(),
    )
    return jax.shard_map(body, mesh=mesh, in_specs=placed, out_specs=P("row"), check_vma=False)
```

```python
import functools

import jax
import jax.numpy as jnp
from jax import lax
from jax.experimental import pallas as pl
from jax.experimental.pallas import tpu as pltpu
from jax.sharding import PartitionSpec as P

F = 32
K = 64
H = 2048
NZ = 8
NY = 4
GROUPS = 8
PER = 4
HALF = 128

DIRECTIONS = ((1, 0), (-1, 0), (0, 1), (0, -1))
SPREAD = (
    ((2, (0, 0), (0, 1)), (0, (0, 0), (1, 0)), (3, (0, 0), (0, 3)), (1, (0, 0), (7, 0))),
    ((1, (0, 1), (7, 1)), (0, (1, 0), (2, 0)), (3, (1, 0), (1, 3)), (2, (1, 0), (1, 1))),
    ((0, (2, 0), (3, 0)), (3, (7, 0), (7, 3)), (1, (7, 0), (6, 0)), (2, (0, 1), (0, 2))),
    ((2, (7, 1), (7, 2)), (1, (7, 1), (6, 1)), (0, (1, 3), (2, 3)), (3, (1, 3), (1, 2))),
    ((0, (3, 0), (4, 0)), (3, (6, 0), (6, 3)), (2, (3, 0), (3, 1)), (1, (6, 0), (5, 0))),
    ((3, (2, 3), (2, 2)), (1, (6, 1), (5, 1)), (2, (6, 1), (6, 2)), (0, (2, 3), (3, 3))),
    ((1, (3, 1), (2, 1)), (2, (3, 1), (3, 2)), (0, (3, 1), (4, 1)), (3, (4, 0), (4, 3))),
    ((2, (5, 1), (5, 2)), (3, (5, 0), (5, 3)), (0, (3, 2), (4, 2))),
)


def step_pairs(direction):
    dz, dy = direction
    return [
        (z * NY + y, ((z + dz) % NZ) * NY + (y + dy) % NY) for z in range(NZ) for y in range(NY)
    ]


def place_kernel(slots, rows, *refs):
    pieces, table, sems = refs[: len(slots)], refs[-2], refs[-1]
    copies = [
        pltpu.make_async_copy(piece, table.at[pl.ds(slot * rows, rows)], sems.at[n])
        for n, (slot, piece) in enumerate(zip(slots, pieces))
    ]
    for copy in copies:
        copy.start()
    for copy in copies:
        copy.wait()


def place_pieces(table, slots, pieces):
    rows = pieces[0].shape[0]
    shape = (NZ * NY * rows,) + pieces[0].shape[1:]
    held = [] if table is None else [table]
    count = len(pieces)
    return pl.pallas_call(
        functools.partial(place_kernel, slots, rows),
        out_shape=pltpu.HBM(shape, pieces[0].dtype),
        in_specs=[pl.BlockSpec(memory_space=pl.ANY)] * count
        + [pl.BlockSpec(memory_space=pltpu.HBM)] * len(held),
        out_specs=pl.BlockSpec(memory_space=pltpu.HBM),
        scratch_shapes=[pltpu.SemaphoreType.DMA((count,))],
        input_output_aliases={count: 0} if held else {},
        compiler_params=pltpu.CompilerParams(vmem_limit_bytes=1 << 20),
        cost_estimate=pl.CostEstimate(
            flops=0, bytes_accessed=2 * count * rows * 512, transcendentals=0
        ),
        name="place",
    )(*pieces, *held)


def spread_shard(own):
    pieces = {(0, 0): own}
    table = place_pieces(None, [0], [own])
    arrived = []
    for step in SPREAD:
        sources = sorted({source for _, source, _ in step})
        kept = lax.optimization_barrier(([pieces[source] for source in sources], table))
        ready, table = dict(zip(sources, kept[0])), kept[1]
        for way, source, target in step:
            pieces[target] = lax.ppermute(ready[source], "row", step_pairs(DIRECTIONS[way]))
        if arrived:
            table = place_pieces(
                table, [dz * NY + dy for dz, dy in arrived], [pieces[name] for name in arrived]
            )
        arrived = [target for _, _, target in step]
    return place_pieces(
        table, [dz * NY + dy for dz, dy in arrived], [pieces[name] for name in arrived]
    )


def gather_kernel(count, parts, index, table_hbm, out, found, table, table_sem, sems):
    copy = pltpu.make_async_copy(table_hbm, table, table_sem)
    copy.start()
    copy.wait()
    unroll = 32
    size = count // parts
    leaving = []
    for part in range(parts):

        def some(i, carry):
            first = part * size + i * unroll
            for u in range(unroll):
                found[first + u] = table[index[first + u]]
            return carry

        lax.fori_loop(0, size // unroll, some, 0)
        span = pl.ds(part * size, size)
        leaving.append(pltpu.make_async_copy(found.at[span], out.at[span], sems.at[part]))
        leaving[-1].start()
    for copy in leaving:
        copy.wait()


def gather_rows(index, table, name):
    count = index.shape[0]
    parts = 8
    return pl.pallas_call(
        functools.partial(gather_kernel, count, parts),
        out_shape=pltpu.HBM((count, 2, 128), jnp.bfloat16),
        grid_spec=pltpu.PrefetchScalarGridSpec(
            num_scalar_prefetch=1,
            grid=(),
            in_specs=[pl.BlockSpec(memory_space=pltpu.HBM)],
            out_specs=pl.BlockSpec(memory_space=pltpu.HBM),
            scratch_shapes=[
                pltpu.VMEM((count, 2, 128), jnp.bfloat16),
                pltpu.VMEM(table.shape, table.dtype),
                pltpu.SemaphoreType.DMA,
                pltpu.SemaphoreType.DMA((parts,)),
            ],
        ),
        compiler_params=pltpu.CompilerParams(vmem_limit_bytes=56 << 20),
        cost_estimate=pl.CostEstimate(
            flops=0, bytes_accessed=4 * count * 512, transcendentals=0
        ),
        name=name,
    )(index, table)


def pair_kernel(me_ref, local_hbm, other_hbm, out_ref, local_ref, other_ref, sums_ref, sems):
    me = me_ref[0]
    copies = [
        [
            pltpu.make_async_copy(source.at[a], target.at[a], sems.at[n, a])
            for n, (source, target) in enumerate(((local_hbm, local_ref), (other_hbm, other_ref)))
        ]
        for a in range(GROUPS)
    ]
    for pair in copies:
        for copy in pair:
            copy.start()
    rows = 2 * HALF
    lane = lax.broadcasted_iota(jnp.int32, (rows, 128), 1)
    block = lane // 32
    unit = lane // 16
    inner = lane % 16
    depth = lax.broadcasted_iota(jnp.int32, (512, 128), 0)
    column = lax.broadcasted_iota(jnp.int32, (512, 128), 1)
    turn = depth // 128
    second = (depth % 128) // 32
    place = ((second + turn) % PER) * PER + second
    collect = jnp.where(column % 16 == place, 1.0, 0.0).astype(jnp.bfloat16)

    def choose(tiles, offsets):
        value = tiles[offsets[3]]
        for b in (2, 1, 0):
            value = jnp.where(block == b, tiles[offsets[b]], value)
        return value

    def products(first, second):
        high, low = [], []
        for d in range(PER):
            left = choose(first, [(b + d) % PER for b in range(PER)])
            right = choose(second, [(b - d) % PER for b in range(PER)])
            if d:
                right = pltpu.roll(right, 128 - 32 * d, 1)
            value = left * right
            rounded = value.astype(jnp.bfloat16)
            high.append(rounded)
            low.append((value - rounded.astype(jnp.float32)).astype(jnp.bfloat16))
        high = jnp.concatenate(high, axis=1)
        low = jnp.concatenate(low, axis=1)
        return jnp.dot(high, collect, preferred_element_type=jnp.float32) + jnp.dot(
            low, collect, preferred_element_type=jnp.float32
        )

    def tiles(ref, a):
        return [ref[a, n].astype(jnp.float32) for n in range(PER)]

    total = jnp.zeros((rows, 128), jnp.float32)
    for a in range(GROUPS):
        for copy in copies[a]:
            copy.wait()
        dots = products(tiles(local_ref, a), tiles(other_ref, a))
        total = total + jnp.where(unit == a, dots, 0.0)
    own_first = tiles(other_ref, me)
    own_second = tiles(local_ref, me)
    first_dots = products(own_first, own_first)
    second_dots = products(own_second, own_second)
    i, j = inner // PER, inner % PER
    zero = jnp.zeros_like(total)
    sums_ref[0] = jnp.where(
        unit < me, total, jnp.where((unit == me) & (i < j), first_dots, zero)
    )
    sums_ref[1] = jnp.where(
        unit > me, total, jnp.where((unit == me) & (i > j), second_dots, zero)
    )
    for half in range(2):
        value = sums_ref[half, pl.ds(0, HALF, stride=2), :] + sums_ref[
            half, pl.ds(1, HALF, stride=2), :
        ]
        out_ref[pl.ds(half * HALF, HALF), :] = value.astype(jnp.bfloat16)


def pair_products(me, local, other):
    return pl.pallas_call(
        pair_kernel,
        out_shape=jax.ShapeDtypeStruct((2 * HALF, 128), jnp.bfloat16),
        grid_spec=pltpu.PrefetchScalarGridSpec(
            num_scalar_prefetch=1,
            grid=(),
            in_specs=[pl.BlockSpec(memory_space=pltpu.HBM)] * 2,
            out_specs=pl.BlockSpec(memory_space=pltpu.VMEM),
            scratch_shapes=[
                pltpu.VMEM((GROUPS, PER, 2 * HALF, 128), jnp.bfloat16),
                pltpu.VMEM((GROUPS, PER, 2 * HALF, 128), jnp.bfloat16),
                pltpu.VMEM((2, 2 * HALF, 128), jnp.float32),
                pltpu.SemaphoreType.DMA((2, GROUPS)),
            ],
        ),
        compiler_params=pltpu.CompilerParams(vmem_limit_bytes=56 << 20),
        name="pair_products",
    )(me, local, other)


def body(row_owner, row_slot, feature_table, w_first, w_hidden, w_out):
    samples = row_slot.shape[0]
    rows = feature_table.shape[0]
    me = lax.axis_index("field")
    mine = lax.axis_index("row")

    source = jnp.arange(2 * 128, dtype=jnp.int32)
    wanted = (source % 128) // 32 * K + source // 128 * 32 + source % 32
    reorder = (source[:, None] == wanted[None, :]).astype(jnp.bfloat16)
    packed = jnp.dot(feature_table, reorder, preferred_element_type=jnp.float32)
    packed = packed.astype(jnp.bfloat16).reshape(rows, 2, 128)
    table = spread_shard(packed)

    full_hidden = lax.all_gather(w_hidden, "field", axis=1, tiled=True)

    owner = row_owner[:, :, 0]
    piece = (mine // NY - owner // NY) % NZ * NY + (mine % NY - owner % NY) % NY
    ids = (piece * rows + row_slot).T.reshape(GROUPS, PER, 2, HALF)
    early = (me <= jnp.arange(GROUPS, dtype=jnp.int32))[:, None, None]
    send_ids = jnp.where(early, ids[:, :, 0], ids[:, :, 1]).reshape(-1)
    local_ids = jnp.where(early, ids[:, :, 1], ids[:, :, 0]).reshape(-1)

    col = jnp.arange(F * F, dtype=jnp.int32)
    b, a, i, j = col // 128, col // 16 % 8, col // 4 % 4, col % 4
    forward = (a * PER + i) * F + b * PER + j
    backward = (b * PER + j) * F + a * PER + i
    rows_of = jnp.where(me < GROUPS // 2, forward, backward)
    first_order = (rows_of[:, None] == col[None, :]).astype(jnp.bfloat16)
    first = jnp.dot(
        first_order, w_first.reshape(F * F, H), preferred_element_type=jnp.float32
    ).astype(jnp.bfloat16)

    sent = gather_rows(send_ids, table, "gather_sent")
    other = lax.all_to_all(
        sent.reshape(GROUPS, PER * HALF, 2, 128), "field", split_axis=0, concat_axis=0, tiled=True
    )
    local = gather_rows(local_ids, table, "gather_local")
    dots = pair_products(
        me.reshape(1),
        local.reshape(GROUPS, PER, 2 * HALF, 128),
        other.reshape(GROUPS, PER, 2 * HALF, 128),
    )
    block = samples // GROUPS
    own_dots = lax.all_to_all(
        dots.reshape(GROUPS, block, 128), "field", split_axis=0, concat_axis=0, tiled=True
    )
    hidden = jnp.dot(
        own_dots.transpose(1, 0, 2).reshape(block, F * F), first, preferred_element_type=jnp.float32
    )
    hidden = jax.nn.relu(hidden).astype(jnp.bfloat16)
    for depth in range(w_hidden.shape[0]):
        hidden = jax.nn.relu(
            jnp.dot(hidden, full_hidden[depth], preferred_element_type=jnp.float32)
        ).astype(jnp.bfloat16)
    logits = jnp.dot(hidden, w_out, preferred_element_type=jnp.float32)
    everyone = lax.all_to_all(
        jnp.broadcast_to(logits[None], (GROUPS, block)),
        "field",
        split_axis=0,
        concat_axis=0,
        tiled=True,
    )
    return everyone.reshape(samples)


def solution(mesh):
    placed = (
        P("row", None, None),
        P("row", None),
        P("row", "field"),
        P(),
        P(None, "field", None),
        P(),
    )
    return jax.shard_map(body, mesh=mesh, in_specs=placed, out_specs=P("row"), check_vma=False)
```

```python
import functools

import jax
import jax.numpy as jnp
from jax import lax
from jax.experimental import pallas as pl
from jax.experimental.pallas import tpu as pltpu
from jax.sharding import PartitionSpec as P

F = 32
K = 64
H = 2048
NZ = 8
NY = 4
GROUPS = 8
PER = 4
HALF = 128
LOADS = 16

DIRECTIONS = ((1, 0), (-1, 0), (0, 1), (0, -1))
SPREAD = (
    ((2, (0, 0), (0, 1)), (0, (0, 0), (1, 0)), (3, (0, 0), (0, 3)), (1, (0, 0), (7, 0))),
    ((1, (0, 1), (7, 1)), (0, (1, 0), (2, 0)), (3, (1, 0), (1, 3)), (2, (1, 0), (1, 1))),
    ((0, (2, 0), (3, 0)), (3, (7, 0), (7, 3)), (1, (7, 0), (6, 0)), (2, (0, 1), (0, 2))),
    ((2, (7, 1), (7, 2)), (1, (7, 1), (6, 1)), (0, (1, 3), (2, 3)), (3, (1, 3), (1, 2))),
    ((0, (3, 0), (4, 0)), (3, (6, 0), (6, 3)), (2, (3, 0), (3, 1)), (1, (6, 0), (5, 0))),
    ((3, (2, 3), (2, 2)), (1, (6, 1), (5, 1)), (2, (6, 1), (6, 2)), (0, (2, 3), (3, 3))),
    ((1, (3, 1), (2, 1)), (2, (3, 1), (3, 2)), (0, (3, 1), (4, 1)), (3, (4, 0), (4, 3))),
    ((2, (5, 1), (5, 2)), (3, (5, 0), (5, 3)), (0, (3, 2), (4, 2))),
)


def step_pairs(direction):
    dz, dy = direction
    return [
        (z * NY + y, ((z + dz) % NZ) * NY + (y + dy) % NY) for z in range(NZ) for y in range(NY)
    ]


def place_kernel(slots, rows, *refs):
    pieces, table, sems = refs[: len(slots)], refs[-2], refs[-1]
    copies = [
        pltpu.make_async_copy(piece, table.at[pl.ds(slot * rows, rows)], sems.at[n])
        for n, (slot, piece) in enumerate(zip(slots, pieces))
    ]
    for copy in copies:
        copy.start()
    for copy in copies:
        copy.wait()


def place_pieces(table, slots, pieces):
    rows = pieces[0].shape[0]
    shape = (NZ * NY * rows,) + pieces[0].shape[1:]
    held = [] if table is None else [table]
    count = len(pieces)
    return pl.pallas_call(
        functools.partial(place_kernel, slots, rows),
        out_shape=pltpu.HBM(shape, pieces[0].dtype),
        in_specs=[pl.BlockSpec(memory_space=pltpu.VMEM)] * count
        + [pl.BlockSpec(memory_space=pltpu.HBM)] * len(held),
        out_specs=pl.BlockSpec(memory_space=pltpu.HBM),
        scratch_shapes=[pltpu.SemaphoreType.DMA((count,))],
        input_output_aliases={count: 0} if held else {},
        compiler_params=pltpu.CompilerParams(vmem_limit_bytes=1 << 20),
        cost_estimate=pl.CostEstimate(
            flops=0, bytes_accessed=2 * count * rows * 512, transcendentals=0
        ),
        name="place",
    )(*pieces, *held)


def spread_shard(own):
    pieces = {(0, 0): own}
    table = place_pieces(None, [0], [own])
    arrived = []
    for step in SPREAD:
        sources = sorted({source for _, source, _ in step})
        kept = lax.optimization_barrier(([pieces[source] for source in sources], table))
        ready, table = dict(zip(sources, kept[0])), kept[1]
        for way, source, target in step:
            pieces[target] = lax.ppermute(ready[source], "row", step_pairs(DIRECTIONS[way]))
        if arrived:
            table = place_pieces(
                table, [dz * NY + dy for dz, dy in arrived], [pieces[name] for name in arrived]
            )
        arrived = [target for _, _, target in step]
    return place_pieces(
        table, [dz * NY + dy for dz, dy in arrived], [pieces[name] for name in arrived]
    )


def gather_kernel(count, parts, index, table_hbm, out, found, table, load_sems, sems):
    block = table.shape[0] // LOADS
    loads = [
        pltpu.make_async_copy(
            table_hbm.at[pl.ds(n * block, block)], table.at[pl.ds(n * block, block)], load_sems.at[n]
        )
        for n in range(LOADS)
    ]
    for copy in loads:
        copy.start()
    for copy in loads:
        copy.wait()
    unroll = 32
    size = count // parts
    leaving = []
    for part in range(parts):

        def some(i, carry):
            first = part * size + i * unroll
            for u in range(unroll):
                found[first + u] = table[index[first + u]]
            return carry

        lax.fori_loop(0, size // unroll, some, 0)
        span = pl.ds(part * size, size)
        leaving.append(pltpu.make_async_copy(found.at[span], out.at[span], sems.at[part]))
        leaving[-1].start()
    for copy in leaving:
        copy.wait()


def gather_rows(index, table, name):
    count = index.shape[0]
    parts = 8
    return pl.pallas_call(
        functools.partial(gather_kernel, count, parts),
        out_shape=pltpu.HBM((count, 2, 128), jnp.bfloat16),
        grid_spec=pltpu.PrefetchScalarGridSpec(
            num_scalar_prefetch=1,
            grid=(),
            in_specs=[pl.BlockSpec(memory_space=pltpu.HBM)],
            out_specs=pl.BlockSpec(memory_space=pltpu.HBM),
            scratch_shapes=[
                pltpu.VMEM((count, 2, 128), jnp.bfloat16),
                pltpu.VMEM(table.shape, table.dtype),
                pltpu.SemaphoreType.DMA((LOADS,)),
                pltpu.SemaphoreType.DMA((parts,)),
            ],
        ),
        compiler_params=pltpu.CompilerParams(vmem_limit_bytes=24 << 20),
        cost_estimate=pl.CostEstimate(
            flops=0, bytes_accessed=4 * count * 512, transcendentals=0
        ),
        name=name,
    )(index, pltpu.with_memory_space_constraint(table, pltpu.HBM))


def pair_kernel(me_ref, local_hbm, other_hbm, out_ref, local_ref, other_ref, sums_ref, sems):
    me = me_ref[0]
    copies = [
        [
            pltpu.make_async_copy(source.at[a], target.at[a], sems.at[n, a])
            for n, (source, target) in enumerate(((local_hbm, local_ref), (other_hbm, other_ref)))
        ]
        for a in range(GROUPS)
    ]
    for pair in copies:
        for copy in pair:
            copy.start()
    rows = 2 * HALF
    lane = lax.broadcasted_iota(jnp.int32, (rows, 128), 1)
    block = lane // 32
    unit = lane // 16
    inner = lane % 16
    depth = lax.broadcasted_iota(jnp.int32, (512, 128), 0)
    column = lax.broadcasted_iota(jnp.int32, (512, 128), 1)
    turn = depth // 128
    second = (depth % 128) // 32
    place = ((second + turn) % PER) * PER + second
    collect = jnp.where(column % 16 == place, 1.0, 0.0).astype(jnp.bfloat16)

    def choose(tiles, offsets):
        value = tiles[offsets[3]]
        for b in (2, 1, 0):
            value = jnp.where(block == b, tiles[offsets[b]], value)
        return value

    def products(first, second):
        high, low = [], []
        for d in range(PER):
            left = choose(first, [(b + d) % PER for b in range(PER)])
            right = choose(second, [(b - d) % PER for b in range(PER)])
            if d:
                right = pltpu.roll(right, 128 - 32 * d, 1)
            value = left * right
            rounded = value.astype(jnp.bfloat16)
            high.append(rounded)
            low.append((value - rounded.astype(jnp.float32)).astype(jnp.bfloat16))
        high = jnp.concatenate(high, axis=1)
        low = jnp.concatenate(low, axis=1)
        return jnp.dot(high, collect, preferred_element_type=jnp.float32) + jnp.dot(
            low, collect, preferred_element_type=jnp.float32
        )

    def tiles(ref, a):
        return [ref[a, n].astype(jnp.float32) for n in range(PER)]

    total = jnp.zeros((rows, 128), jnp.float32)
    for a in range(GROUPS):
        for copy in copies[a]:
            copy.wait()
        dots = products(tiles(local_ref, a), tiles(other_ref, a))
        total = total + jnp.where(unit == a, dots, 0.0)
    own_first = tiles(other_ref, me)
    own_second = tiles(local_ref, me)
    first_dots = products(own_first, own_first)
    second_dots = products(own_second, own_second)
    i, j = inner // PER, inner % PER
    zero = jnp.zeros_like(total)
    sums_ref[0] = jnp.where(
        unit < me, total, jnp.where((unit == me) & (i < j), first_dots, zero)
    )
    sums_ref[1] = jnp.where(
        unit > me, total, jnp.where((unit == me) & (i > j), second_dots, zero)
    )
    for half in range(2):
        value = sums_ref[half, pl.ds(0, HALF, stride=2), :] + sums_ref[
            half, pl.ds(1, HALF, stride=2), :
        ]
        out_ref[pl.ds(half * HALF, HALF), :] = value.astype(jnp.bfloat16)


def pair_products(me, local, other):
    return pl.pallas_call(
        pair_kernel,
        out_shape=jax.ShapeDtypeStruct((2 * HALF, 128), jnp.bfloat16),
        grid_spec=pltpu.PrefetchScalarGridSpec(
            num_scalar_prefetch=1,
            grid=(),
            in_specs=[
                pl.BlockSpec(memory_space=pltpu.HBM),
                pl.BlockSpec(memory_space=pl.ANY),
            ],
            out_specs=pl.BlockSpec(memory_space=pltpu.VMEM),
            scratch_shapes=[
                pltpu.VMEM((GROUPS, PER, 2 * HALF, 128), jnp.bfloat16),
                pltpu.VMEM((GROUPS, PER, 2 * HALF, 128), jnp.bfloat16),
                pltpu.VMEM((2, 2 * HALF, 128), jnp.float32),
                pltpu.SemaphoreType.DMA((2, GROUPS)),
            ],
        ),
        compiler_params=pltpu.CompilerParams(vmem_limit_bytes=16 << 20),
        name="pair_products",
    )(
        me,
        pltpu.with_memory_space_constraint(local, pltpu.HBM),
        other,
    )


def network_kernel(dots_ref, first_hbm, hidden_hbm, out_weights_ref, out_ref, first, hidden, sems):
    layers = hidden.shape[0]
    size = hidden.shape[1] // GROUPS
    first_size = first.shape[0] // GROUPS
    first_copies = [
        pltpu.make_async_copy(
            first_hbm.at[pl.ds(b * first_size, first_size)],
            first.at[pl.ds(b * first_size, first_size)],
            sems.at[layers, b],
        )
        for b in range(GROUPS)
    ]
    hidden_copies = [
        [
            pltpu.make_async_copy(
                hidden_hbm.at[depth, pl.ds(b * size, size)],
                hidden.at[depth, pl.ds(b * size, size)],
                sems.at[depth, b],
            )
            for b in range(GROUPS)
        ]
        for depth in range(layers)
    ]
    for copies in [first_copies] + hidden_copies:
        for copy in copies:
            copy.start()

    def rounded(value):
        return jnp.maximum(value, 0.0).astype(jnp.bfloat16)

    samples = dots_ref.shape[1]
    value = jnp.zeros((samples, H), jnp.float32)
    for b in range(GROUPS):
        first_copies[b].wait()
        value = value + jnp.dot(
            dots_ref[b],
            first[pl.ds(b * first_size, first_size), :],
            preferred_element_type=jnp.float32,
        )
    units = rounded(value)
    for depth in range(layers):
        value = jnp.zeros((samples, H), jnp.float32)
        for b in range(GROUPS):
            hidden_copies[depth][b].wait()
            value = value + jnp.dot(
                units[:, b * size : (b + 1) * size],
                hidden[depth, pl.ds(b * size, size), :],
                preferred_element_type=jnp.float32,
            )
        units = rounded(value)
    product = units.astype(jnp.float32) * out_weights_ref[...].astype(jnp.float32)
    total = jnp.sum(product, axis=1, keepdims=True)
    out_ref[...] = jnp.broadcast_to(total, out_ref.shape)


def network(dots, first, hidden, out_weights):
    return pl.pallas_call(
        network_kernel,
        out_shape=jax.ShapeDtypeStruct((dots.shape[1], 128), jnp.float32),
        in_specs=[
            pl.BlockSpec(memory_space=pltpu.VMEM),
            pl.BlockSpec(memory_space=pltpu.HBM),
            pl.BlockSpec(memory_space=pltpu.HBM),
            pl.BlockSpec(memory_space=pltpu.VMEM),
        ],
        out_specs=pl.BlockSpec(memory_space=pltpu.VMEM),
        scratch_shapes=[
            pltpu.VMEM(first.shape, first.dtype),
            pltpu.VMEM(hidden.shape, hidden.dtype),
            pltpu.SemaphoreType.DMA((hidden.shape[0] + 1, GROUPS)),
        ],
        compiler_params=pltpu.CompilerParams(vmem_limit_bytes=26 << 20),
        name="network",
    )(
        dots,
        pltpu.with_memory_space_constraint(first, pltpu.HBM),
        pltpu.with_memory_space_constraint(hidden, pltpu.HBM),
        out_weights,
    )


def body(row_owner, row_slot, feature_table, w_first, w_hidden, w_out):
    samples = row_slot.shape[0]
    rows = feature_table.shape[0]
    me = lax.axis_index("field")
    mine = lax.axis_index("row")

    source = jnp.arange(2 * 128, dtype=jnp.int32)
    wanted = (source % 128) // 32 * K + source // 128 * 32 + source % 32
    reorder = (source[:, None] == wanted[None, :]).astype(jnp.bfloat16)
    packed = jnp.dot(feature_table, reorder, preferred_element_type=jnp.float32)
    packed = packed.astype(jnp.bfloat16).reshape(rows, 2, 128)
    table = spread_shard(packed)

    full_hidden = lax.all_gather(w_hidden, "field", axis=1, tiled=True)

    owner = row_owner[:, :, 0]
    piece = (mine // NY - owner // NY) % NZ * NY + (mine % NY - owner % NY) % NY
    ids = (piece * rows + row_slot).T.reshape(GROUPS, PER, 2, HALF)
    early = (me <= jnp.arange(GROUPS, dtype=jnp.int32))[:, None, None]
    send_ids = jnp.where(early, ids[:, :, 0], ids[:, :, 1]).reshape(-1)
    local_ids = jnp.where(early, ids[:, :, 1], ids[:, :, 0]).reshape(-1)

    col = jnp.arange(F * F, dtype=jnp.int32)
    b, a, i, j = col // 128, col // 16 % 8, col // 4 % 4, col % 4
    forward = (a * PER + i) * F + b * PER + j
    backward = (b * PER + j) * F + a * PER + i
    rows_of = jnp.where(me < GROUPS // 2, forward, backward)
    first_order = (rows_of[:, None] == col[None, :]).astype(jnp.bfloat16)
    first = jnp.dot(
        first_order, w_first.reshape(F * F, H), preferred_element_type=jnp.float32
    ).astype(jnp.bfloat16)
    table, first, full_hidden = lax.optimization_barrier((table, first, full_hidden))

    sent = gather_rows(send_ids, table, "gather_sent")
    other = lax.all_to_all(
        sent.reshape(GROUPS, PER * HALF, 2, 128), "field", split_axis=0, concat_axis=0, tiled=True
    )
    local = gather_rows(local_ids, table, "gather_local")
    dots = pair_products(
        me.reshape(1),
        local.reshape(GROUPS, PER, 2 * HALF, 128),
        other.reshape(GROUPS, PER, 2 * HALF, 128),
    )
    block = samples // GROUPS
    own_dots = lax.all_to_all(
        dots.reshape(GROUPS, block, 128), "field", split_axis=0, concat_axis=0, tiled=True
    )
    logits = network(own_dots, first, full_hidden, w_out.reshape(1, H))[:, 0]
    everyone = lax.all_to_all(
        jnp.broadcast_to(logits[None], (GROUPS, block)),
        "field",
        split_axis=0,
        concat_axis=0,
        tiled=True,
    )
    return everyone.reshape(samples)


def solution(mesh):
    placed = (
        P("row", None, None),
        P("row", None),
        P("row", "field"),
        P(),
        P(None, "field", None),
        P(),
    )
    return jax.shard_map(body, mesh=mesh, in_specs=placed, out_specs=P("row"), check_vma=False)
```

```python
import functools

import jax
import jax.numpy as jnp
from jax import lax
from jax.experimental import pallas as pl
from jax.experimental.pallas import tpu as pltpu
from jax.sharding import PartitionSpec as P

F = 32
K = 64
H = 2048
NZ = 8
NY = 4
GROUPS = 8
PER = 4
HALF = 128
LOADS = 16
CHUNK = 64

DIRECTIONS = ((1, 0), (-1, 0), (0, 1), (0, -1))
SPREAD = (
    ((2, (0, 0), (0, 1)), (0, (0, 0), (1, 0)), (3, (0, 0), (0, 3)), (1, (0, 0), (7, 0))),
    ((1, (0, 1), (7, 1)), (0, (1, 0), (2, 0)), (3, (1, 0), (1, 3)), (2, (1, 0), (1, 1))),
    ((0, (2, 0), (3, 0)), (3, (7, 0), (7, 3)), (1, (7, 0), (6, 0)), (2, (0, 1), (0, 2))),
    ((2, (7, 1), (7, 2)), (1, (7, 1), (6, 1)), (0, (1, 3), (2, 3)), (3, (1, 3), (1, 2))),
    ((0, (3, 0), (4, 0)), (3, (6, 0), (6, 3)), (2, (3, 0), (3, 1)), (1, (6, 0), (5, 0))),
    ((3, (2, 3), (2, 2)), (1, (6, 1), (5, 1)), (2, (6, 1), (6, 2)), (0, (2, 3), (3, 3))),
    ((1, (3, 1), (2, 1)), (2, (3, 1), (3, 2)), (0, (3, 1), (4, 1)), (3, (4, 0), (4, 3))),
    ((2, (5, 1), (5, 2)), (3, (5, 0), (5, 3)), (0, (3, 2), (4, 2))),
)


def step_pairs(direction):
    dz, dy = direction
    return [
        (z * NY + y, ((z + dz) % NZ) * NY + (y + dy) % NY) for z in range(NZ) for y in range(NY)
    ]


def place_kernel(slots, rows, *refs):
    pieces, table, sems = refs[: len(slots)], refs[-2], refs[-1]
    copies = [
        pltpu.make_async_copy(piece, table.at[pl.ds(slot * rows, rows)], sems.at[n])
        for n, (slot, piece) in enumerate(zip(slots, pieces))
    ]
    for copy in copies:
        copy.start()
    for copy in copies:
        copy.wait()


def place_pieces(table, slots, pieces):
    rows = pieces[0].shape[0]
    shape = (NZ * NY * rows,) + pieces[0].shape[1:]
    held = [] if table is None else [table]
    count = len(pieces)
    return pl.pallas_call(
        functools.partial(place_kernel, slots, rows),
        out_shape=pltpu.HBM(shape, pieces[0].dtype),
        in_specs=[pl.BlockSpec(memory_space=pltpu.VMEM)] * count
        + [pl.BlockSpec(memory_space=pltpu.HBM)] * len(held),
        out_specs=pl.BlockSpec(memory_space=pltpu.HBM),
        scratch_shapes=[pltpu.SemaphoreType.DMA((count,))],
        input_output_aliases={count: 0} if held else {},
        compiler_params=pltpu.CompilerParams(vmem_limit_bytes=8 << 20),
        cost_estimate=pl.CostEstimate(
            flops=0, bytes_accessed=2 * count * rows * 512, transcendentals=0
        ),
        name="place",
    )(*pieces, *held)


def spread_shard(own):
    pieces = {(0, 0): own}
    table = place_pieces(None, [0], [own])
    arrived = []
    for step in SPREAD:
        sources = sorted({source for _, source, _ in step})
        kept = lax.optimization_barrier(([pieces[source] for source in sources], table))
        ready, table = dict(zip(sources, kept[0])), kept[1]
        for way, source, target in step:
            pieces[target] = lax.ppermute(ready[source], "row", step_pairs(DIRECTIONS[way]))
        if arrived:
            table = place_pieces(
                table, [dz * NY + dy for dz, dy in arrived], [pieces[name] for name in arrived]
            )
        arrived = [target for _, _, target in step]
    return place_pieces(
        table, [dz * NY + dy for dz, dy in arrived], [pieces[name] for name in arrived]
    )


def gather_kernel(count, parts, index, table_hbm, out, found, table, load_sems, sems):
    block = table.shape[0] // LOADS
    loads = [
        pltpu.make_async_copy(
            table_hbm.at[pl.ds(n * block, block)], table.at[pl.ds(n * block, block)], load_sems.at[n]
        )
        for n in range(LOADS)
    ]
    for copy in loads:
        copy.start()
    for copy in loads:
        copy.wait()
    unroll = 32
    size = count // parts
    leaving = []
    for part in range(parts):

        def some(i, carry):
            first = part * size + i * unroll
            for u in range(unroll):
                found[first + u] = table[index[first + u]]
            return carry

        lax.fori_loop(0, size // unroll, some, 0)
        span = pl.ds(part * size, size)
        leaving.append(pltpu.make_async_copy(found.at[span], out.at[span], sems.at[part]))
        leaving[-1].start()
    for copy in leaving:
        copy.wait()


def gather_rows(index, table, name):
    count = index.shape[0]
    parts = 8
    return pl.pallas_call(
        functools.partial(gather_kernel, count, parts),
        out_shape=pltpu.HBM((count, 2, 128), jnp.bfloat16),
        grid_spec=pltpu.PrefetchScalarGridSpec(
            num_scalar_prefetch=1,
            grid=(),
            in_specs=[pl.BlockSpec(memory_space=pltpu.HBM)],
            out_specs=pl.BlockSpec(memory_space=pltpu.HBM),
            scratch_shapes=[
                pltpu.VMEM((count, 2, 128), jnp.bfloat16),
                pltpu.VMEM(table.shape, table.dtype),
                pltpu.SemaphoreType.DMA((LOADS,)),
                pltpu.SemaphoreType.DMA((parts,)),
            ],
        ),
        compiler_params=pltpu.CompilerParams(vmem_limit_bytes=24 << 20),
        cost_estimate=pl.CostEstimate(
            flops=0, bytes_accessed=4 * count * 512, transcendentals=0
        ),
        name=name,
    )(index, pltpu.with_memory_space_constraint(table, pltpu.HBM))


def pair_kernel(
    me_ref, local_hbm, other_hbm, out_ref, local_ref, other_ref, total_ref, sums_ref, sems
):
    me = me_ref[0]
    copies = [
        [
            pltpu.make_async_copy(source.at[a], target.at[a], sems.at[n, a])
            for n, (source, target) in enumerate(((local_hbm, local_ref), (other_hbm, other_ref)))
        ]
        for a in range(GROUPS)
    ]
    for pair in copies:
        for copy in pair:
            copy.start()
    rows = 2 * HALF
    lane = lax.broadcasted_iota(jnp.int32, (CHUNK, 128), 1)
    block = lane // 32
    unit = lane // 16
    inner = lane % 16
    i, j = inner // PER, inner % PER
    depth = lax.broadcasted_iota(jnp.int32, (512, 128), 0)
    column = lax.broadcasted_iota(jnp.int32, (512, 128), 1)
    turn = depth // 128
    second = (depth % 128) // 32
    place = ((second + turn) % PER) * PER + second
    collect = jnp.where(column % 16 == place, 1.0, 0.0).astype(jnp.bfloat16)
    odd = block % 2 == 1
    upper = block >= 2
    outer = (block == 0) | (block == 3)

    def turned(tiles):
        even_low = jnp.where(odd, tiles[1], tiles[0])
        even_high = jnp.where(odd, tiles[3], tiles[2])
        odd_low = jnp.where(odd, tiles[0], tiles[1])
        odd_high = jnp.where(odd, tiles[2], tiles[3])
        return (
            jnp.where(upper, even_high, even_low),
            jnp.where(outer, odd_low, odd_high),
            jnp.where(upper, even_low, even_high),
            jnp.where(outer, odd_high, odd_low),
        )

    def products(first, second):
        high, low = [], []
        lefts, rights = turned(first), turned(second)
        for d in range(PER):
            right = rights[-d % PER]
            if d:
                right = pltpu.roll(right, 128 - 32 * d, 1)
            value = lefts[d] * right
            rounded = value.astype(jnp.bfloat16)
            high.append(rounded)
            low.append((value - rounded.astype(jnp.float32)).astype(jnp.bfloat16))
        high = jnp.concatenate(high, axis=1)
        low = jnp.concatenate(low, axis=1)
        return jnp.dot(high, collect, preferred_element_type=jnp.float32) + jnp.dot(
            low, collect, preferred_element_type=jnp.float32
        )

    def tiles(ref, a, span):
        return [ref[a, n, span, :].astype(jnp.float32) for n in range(PER)]

    for a in range(GROUPS):
        for copy in copies[a]:
            copy.wait()

        def some(r, carry, a=a):
            span = pl.ds(r * CHUNK, CHUNK)
            dots = products(tiles(local_ref, a, span), tiles(other_ref, a, span))
            total_ref[span, :] = jnp.where(unit == a, dots, total_ref[span, :])
            return carry

        lax.fori_loop(0, rows // CHUNK, some, 0)

    def finish(r, carry):
        span = pl.ds(r * CHUNK, CHUNK)
        own_first = tiles(other_ref, me, span)
        own_second = tiles(local_ref, me, span)
        first_dots = products(own_first, own_first)
        second_dots = products(own_second, own_second)
        total = total_ref[span, :]
        sums_ref[0, span, :] = jnp.where(
            unit < me, total, jnp.where((unit == me) & (i < j), first_dots, 0.0)
        )
        sums_ref[1, span, :] = jnp.where(
            unit > me, total, jnp.where((unit == me) & (i > j), second_dots, 0.0)
        )
        return carry

    lax.fori_loop(0, rows // CHUNK, finish, 0)
    for half in range(2):
        value = sums_ref[half, pl.ds(0, HALF, stride=2), :] + sums_ref[
            half, pl.ds(1, HALF, stride=2), :
        ]
        out_ref[pl.ds(half * HALF, HALF), :] = value.astype(jnp.bfloat16)


def pair_products(me, local, other):
    return pl.pallas_call(
        pair_kernel,
        out_shape=jax.ShapeDtypeStruct((2 * HALF, 128), jnp.bfloat16),
        grid_spec=pltpu.PrefetchScalarGridSpec(
            num_scalar_prefetch=1,
            grid=(),
            in_specs=[
                pl.BlockSpec(memory_space=pltpu.HBM),
                pl.BlockSpec(memory_space=pl.ANY),
            ],
            out_specs=pl.BlockSpec(memory_space=pltpu.VMEM),
            scratch_shapes=[
                pltpu.VMEM((GROUPS, PER, 2 * HALF, 128), jnp.bfloat16),
                pltpu.VMEM((GROUPS, PER, 2 * HALF, 128), jnp.bfloat16),
                pltpu.VMEM((2 * HALF, 128), jnp.float32),
                pltpu.VMEM((2, 2 * HALF, 128), jnp.float32),
                pltpu.SemaphoreType.DMA((2, GROUPS)),
            ],
        ),
        compiler_params=pltpu.CompilerParams(vmem_limit_bytes=16 << 20),
        name="pair_products",
    )(
        me,
        pltpu.with_memory_space_constraint(local, pltpu.HBM),
        other,
    )


def network_kernel(dots_ref, first_hbm, hidden_hbm, out_weights_ref, out_ref, first, hidden, sems):
    layers = hidden.shape[0]
    size = hidden.shape[1] // GROUPS
    first_size = first.shape[0] // GROUPS
    first_copies = [
        pltpu.make_async_copy(
            first_hbm.at[pl.ds(b * first_size, first_size)],
            first.at[pl.ds(b * first_size, first_size)],
            sems.at[layers, b],
        )
        for b in range(GROUPS)
    ]
    hidden_copies = [
        [
            pltpu.make_async_copy(
                hidden_hbm.at[depth, pl.ds(b * size, size)],
                hidden.at[depth, pl.ds(b * size, size)],
                sems.at[depth, b],
            )
            for b in range(GROUPS)
        ]
        for depth in range(layers)
    ]
    for copies in [first_copies] + hidden_copies:
        for copy in copies:
            copy.start()

    def rounded(value):
        return jnp.maximum(value, 0.0).astype(jnp.bfloat16)

    samples = dots_ref.shape[1]
    value = jnp.zeros((samples, H), jnp.float32)
    for b in range(GROUPS):
        first_copies[b].wait()
        value = value + jnp.dot(
            dots_ref[b],
            first[pl.ds(b * first_size, first_size), :],
            preferred_element_type=jnp.float32,
        )
    units = rounded(value)
    for depth in range(layers):
        value = jnp.zeros((samples, H), jnp.float32)
        for b in range(GROUPS):
            hidden_copies[depth][b].wait()
            value = value + jnp.dot(
                units[:, b * size : (b + 1) * size],
                hidden[depth, pl.ds(b * size, size), :],
                preferred_element_type=jnp.float32,
            )
        units = rounded(value)
    product = units.astype(jnp.float32) * out_weights_ref[...].astype(jnp.float32)
    total = jnp.sum(product, axis=1, keepdims=True)
    out_ref[...] = jnp.broadcast_to(total, out_ref.shape)


def network(dots, first, hidden, out_weights):
    return pl.pallas_call(
        network_kernel,
        out_shape=jax.ShapeDtypeStruct((dots.shape[1], 128), jnp.float32),
        in_specs=[
            pl.BlockSpec(memory_space=pltpu.VMEM),
            pl.BlockSpec(memory_space=pltpu.HBM),
            pl.BlockSpec(memory_space=pltpu.HBM),
            pl.BlockSpec(memory_space=pltpu.VMEM),
        ],
        out_specs=pl.BlockSpec(memory_space=pltpu.VMEM),
        scratch_shapes=[
            pltpu.VMEM(first.shape, first.dtype),
            pltpu.VMEM(hidden.shape, hidden.dtype),
            pltpu.SemaphoreType.DMA((hidden.shape[0] + 1, GROUPS)),
        ],
        compiler_params=pltpu.CompilerParams(vmem_limit_bytes=26 << 20),
        name="network",
    )(
        dots,
        pltpu.with_memory_space_constraint(first, pltpu.HBM),
        pltpu.with_memory_space_constraint(hidden, pltpu.HBM),
        out_weights,
    )


def body(row_owner, row_slot, feature_table, w_first, w_hidden, w_out):
    samples = row_slot.shape[0]
    rows = feature_table.shape[0]
    me = lax.axis_index("field")
    mine = lax.axis_index("row")

    source = jnp.arange(2 * 128, dtype=jnp.int32)
    wanted = (source % 128) // 32 * K + source // 128 * 32 + source % 32
    reorder = (source[:, None] == wanted[None, :]).astype(jnp.bfloat16)
    packed = jnp.dot(feature_table, reorder, preferred_element_type=jnp.float32)
    packed = packed.astype(jnp.bfloat16).reshape(rows, 2, 128)
    table = spread_shard(packed)

    full_hidden = lax.all_gather(w_hidden, "field", axis=1, tiled=True)

    owner = row_owner[:, :, 0]
    piece = (mine // NY - owner // NY) % NZ * NY + (mine % NY - owner % NY) % NY
    ids = (piece * rows + row_slot).T.reshape(GROUPS, PER, 2, HALF)
    early = (me <= jnp.arange(GROUPS, dtype=jnp.int32))[:, None, None]
    send_ids = jnp.where(early, ids[:, :, 0], ids[:, :, 1]).reshape(-1)
    local_ids = jnp.where(early, ids[:, :, 1], ids[:, :, 0]).reshape(-1)

    table, full_hidden = lax.optimization_barrier((table, full_hidden))

    sent = gather_rows(send_ids, table, "gather_sent")
    other = lax.all_to_all(
        sent.reshape(GROUPS, PER * HALF, 2, 128), "field", split_axis=0, concat_axis=0, tiled=True
    )
    local = gather_rows(local_ids, table, "gather_local")
    local, w_pairs = lax.optimization_barrier((local, w_first))

    col = jnp.arange(F * F, dtype=jnp.int32)
    b, a, i, j = col // 128, col // 16 % 8, col // 4 % 4, col % 4
    forward = (a * PER + i) * F + b * PER + j
    backward = (b * PER + j) * F + a * PER + i
    rows_of = jnp.where(me < GROUPS // 2, forward, backward)
    first_order = (rows_of[:, None] == col[None, :]).astype(jnp.bfloat16)
    first = jnp.dot(
        first_order, w_pairs.reshape(F * F, H), preferred_element_type=jnp.float32
    ).astype(jnp.bfloat16)
    dots = pair_products(
        me.reshape(1),
        local.reshape(GROUPS, PER, 2 * HALF, 128),
        other.reshape(GROUPS, PER, 2 * HALF, 128),
    )
    block = samples // GROUPS
    own_dots = lax.all_to_all(
        dots.reshape(GROUPS, block, 128), "field", split_axis=0, concat_axis=0, tiled=True
    )
    logits = network(own_dots, first, full_hidden, w_out.reshape(1, H))[:, 0]
    everyone = lax.all_to_all(
        jnp.broadcast_to(logits[None], (GROUPS, block)),
        "field",
        split_axis=0,
        concat_axis=0,
        tiled=True,
    )
    return everyone.reshape(samples)


def solution(mesh):
    placed = (
        P("row", None, None),
        P("row", None),
        P("row", "field"),
        P(),
        P(None, "field", None),
        P(),
    )
    return jax.shard_map(body, mesh=mesh, in_specs=placed, out_specs=P("row"), check_vma=False)
```

```python
import functools

import jax
import jax.numpy as jnp
from jax import lax
from jax.experimental import pallas as pl
from jax.experimental.pallas import tpu as pltpu
from jax.sharding import PartitionSpec as P

F = 32
K = 64
H = 2048
NZ = 8
NY = 4
GROUPS = 8
PER = 4
HALF = 128
LAG = 3
CHUNK = 128

DIRECTIONS = ((1, 0), (-1, 0), (0, 1), (0, -1))
SPREAD = (
    ((2, (0, 0), (0, 1)), (0, (0, 0), (1, 0)), (3, (0, 0), (0, 3)), (1, (0, 0), (7, 0))),
    ((1, (0, 1), (7, 1)), (0, (1, 0), (2, 0)), (3, (1, 0), (1, 3)), (2, (1, 0), (1, 1))),
    ((0, (2, 0), (3, 0)), (3, (7, 0), (7, 3)), (1, (7, 0), (6, 0)), (2, (0, 1), (0, 2))),
    ((2, (7, 1), (7, 2)), (1, (7, 1), (6, 1)), (0, (1, 3), (2, 3)), (3, (1, 3), (1, 2))),
    ((0, (3, 0), (4, 0)), (3, (6, 0), (6, 3)), (2, (3, 0), (3, 1)), (1, (6, 0), (5, 0))),
    ((3, (2, 3), (2, 2)), (1, (6, 1), (5, 1)), (2, (6, 1), (6, 2)), (0, (2, 3), (3, 3))),
    ((1, (3, 1), (2, 1)), (2, (3, 1), (3, 2)), (0, (3, 1), (4, 1)), (3, (4, 0), (4, 3))),
    ((2, (5, 1), (5, 2)), (3, (5, 0), (5, 3)), (0, (3, 2), (4, 2))),
)


def step_pairs(direction):
    dz, dy = direction
    return [
        (z * NY + y, ((z + dz) % NZ) * NY + (y + dy) % NY) for z in range(NZ) for y in range(NY)
    ]


def place_kernel(slots, rows, *refs):
    pieces, table, sems = refs[: len(slots)], refs[-2], refs[-1]
    copies = [
        pltpu.make_async_copy(piece, table.at[pl.ds(slot * rows, rows)], sems.at[n])
        for n, (slot, piece) in enumerate(zip(slots, pieces))
    ]
    for copy in copies:
        copy.start()
    for copy in copies:
        copy.wait()


def place_pieces(table, slots, pieces):
    rows = pieces[0].shape[0]
    shape = (NZ * NY * rows,) + pieces[0].shape[1:]
    held = [] if table is None else [table]
    count = len(pieces)
    return pl.pallas_call(
        functools.partial(place_kernel, slots, rows),
        out_shape=pltpu.HBM(shape, pieces[0].dtype),
        in_specs=[pl.BlockSpec(memory_space=pltpu.VMEM)] * count
        + [pl.BlockSpec(memory_space=pltpu.HBM)] * len(held),
        out_specs=pl.BlockSpec(memory_space=pltpu.HBM),
        scratch_shapes=[pltpu.SemaphoreType.DMA((count,))],
        input_output_aliases={count: 0} if held else {},
        compiler_params=pltpu.CompilerParams(vmem_limit_bytes=8 << 20),
        cost_estimate=pl.CostEstimate(
            flops=0, bytes_accessed=2 * count * rows * 512, transcendentals=0
        ),
        name="place",
    )(*pieces, *held)


def slot_of(name):
    return name[0] * NY + name[1]


def spread_shard(own):
    pieces = {(0, 0): own}
    table = place_pieces(None, [0], [own])
    waiting = []
    for step in SPREAD:
        sources = sorted({source for _, source, _ in step})
        kept = lax.optimization_barrier(([pieces[source] for source in sources], table))
        ready, table = dict(zip(sources, kept[0])), kept[1]
        for way, source, target in step:
            pieces[target] = lax.ppermute(ready[source], "row", step_pairs(DIRECTIONS[way]))
        waiting.append([target for _, _, target in step])
        if len(waiting) >= LAG:
            names = waiting.pop(0)
            table = place_pieces(table, [slot_of(n) for n in names], [pieces[n] for n in names])
    while len(waiting) > 2:
        names = waiting.pop(0)
        table = place_pieces(table, [slot_of(n) for n in names], [pieces[n] for n in names])
    late = waiting[0] + waiting[1]
    return table, [slot_of(n) for n in late], [pieces[n] for n in late]


def gather_kernel(count, parts, late_slots, index, table_hbm, *refs):
    late, (out, found, table, load_sems, sems) = refs[: len(late_slots)], refs[len(late_slots) :]
    rows = table.shape[0] // (NZ * NY)
    loads = []
    for slot in range(NZ * NY):
        span = pl.ds(slot * rows, rows)
        source = late[late_slots.index(slot)] if slot in late_slots else table_hbm.at[span]
        loads.append(pltpu.make_async_copy(source, table.at[span], load_sems.at[slot]))
    for copy in loads:
        copy.start()
    for copy in loads:
        copy.wait()
    unroll = 32
    size = count // parts
    leaving = []
    for part in range(parts):

        def some(i, carry):
            first = part * size + i * unroll
            for u in range(unroll):
                found[first + u] = table[index[first + u]]
            return carry

        lax.fori_loop(0, size // unroll, some, 0)
        span = pl.ds(part * size, size)
        leaving.append(pltpu.make_async_copy(found.at[span], out.at[span], sems.at[part]))
        leaving[-1].start()
    for copy in leaving:
        copy.wait()


def gather_rows(index, table, late_slots, late, name):
    count = index.shape[0]
    parts = 8
    return pl.pallas_call(
        functools.partial(gather_kernel, count, parts, late_slots),
        out_shape=pltpu.HBM((count, 2, 128), jnp.bfloat16),
        grid_spec=pltpu.PrefetchScalarGridSpec(
            num_scalar_prefetch=1,
            grid=(),
            in_specs=[pl.BlockSpec(memory_space=pltpu.HBM)]
            + [pl.BlockSpec(memory_space=pl.ANY)] * len(late),
            out_specs=pl.BlockSpec(memory_space=pltpu.HBM),
            scratch_shapes=[
                pltpu.VMEM((count, 2, 128), jnp.bfloat16),
                pltpu.VMEM(table.shape, table.dtype),
                pltpu.SemaphoreType.DMA((NZ * NY,)),
                pltpu.SemaphoreType.DMA((parts,)),
            ],
        ),
        compiler_params=pltpu.CompilerParams(vmem_limit_bytes=24 << 20),
        cost_estimate=pl.CostEstimate(
            flops=0, bytes_accessed=4 * count * 512, transcendentals=0
        ),
        name=name,
    )(index, pltpu.with_memory_space_constraint(table, pltpu.HBM), *late)


def pair_kernel(
    me_ref, local_hbm, other_hbm, out_ref, local_ref, other_ref, total_ref, sums_ref, sems
):
    me = me_ref[0]
    copies = [
        [
            pltpu.make_async_copy(source.at[a], target.at[a], sems.at[n, a])
            for n, (source, target) in enumerate(((local_hbm, local_ref), (other_hbm, other_ref)))
        ]
        for a in range(GROUPS)
    ]
    for pair in copies:
        for copy in pair:
            copy.start()
    rows = 2 * HALF
    lane = lax.broadcasted_iota(jnp.int32, (CHUNK, 128), 1)
    block = lane // 32
    unit = lane // 16
    inner = lane % 16
    i, j = inner // PER, inner % PER
    depth = lax.broadcasted_iota(jnp.int32, (512, 128), 0)
    column = lax.broadcasted_iota(jnp.int32, (512, 128), 1)
    turn = depth // 128
    second = (depth % 128) // 32
    place = ((second + turn) % PER) * PER + second
    collect = jnp.where(column % 16 == place, 1.0, 0.0).astype(jnp.bfloat16)
    odd = block % 2 == 1
    upper = block >= 2
    outer = (block == 0) | (block == 3)

    def turned(tiles):
        even_low = jnp.where(odd, tiles[1], tiles[0])
        even_high = jnp.where(odd, tiles[3], tiles[2])
        odd_low = jnp.where(odd, tiles[0], tiles[1])
        odd_high = jnp.where(odd, tiles[2], tiles[3])
        return (
            jnp.where(upper, even_high, even_low),
            jnp.where(outer, odd_low, odd_high),
            jnp.where(upper, even_low, even_high),
            jnp.where(outer, odd_high, odd_low),
        )

    def products(first, second):
        high, low = [], []
        lefts, rights = turned(first), turned(second)
        for d in range(PER):
            right = rights[-d % PER]
            if d:
                right = pltpu.roll(right, 128 - 32 * d, 1)
            value = lefts[d] * right
            rounded = value.astype(jnp.bfloat16)
            high.append(rounded)
            low.append((value - rounded.astype(jnp.float32)).astype(jnp.bfloat16))
        high = jnp.concatenate(high, axis=1)
        low = jnp.concatenate(low, axis=1)
        return jnp.dot(high, collect, preferred_element_type=jnp.float32) + jnp.dot(
            low, collect, preferred_element_type=jnp.float32
        )

    def tiles(ref, a, span):
        return [ref[a, n, span, :].astype(jnp.float32) for n in range(PER)]

    for a in range(GROUPS):
        for copy in copies[a]:
            copy.wait()

        for r in range(rows // CHUNK):
            span = pl.ds(r * CHUNK, CHUNK)
            dots = products(tiles(local_ref, a, span), tiles(other_ref, a, span))
            total_ref[span, :] = jnp.where(unit == a, dots, total_ref[span, :])

    for r in range(rows // CHUNK):
        span = pl.ds(r * CHUNK, CHUNK)
        own_first = tiles(other_ref, me, span)
        own_second = tiles(local_ref, me, span)
        first_dots = products(own_first, own_first)
        second_dots = products(own_second, own_second)
        total = total_ref[span, :]
        sums_ref[0, span, :] = jnp.where(
            unit < me, total, jnp.where((unit == me) & (i < j), first_dots, 0.0)
        )
        sums_ref[1, span, :] = jnp.where(
            unit > me, total, jnp.where((unit == me) & (i > j), second_dots, 0.0)
        )
    for half in range(2):
        value = sums_ref[half, pl.ds(0, HALF, stride=2), :] + sums_ref[
            half, pl.ds(1, HALF, stride=2), :
        ]
        out_ref[pl.ds(half * HALF, HALF), :] = value.astype(jnp.bfloat16)


def pair_products(me, local, other):
    return pl.pallas_call(
        pair_kernel,
        out_shape=jax.ShapeDtypeStruct((2 * HALF, 128), jnp.bfloat16),
        grid_spec=pltpu.PrefetchScalarGridSpec(
            num_scalar_prefetch=1,
            grid=(),
            in_specs=[
                pl.BlockSpec(memory_space=pltpu.HBM),
                pl.BlockSpec(memory_space=pl.ANY),
            ],
            out_specs=pl.BlockSpec(memory_space=pltpu.VMEM),
            scratch_shapes=[
                pltpu.VMEM((GROUPS, PER, 2 * HALF, 128), jnp.bfloat16),
                pltpu.VMEM((GROUPS, PER, 2 * HALF, 128), jnp.bfloat16),
                pltpu.VMEM((2 * HALF, 128), jnp.float32),
                pltpu.VMEM((2, 2 * HALF, 128), jnp.float32),
                pltpu.SemaphoreType.DMA((2, GROUPS)),
            ],
        ),
        compiler_params=pltpu.CompilerParams(vmem_limit_bytes=16 << 20),
        name="pair_products",
    )(
        me,
        pltpu.with_memory_space_constraint(local, pltpu.HBM),
        other,
    )


def network_kernel(dots_ref, first_hbm, hidden_hbm, out_weights_ref, out_ref, first, hidden, sems):
    layers = hidden.shape[0]
    size = hidden.shape[1] // GROUPS
    first_size = first.shape[0] // GROUPS
    first_copies = [
        pltpu.make_async_copy(
            first_hbm.at[pl.ds(b * first_size, first_size)],
            first.at[pl.ds(b * first_size, first_size)],
            sems.at[layers, b],
        )
        for b in range(GROUPS)
    ]
    hidden_copies = [
        [
            pltpu.make_async_copy(
                hidden_hbm.at[depth, pl.ds(b * size, size)],
                hidden.at[depth, pl.ds(b * size, size)],
                sems.at[depth, b],
            )
            for b in range(GROUPS)
        ]
        for depth in range(layers)
    ]
    for copies in [first_copies] + hidden_copies:
        for copy in copies:
            copy.start()

    def rounded(value):
        return jnp.maximum(value, 0.0).astype(jnp.bfloat16)

    samples = dots_ref.shape[1]
    value = jnp.zeros((samples, H), jnp.float32)
    for b in range(GROUPS):
        first_copies[b].wait()
        value = value + jnp.dot(
            dots_ref[b],
            first[pl.ds(b * first_size, first_size), :],
            preferred_element_type=jnp.float32,
        )
    units = rounded(value)
    for depth in range(layers):
        value = jnp.zeros((samples, H), jnp.float32)
        for b in range(GROUPS):
            hidden_copies[depth][b].wait()
            value = value + jnp.dot(
                units[:, b * size : (b + 1) * size],
                hidden[depth, pl.ds(b * size, size), :],
                preferred_element_type=jnp.float32,
            )
        units = rounded(value)
    product = units.astype(jnp.float32) * out_weights_ref[...].astype(jnp.float32)
    total = jnp.sum(product, axis=1, keepdims=True)
    out_ref[...] = jnp.broadcast_to(total, out_ref.shape)


def network(dots, first, hidden, out_weights):
    return pl.pallas_call(
        network_kernel,
        out_shape=jax.ShapeDtypeStruct((dots.shape[1], 128), jnp.float32),
        in_specs=[
            pl.BlockSpec(memory_space=pltpu.VMEM),
            pl.BlockSpec(memory_space=pltpu.HBM),
            pl.BlockSpec(memory_space=pltpu.HBM),
            pl.BlockSpec(memory_space=pltpu.VMEM),
        ],
        out_specs=pl.BlockSpec(memory_space=pltpu.VMEM),
        scratch_shapes=[
            pltpu.VMEM(first.shape, first.dtype),
            pltpu.VMEM(hidden.shape, hidden.dtype),
            pltpu.SemaphoreType.DMA((hidden.shape[0] + 1, GROUPS)),
        ],
        compiler_params=pltpu.CompilerParams(vmem_limit_bytes=26 << 20),
        name="network",
    )(
        dots,
        pltpu.with_memory_space_constraint(first, pltpu.HBM),
        pltpu.with_memory_space_constraint(hidden, pltpu.HBM),
        out_weights,
    )


def body(row_owner, row_slot, feature_table, w_first, w_hidden, w_out):
    samples = row_slot.shape[0]
    rows = feature_table.shape[0]
    me = lax.axis_index("field")
    mine = lax.axis_index("row")

    source = jnp.arange(2 * 128, dtype=jnp.int32)
    wanted = (source % 128) // 32 * K + source // 128 * 32 + source % 32
    reorder = (source[:, None] == wanted[None, :]).astype(jnp.bfloat16)
    packed = jnp.dot(feature_table, reorder, preferred_element_type=jnp.float32)
    packed = packed.astype(jnp.bfloat16).reshape(rows, 2, 128)
    table, late_slots, late = spread_shard(packed)

    full_hidden = lax.all_gather(w_hidden, "field", axis=1, tiled=True)

    owner = row_owner[:, :, 0]
    piece = (mine // NY - owner // NY) % NZ * NY + (mine % NY - owner % NY) % NY
    ids = (piece * rows + row_slot).T.reshape(GROUPS, PER, 2, HALF)
    early = (me <= jnp.arange(GROUPS, dtype=jnp.int32))[:, None, None]
    send_ids = jnp.where(early, ids[:, :, 0], ids[:, :, 1]).reshape(-1)
    local_ids = jnp.where(early, ids[:, :, 1], ids[:, :, 0]).reshape(-1)

    table, full_hidden = lax.optimization_barrier((table, full_hidden))

    sent = gather_rows(send_ids, table, late_slots, late, "gather_sent")
    other = lax.all_to_all(
        sent.reshape(GROUPS, PER * HALF, 2, 128), "field", split_axis=0, concat_axis=0, tiled=True
    )
    local = gather_rows(local_ids, table, late_slots, late, "gather_local")
    local, w_pairs = lax.optimization_barrier((local, w_first))

    col = jnp.arange(F * F, dtype=jnp.int32)
    b, a, i, j = col // 128, col // 16 % 8, col // 4 % 4, col % 4
    forward = (a * PER + i) * F + b * PER + j
    backward = (b * PER + j) * F + a * PER + i
    rows_of = jnp.where(me < GROUPS // 2, forward, backward)
    first_order = (rows_of[:, None] == col[None, :]).astype(jnp.bfloat16)
    first = jnp.dot(
        first_order, w_pairs.reshape(F * F, H), preferred_element_type=jnp.float32
    ).astype(jnp.bfloat16)
    local, first = lax.optimization_barrier((local, first))
    dots = pair_products(
        me.reshape(1),
        local.reshape(GROUPS, PER, 2 * HALF, 128),
        other.reshape(GROUPS, PER, 2 * HALF, 128),
    )
    block = samples // GROUPS
    own_dots = lax.all_to_all(
        dots.reshape(GROUPS, block, 128), "field", split_axis=0, concat_axis=0, tiled=True
    )
    logits = network(own_dots, first, full_hidden, w_out.reshape(1, H))[:, 0]
    everyone = lax.all_to_all(
        jnp.broadcast_to(logits[None], (GROUPS, block)),
        "field",
        split_axis=0,
        concat_axis=0,
        tiled=True,
    )
    return everyone.reshape(samples)


def solution(mesh):
    placed = (
        P("row", None, None),
        P("row", None),
        P("row", "field"),
        P(),
        P(None, "field", None),
        P(),
    )
    return jax.shard_map(body, mesh=mesh, in_specs=placed, out_specs=P("row"), check_vma=False)
```

```python
import functools

import jax
import jax.numpy as jnp
from jax import lax
from jax.experimental import pallas as pl
from jax.experimental.pallas import tpu as pltpu
from jax.sharding import PartitionSpec as P

F = 32
K = 64
H = 2048
NZ = 8
NY = 4
GROUPS = 8
PER = 4
HALF = 128
LAG = 2
CHUNK = 128

DIRECTIONS = ((1, 0), (-1, 0), (0, 1), (0, -1))
SPREAD = (
    ((2, (0, 0), (0, 1)), (0, (0, 0), (1, 0)), (3, (0, 0), (0, 3)), (1, (0, 0), (7, 0))),
    ((1, (0, 1), (7, 1)), (0, (1, 0), (2, 0)), (3, (1, 0), (1, 3)), (2, (1, 0), (1, 1))),
    ((0, (2, 0), (3, 0)), (3, (7, 0), (7, 3)), (1, (7, 0), (6, 0)), (2, (0, 1), (0, 2))),
    ((2, (7, 1), (7, 2)), (1, (7, 1), (6, 1)), (0, (1, 3), (2, 3)), (3, (1, 3), (1, 2))),
    ((0, (3, 0), (4, 0)), (3, (6, 0), (6, 3)), (2, (3, 0), (3, 1)), (1, (6, 0), (5, 0))),
    ((3, (2, 3), (2, 2)), (1, (6, 1), (5, 1)), (2, (6, 1), (6, 2)), (0, (2, 3), (3, 3))),
    ((1, (3, 1), (2, 1)), (2, (3, 1), (3, 2)), (0, (3, 1), (4, 1)), (3, (4, 0), (4, 3))),
    ((2, (5, 1), (5, 2)), (3, (5, 0), (5, 3)), (0, (3, 2), (4, 2))),
)


def step_pairs(direction):
    dz, dy = direction
    return [
        (z * NY + y, ((z + dz) % NZ) * NY + (y + dy) % NY) for z in range(NZ) for y in range(NY)
    ]


def place_kernel(slots, rows, *refs):
    pieces, table, sems = refs[: len(slots)], refs[-2], refs[-1]
    copies = [
        pltpu.make_async_copy(piece, table.at[pl.ds(slot * rows, rows)], sems.at[n])
        for n, (slot, piece) in enumerate(zip(slots, pieces))
    ]
    for copy in copies:
        copy.start()
    for copy in copies:
        copy.wait()


def place_pieces(table, slots, pieces):
    rows = pieces[0].shape[0]
    shape = (NZ * NY * rows,) + pieces[0].shape[1:]
    held = [] if table is None else [table]
    count = len(pieces)
    return pl.pallas_call(
        functools.partial(place_kernel, slots, rows),
        out_shape=pltpu.HBM(shape, pieces[0].dtype),
        in_specs=[pl.BlockSpec(memory_space=pltpu.VMEM)] * count
        + [pl.BlockSpec(memory_space=pltpu.HBM)] * len(held),
        out_specs=pl.BlockSpec(memory_space=pltpu.HBM),
        scratch_shapes=[pltpu.SemaphoreType.DMA((count,))],
        input_output_aliases={count: 0} if held else {},
        compiler_params=pltpu.CompilerParams(vmem_limit_bytes=8 << 20),
        cost_estimate=pl.CostEstimate(
            flops=0, bytes_accessed=2 * count * rows * 512, transcendentals=0
        ),
        name="place",
    )(*pieces, *held)


def slot_of(name):
    return name[0] * NY + name[1]


def spread_shard(own):
    pieces = {(0, 0): own}
    table = place_pieces(None, [0], [own])
    waiting = []
    for step in SPREAD:
        sources = sorted({source for _, source, _ in step})
        kept = lax.optimization_barrier(([pieces[source] for source in sources], table))
        ready, table = dict(zip(sources, kept[0])), kept[1]
        for way, source, target in step:
            pieces[target] = lax.ppermute(ready[source], "row", step_pairs(DIRECTIONS[way]))
        waiting.append([target for _, _, target in step])
        if len(waiting) >= LAG and step is not SPREAD[-1]:
            names = waiting.pop(0)
            table = place_pieces(table, [slot_of(n) for n in names], [pieces[n] for n in names])
    late = waiting[0] + waiting[1]
    return table, [slot_of(n) for n in late], [pieces[n] for n in late]


def gather_kernel(count, parts, late_slots, index, table_hbm, *refs):
    late, (out, found, table, load_sems, sems) = refs[: len(late_slots)], refs[len(late_slots) :]
    rows = table.shape[0] // (NZ * NY)
    loads = []
    for slot in range(NZ * NY):
        span = pl.ds(slot * rows, rows)
        source = late[late_slots.index(slot)] if slot in late_slots else table_hbm.at[span]
        loads.append(pltpu.make_async_copy(source, table.at[span], load_sems.at[slot]))
    for copy in loads:
        copy.start()
    for copy in loads:
        copy.wait()
    unroll = 32
    size = count // parts
    leaving = []
    for part in range(parts):

        def some(i, carry):
            first = part * size + i * unroll
            for u in range(unroll):
                found[first + u] = table[index[first + u]]
            return carry

        lax.fori_loop(0, size // unroll, some, 0)
        span = pl.ds(part * size, size)
        leaving.append(pltpu.make_async_copy(found.at[span], out.at[span], sems.at[part]))
        leaving[-1].start()
    for copy in leaving:
        copy.wait()


def gather_rows(index, table, late_slots, late, name):
    count = index.shape[0]
    parts = 8
    return pl.pallas_call(
        functools.partial(gather_kernel, count, parts, late_slots),
        out_shape=pltpu.HBM((count, 2, 128), jnp.bfloat16),
        grid_spec=pltpu.PrefetchScalarGridSpec(
            num_scalar_prefetch=1,
            grid=(),
            in_specs=[pl.BlockSpec(memory_space=pltpu.HBM)]
            + [pl.BlockSpec(memory_space=pl.ANY)] * len(late),
            out_specs=pl.BlockSpec(memory_space=pltpu.HBM),
            scratch_shapes=[
                pltpu.VMEM((count, 2, 128), jnp.bfloat16),
                pltpu.VMEM(table.shape, table.dtype),
                pltpu.SemaphoreType.DMA((NZ * NY,)),
                pltpu.SemaphoreType.DMA((parts,)),
            ],
        ),
        compiler_params=pltpu.CompilerParams(vmem_limit_bytes=24 << 20),
        cost_estimate=pl.CostEstimate(
            flops=0, bytes_accessed=4 * count * 512, transcendentals=0
        ),
        name=name,
    )(index, pltpu.with_memory_space_constraint(table, pltpu.HBM), *late)


def pair_kernel(
    me_ref, local_hbm, other_hbm, out_ref, local_ref, other_ref, total_ref, sums_ref, sems
):
    me = me_ref[0]
    copies = [
        [
            pltpu.make_async_copy(source.at[a], target.at[a], sems.at[n, a])
            for n, (source, target) in enumerate(((local_hbm, local_ref), (other_hbm, other_ref)))
        ]
        for a in range(GROUPS)
    ]
    for pair in copies:
        for copy in pair:
            copy.start()
    rows = 2 * HALF
    lane = lax.broadcasted_iota(jnp.int32, (CHUNK, 128), 1)
    block = lane // 32
    unit = lane // 16
    inner = lane % 16
    i, j = inner // PER, inner % PER
    depth = lax.broadcasted_iota(jnp.int32, (512, 128), 0)
    column = lax.broadcasted_iota(jnp.int32, (512, 128), 1)
    turn = depth // 128
    second = (depth % 128) // 32
    place = ((second + turn) % PER) * PER + second
    collect = jnp.where(column % 16 == place, 1.0, 0.0).astype(jnp.bfloat16)
    odd = block % 2 == 1
    upper = block >= 2
    outer = (block == 0) | (block == 3)

    def turned(tiles):
        even_low = jnp.where(odd, tiles[1], tiles[0])
        even_high = jnp.where(odd, tiles[3], tiles[2])
        odd_low = jnp.where(odd, tiles[0], tiles[1])
        odd_high = jnp.where(odd, tiles[2], tiles[3])
        return (
            jnp.where(upper, even_high, even_low),
            jnp.where(outer, odd_low, odd_high),
            jnp.where(upper, even_low, even_high),
            jnp.where(outer, odd_high, odd_low),
        )

    def products(first, second):
        high, low = [], []
        lefts, rights = turned(first), turned(second)
        for d in range(PER):
            right = rights[-d % PER]
            if d:
                right = pltpu.roll(right, 128 - 32 * d, 1)
            value = lefts[d] * right
            rounded = value.astype(jnp.bfloat16)
            high.append(rounded)
            low.append((value - rounded.astype(jnp.float32)).astype(jnp.bfloat16))
        high = jnp.concatenate(high, axis=1)
        low = jnp.concatenate(low, axis=1)
        return jnp.dot(high, collect, preferred_element_type=jnp.float32) + jnp.dot(
            low, collect, preferred_element_type=jnp.float32
        )

    def tiles(ref, a, span):
        return [ref[a, n, span, :].astype(jnp.float32) for n in range(PER)]

    for a in range(GROUPS):
        for copy in copies[a]:
            copy.wait()

        for r in range(rows // CHUNK):
            span = pl.ds(r * CHUNK, CHUNK)
            dots = products(tiles(local_ref, a, span), tiles(other_ref, a, span))
            total_ref[span, :] = jnp.where(unit == a, dots, total_ref[span, :])

    for r in range(rows // CHUNK):
        span = pl.ds(r * CHUNK, CHUNK)
        own_first = tiles(other_ref, me, span)
        own_second = tiles(local_ref, me, span)
        first_dots = products(own_first, own_first)
        second_dots = products(own_second, own_second)
        total = total_ref[span, :]
        sums_ref[0, span, :] = jnp.where(
            unit < me, total, jnp.where((unit == me) & (i < j), first_dots, 0.0)
        )
        sums_ref[1, span, :] = jnp.where(
            unit > me, total, jnp.where((unit == me) & (i > j), second_dots, 0.0)
        )
    for half in range(2):
        value = sums_ref[half, pl.ds(0, HALF, stride=2), :] + sums_ref[
            half, pl.ds(1, HALF, stride=2), :
        ]
        out_ref[pl.ds(half * HALF, HALF), :] = value.astype(jnp.bfloat16)


def pair_products(me, local, other):
    return pl.pallas_call(
        pair_kernel,
        out_shape=jax.ShapeDtypeStruct((2 * HALF, 128), jnp.bfloat16),
        grid_spec=pltpu.PrefetchScalarGridSpec(
            num_scalar_prefetch=1,
            grid=(),
            in_specs=[
                pl.BlockSpec(memory_space=pltpu.HBM),
                pl.BlockSpec(memory_space=pl.ANY),
            ],
            out_specs=pl.BlockSpec(memory_space=pltpu.VMEM),
            scratch_shapes=[
                pltpu.VMEM((GROUPS, PER, 2 * HALF, 128), jnp.bfloat16),
                pltpu.VMEM((GROUPS, PER, 2 * HALF, 128), jnp.bfloat16),
                pltpu.VMEM((2 * HALF, 128), jnp.float32),
                pltpu.VMEM((2, 2 * HALF, 128), jnp.float32),
                pltpu.SemaphoreType.DMA((2, GROUPS)),
            ],
        ),
        compiler_params=pltpu.CompilerParams(vmem_limit_bytes=16 << 20),
        name="pair_products",
    )(
        me,
        pltpu.with_memory_space_constraint(local, pltpu.HBM),
        other,
    )


def network_kernel(dots_ref, first_hbm, hidden_hbm, out_weights_ref, out_ref, first, hidden, sems):
    layers = hidden.shape[0]
    size = hidden.shape[1] // GROUPS
    first_size = first.shape[0] // GROUPS
    first_copies = [
        pltpu.make_async_copy(
            first_hbm.at[pl.ds(b * first_size, first_size)],
            first.at[pl.ds(b * first_size, first_size)],
            sems.at[layers, b],
        )
        for b in range(GROUPS)
    ]
    hidden_copies = [
        [
            pltpu.make_async_copy(
                hidden_hbm.at[depth, pl.ds(b * size, size)],
                hidden.at[depth, pl.ds(b * size, size)],
                sems.at[depth, b],
            )
            for b in range(GROUPS)
        ]
        for depth in range(layers)
    ]
    for copies in [first_copies] + hidden_copies:
        for copy in copies:
            copy.start()

    def rounded(value):
        return jnp.maximum(value, 0.0).astype(jnp.bfloat16)

    samples = dots_ref.shape[1]
    value = jnp.zeros((samples, H), jnp.float32)
    for b in range(GROUPS):
        first_copies[b].wait()
        value = value + jnp.dot(
            dots_ref[b],
            first[pl.ds(b * first_size, first_size), :],
            preferred_element_type=jnp.float32,
        )
    units = rounded(value)
    for depth in range(layers):
        value = jnp.zeros((samples, H), jnp.float32)
        for b in range(GROUPS):
            hidden_copies[depth][b].wait()
            value = value + jnp.dot(
                units[:, b * size : (b + 1) * size],
                hidden[depth, pl.ds(b * size, size), :],
                preferred_element_type=jnp.float32,
            )
        units = rounded(value)
    product = units.astype(jnp.float32) * out_weights_ref[...].astype(jnp.float32)
    total = jnp.sum(product, axis=1, keepdims=True)
    out_ref[...] = jnp.broadcast_to(total, out_ref.shape)


def network(dots, first, hidden, out_weights):
    return pl.pallas_call(
        network_kernel,
        out_shape=jax.ShapeDtypeStruct((dots.shape[1], 128), jnp.float32),
        in_specs=[
            pl.BlockSpec(memory_space=pltpu.VMEM),
            pl.BlockSpec(memory_space=pltpu.HBM),
            pl.BlockSpec(memory_space=pltpu.HBM),
            pl.BlockSpec(memory_space=pltpu.VMEM),
        ],
        out_specs=pl.BlockSpec(memory_space=pltpu.VMEM),
        scratch_shapes=[
            pltpu.VMEM(first.shape, first.dtype),
            pltpu.VMEM(hidden.shape, hidden.dtype),
            pltpu.SemaphoreType.DMA((hidden.shape[0] + 1, GROUPS)),
        ],
        compiler_params=pltpu.CompilerParams(vmem_limit_bytes=26 << 20),
        name="network",
    )(
        dots,
        pltpu.with_memory_space_constraint(first, pltpu.HBM),
        pltpu.with_memory_space_constraint(hidden, pltpu.HBM),
        out_weights,
    )


def body(row_owner, row_slot, feature_table, w_first, w_hidden, w_out):
    samples = row_slot.shape[0]
    rows = feature_table.shape[0]
    me = lax.axis_index("field")
    mine = lax.axis_index("row")

    source = jnp.arange(2 * 128, dtype=jnp.int32)
    wanted = (source % 128) // 32 * K + source // 128 * 32 + source % 32
    reorder = (source[:, None] == wanted[None, :]).astype(jnp.bfloat16)
    packed = jnp.dot(feature_table, reorder, preferred_element_type=jnp.float32)
    packed = packed.astype(jnp.bfloat16).reshape(rows, 2, 128)
    table, late_slots, late = spread_shard(packed)

    full_hidden = lax.all_gather(w_hidden, "field", axis=1, tiled=True)

    owner = row_owner[:, :, 0]
    piece = (mine // NY - owner // NY) % NZ * NY + (mine % NY - owner % NY) % NY
    ids = (piece * rows + row_slot).T.reshape(GROUPS, PER, 2, HALF)
    early = (me <= jnp.arange(GROUPS, dtype=jnp.int32))[:, None, None]
    send_ids = jnp.where(early, ids[:, :, 0], ids[:, :, 1]).reshape(-1)
    local_ids = jnp.where(early, ids[:, :, 1], ids[:, :, 0]).reshape(-1)

    table, full_hidden = lax.optimization_barrier((table, full_hidden))

    sent = gather_rows(send_ids, table, late_slots, late, "gather_sent")
    other = lax.all_to_all(
        sent.reshape(GROUPS, PER * HALF, 2, 128), "field", split_axis=0, concat_axis=0, tiled=True
    )
    local = gather_rows(local_ids, table, late_slots, late, "gather_local")
    local, w_pairs = lax.optimization_barrier((local, w_first))

    col = jnp.arange(F * F, dtype=jnp.int32)
    b, a, i, j = col // 128, col // 16 % 8, col // 4 % 4, col % 4
    forward = (a * PER + i) * F + b * PER + j
    backward = (b * PER + j) * F + a * PER + i
    rows_of = jnp.where(me < GROUPS // 2, forward, backward)
    first_order = (rows_of[:, None] == col[None, :]).astype(jnp.bfloat16)
    first = jnp.dot(
        first_order, w_pairs.reshape(F * F, H), preferred_element_type=jnp.float32
    ).astype(jnp.bfloat16)
    local, first = lax.optimization_barrier((local, first))
    dots = pair_products(
        me.reshape(1),
        local.reshape(GROUPS, PER, 2 * HALF, 128),
        other.reshape(GROUPS, PER, 2 * HALF, 128),
    )
    block = samples // GROUPS
    own_dots = lax.all_to_all(
        dots.reshape(GROUPS, block, 128), "field", split_axis=0, concat_axis=0, tiled=True
    )
    logits = network(own_dots, first, full_hidden, w_out.reshape(1, H))[:, 0]
    everyone = lax.all_to_all(
        jnp.broadcast_to(logits[None], (GROUPS, block)),
        "field",
        split_axis=0,
        concat_axis=0,
        tiled=True,
    )
    return everyone.reshape(samples)


def solution(mesh):
    placed = (
        P("row", None, None),
        P("row", None),
        P("row", "field"),
        P(),
        P(None, "field", None),
        P(),
    )
    return jax.shard_map(body, mesh=mesh, in_specs=placed, out_specs=P("row"), check_vma=False)
```

```python
import functools

import jax
import jax.numpy as jnp
from jax import lax
from jax.experimental import pallas as pl
from jax.experimental.pallas import tpu as pltpu
from jax.sharding import PartitionSpec as P

F = 32
K = 64
H = 2048
NZ = 8
NY = 4
NX = 4
GROUPS = 8
PER = 4
HALF = 128
LAG = 2
CHUNK = 128

DIRECTIONS = ((1, 0), (-1, 0), (0, 1), (0, -1))
SPREAD = (
    ((2, (0, 0), (0, 1)), (0, (0, 0), (1, 0)), (3, (0, 0), (0, 3)), (1, (0, 0), (7, 0))),
    ((1, (0, 1), (7, 1)), (0, (1, 0), (2, 0)), (3, (1, 0), (1, 3)), (2, (1, 0), (1, 1))),
    ((0, (2, 0), (3, 0)), (3, (7, 0), (7, 3)), (1, (7, 0), (6, 0)), (2, (0, 1), (0, 2))),
    ((2, (7, 1), (7, 2)), (1, (7, 1), (6, 1)), (0, (1, 3), (2, 3)), (3, (1, 3), (1, 2))),
    ((0, (3, 0), (4, 0)), (3, (6, 0), (6, 3)), (2, (3, 0), (3, 1)), (1, (6, 0), (5, 0))),
    ((3, (2, 3), (2, 2)), (1, (6, 1), (5, 1)), (2, (6, 1), (6, 2)), (0, (2, 3), (3, 3))),
    ((1, (3, 1), (2, 1)), (2, (3, 1), (3, 2)), (0, (3, 1), (4, 1)), (3, (4, 0), (4, 3))),
    ((2, (5, 1), (5, 2)), (3, (5, 0), (5, 3)), (0, (3, 2), (4, 2))),
)


def step_pairs(direction):
    dz, dy = direction
    return [
        (z * NY + y, ((z + dz) % NZ) * NY + (y + dy) % NY) for z in range(NZ) for y in range(NY)
    ]


def place_kernel(slots, rows, *refs):
    pieces, table, sems = refs[: len(slots)], refs[-2], refs[-1]
    copies = [
        pltpu.make_async_copy(piece, table.at[pl.ds(slot * rows, rows)], sems.at[n])
        for n, (slot, piece) in enumerate(zip(slots, pieces))
    ]
    for copy in copies:
        copy.start()
    for copy in copies:
        copy.wait()


def place_pieces(table, slots, pieces):
    rows = pieces[0].shape[0]
    shape = (NZ * NY * rows,) + pieces[0].shape[1:]
    held = [] if table is None else [table]
    count = len(pieces)
    return pl.pallas_call(
        functools.partial(place_kernel, slots, rows),
        out_shape=pltpu.HBM(shape, pieces[0].dtype),
        in_specs=[pl.BlockSpec(memory_space=pltpu.VMEM)] * count
        + [pl.BlockSpec(memory_space=pltpu.HBM)] * len(held),
        out_specs=pl.BlockSpec(memory_space=pltpu.HBM),
        scratch_shapes=[pltpu.SemaphoreType.DMA((count,))],
        input_output_aliases={count: 0} if held else {},
        compiler_params=pltpu.CompilerParams(vmem_limit_bytes=8 << 20),
        cost_estimate=pl.CostEstimate(
            flops=0, bytes_accessed=2 * count * rows * 512, transcendentals=0
        ),
        name="place",
    )(*pieces, *held)


def slot_of(name):
    return name[0] * NY + name[1]


def ring_pairs(offset):
    return [
        (x * 2 + core, (x + offset) % NX * 2 + core) for x in range(NX) for core in range(2)
    ]


def twin_pairs():
    return [(index, index ^ 1) for index in range(2 * NX)]


class Weights:
    def __init__(self, own):
        self.own = own

    def values(self, number):
        if number in (0, 1):
            return [self.own]
        if number == 4:
            return [self.up, self.down]
        if number == 5:
            return [self.up]
        if number == 6:
            return [self.down]
        if number == 7:
            return [self.far_up, self.far_down]
        return []

    def send(self, number, ready):
        if number == 0:
            self.up = lax.ppermute(ready[0], "field", ring_pairs(1))
            self.down = lax.ppermute(ready[0], "field", ring_pairs(-1))
        elif number == 1:
            self.twin = lax.ppermute(ready[0], "field", twin_pairs())
        elif number == 4:
            self.up, self.down = ready
            self.far_up = lax.ppermute(self.up[0], "field", ring_pairs(1))
            self.far_down = lax.ppermute(self.down[1], "field", ring_pairs(-1))
        elif number == 5:
            self.twin_up = lax.ppermute(ready[0], "field", twin_pairs())
        elif number == 6:
            self.twin_down = lax.ppermute(ready[0], "field", twin_pairs())
        elif number == 7:
            self.far_up, self.far_down = ready
            self.twin_far_up = lax.ppermute(self.far_up, "field", twin_pairs())
            self.twin_far_down = lax.ppermute(self.far_down, "field", twin_pairs())

    def parts(self):
        me = lax.axis_index("field")
        x, core = me // 2, me % 2
        whole = (self.own, self.twin, self.up, self.twin_up, self.down, self.twin_down)
        arrays = whole + (self.far_up, self.far_down, self.twin_far_up, self.twin_far_down)
        order = []
        for offset in (0, -1, 1, 2):
            chip = (x + NX + offset) % NX
            order += [chip * 2 + core, chip * 2 + 1 - core]
        return arrays, jnp.stack(order).astype(jnp.int32)


def spread_shard(own, weights):
    pieces = {(0, 0): own}
    table = place_pieces(None, [0], [own])
    waiting = []
    for number, step in enumerate(SPREAD):
        sources = sorted({source for _, source, _ in step})
        kept = lax.optimization_barrier(
            ([pieces[source] for source in sources], table, weights.values(number))
        )
        ready, table = dict(zip(sources, kept[0])), kept[1]
        for way, source, target in step:
            pieces[target] = lax.ppermute(ready[source], "row", step_pairs(DIRECTIONS[way]))
        weights.send(number, kept[2])
        waiting.append([target for _, _, target in step])
        if len(waiting) >= LAG and step is not SPREAD[-1]:
            names = waiting.pop(0)
            table = place_pieces(table, [slot_of(n) for n in names], [pieces[n] for n in names])
    late = waiting[0] + waiting[1]
    return table, [slot_of(n) for n in late], [pieces[n] for n in late]


def gather_kernel(count, parts, late_slots, index, table_hbm, *refs):
    late, (out, found, table, load_sems, sems) = refs[: len(late_slots)], refs[len(late_slots) :]
    rows = table.shape[0] // (NZ * NY)
    loads = []
    for slot in range(NZ * NY):
        span = pl.ds(slot * rows, rows)
        source = late[late_slots.index(slot)] if slot in late_slots else table_hbm.at[span]
        loads.append(pltpu.make_async_copy(source, table.at[span], load_sems.at[slot]))
    for copy in loads:
        copy.start()
    for copy in loads:
        copy.wait()
    unroll = 32
    size = count // parts
    leaving = []
    for part in range(parts):

        def some(i, carry):
            first = part * size + i * unroll
            for u in range(unroll):
                found[first + u] = table[index[first + u]]
            return carry

        lax.fori_loop(0, size // unroll, some, 0)
        span = pl.ds(part * size, size)
        leaving.append(pltpu.make_async_copy(found.at[span], out.at[span], sems.at[part]))
        leaving[-1].start()
    for copy in leaving:
        copy.wait()


def gather_rows(index, table, late_slots, late, name):
    count = index.shape[0]
    parts = 8
    return pl.pallas_call(
        functools.partial(gather_kernel, count, parts, late_slots),
        out_shape=pltpu.HBM((count, 2, 128), jnp.bfloat16),
        grid_spec=pltpu.PrefetchScalarGridSpec(
            num_scalar_prefetch=1,
            grid=(),
            in_specs=[pl.BlockSpec(memory_space=pltpu.HBM)]
            + [pl.BlockSpec(memory_space=pl.ANY)] * len(late),
            out_specs=pl.BlockSpec(memory_space=pltpu.HBM),
            scratch_shapes=[
                pltpu.VMEM((count, 2, 128), jnp.bfloat16),
                pltpu.VMEM(table.shape, table.dtype),
                pltpu.SemaphoreType.DMA((NZ * NY,)),
                pltpu.SemaphoreType.DMA((parts,)),
            ],
        ),
        compiler_params=pltpu.CompilerParams(vmem_limit_bytes=24 << 20),
        cost_estimate=pl.CostEstimate(
            flops=0, bytes_accessed=4 * count * 512, transcendentals=0
        ),
        name=name,
    )(index, pltpu.with_memory_space_constraint(table, pltpu.HBM), *late)


def pair_kernel(
    me_ref, local_hbm, other_hbm, out_ref, local_ref, other_ref, total_ref, sums_ref, sems
):
    me = me_ref[0]
    copies = [
        [
            pltpu.make_async_copy(source.at[a], target.at[a], sems.at[n, a])
            for n, (source, target) in enumerate(((local_hbm, local_ref), (other_hbm, other_ref)))
        ]
        for a in range(GROUPS)
    ]
    for pair in copies:
        for copy in pair:
            copy.start()
    rows = 2 * HALF
    lane = lax.broadcasted_iota(jnp.int32, (CHUNK, 128), 1)
    block = lane // 32
    unit = lane // 16
    inner = lane % 16
    i, j = inner // PER, inner % PER
    depth = lax.broadcasted_iota(jnp.int32, (512, 128), 0)
    column = lax.broadcasted_iota(jnp.int32, (512, 128), 1)
    turn = depth // 128
    second = (depth % 128) // 32
    place = ((second + turn) % PER) * PER + second
    collect = jnp.where(column % 16 == place, 1.0, 0.0).astype(jnp.bfloat16)
    odd = block % 2 == 1
    upper = block >= 2
    outer = (block == 0) | (block == 3)

    def turned(tiles):
        even_low = jnp.where(odd, tiles[1], tiles[0])
        even_high = jnp.where(odd, tiles[3], tiles[2])
        odd_low = jnp.where(odd, tiles[0], tiles[1])
        odd_high = jnp.where(odd, tiles[2], tiles[3])
        return (
            jnp.where(upper, even_high, even_low),
            jnp.where(outer, odd_low, odd_high),
            jnp.where(upper, even_low, even_high),
            jnp.where(outer, odd_high, odd_low),
        )

    def products(first, second):
        high, low = [], []
        lefts, rights = turned(first), turned(second)
        for d in range(PER):
            right = rights[-d % PER]
            if d:
                right = pltpu.roll(right, 128 - 32 * d, 1)
            value = lefts[d] * right
            rounded = value.astype(jnp.bfloat16)
            high.append(rounded)
            low.append((value - rounded.astype(jnp.float32)).astype(jnp.bfloat16))
        high = jnp.concatenate(high, axis=1)
        low = jnp.concatenate(low, axis=1)
        return jnp.dot(high, collect, preferred_element_type=jnp.float32) + jnp.dot(
            low, collect, preferred_element_type=jnp.float32
        )

    def tiles(ref, a, span):
        return [ref[a, n, span, :].astype(jnp.float32) for n in range(PER)]

    for a in range(GROUPS):
        for copy in copies[a]:
            copy.wait()

        for r in range(rows // CHUNK):
            span = pl.ds(r * CHUNK, CHUNK)
            dots = products(tiles(local_ref, a, span), tiles(other_ref, a, span))
            total_ref[span, :] = jnp.where(unit == a, dots, total_ref[span, :])

    for r in range(rows // CHUNK):
        span = pl.ds(r * CHUNK, CHUNK)
        own_first = tiles(other_ref, me, span)
        own_second = tiles(local_ref, me, span)
        first_dots = products(own_first, own_first)
        second_dots = products(own_second, own_second)
        total = total_ref[span, :]
        sums_ref[0, span, :] = jnp.where(
            unit < me, total, jnp.where((unit == me) & (i < j), first_dots, 0.0)
        )
        sums_ref[1, span, :] = jnp.where(
            unit > me, total, jnp.where((unit == me) & (i > j), second_dots, 0.0)
        )
    for half in range(2):
        value = sums_ref[half, pl.ds(0, HALF, stride=2), :] + sums_ref[
            half, pl.ds(1, HALF, stride=2), :
        ]
        out_ref[pl.ds(half * HALF, HALF), :] = value.astype(jnp.bfloat16)


def pair_products(me, local, other):
    return pl.pallas_call(
        pair_kernel,
        out_shape=jax.ShapeDtypeStruct((2 * HALF, 128), jnp.bfloat16),
        grid_spec=pltpu.PrefetchScalarGridSpec(
            num_scalar_prefetch=1,
            grid=(),
            in_specs=[
                pl.BlockSpec(memory_space=pltpu.HBM),
                pl.BlockSpec(memory_space=pl.ANY),
            ],
            out_specs=pl.BlockSpec(memory_space=pltpu.VMEM),
            scratch_shapes=[
                pltpu.VMEM((GROUPS, PER, 2 * HALF, 128), jnp.bfloat16),
                pltpu.VMEM((GROUPS, PER, 2 * HALF, 128), jnp.bfloat16),
                pltpu.VMEM((2 * HALF, 128), jnp.float32),
                pltpu.VMEM((2, 2 * HALF, 128), jnp.float32),
                pltpu.SemaphoreType.DMA((2, GROUPS)),
            ],
        ),
        compiler_params=pltpu.CompilerParams(vmem_limit_bytes=16 << 20),
        name="pair_products",
    )(
        me,
        pltpu.with_memory_space_constraint(local, pltpu.HBM),
        other,
    )


def network_kernel(order_ref, dots_ref, first_hbm, out_weights_ref, *refs):
    wholes, fars, (out_ref, first, hidden, units, sems) = refs[:6], refs[6:10], refs[10:]
    layers = hidden.shape[0]
    size = first.shape[0] // GROUPS
    first_copies = [
        pltpu.make_async_copy(
            first_hbm.at[pl.ds(b * size, size)], first.at[pl.ds(b * size, size)], sems.at[layers, b]
        )
        for b in range(GROUPS)
    ]
    hidden_copies = []
    for depth in range(layers):
        sources = [ref.at[depth] for ref in wholes] + [fars[depth], fars[2 + depth]]
        hidden_copies.append(
            [
                pltpu.make_async_copy(source, hidden.at[depth, n], sems.at[depth, n])
                for n, source in enumerate(sources)
            ]
        )
    for copies in [first_copies] + hidden_copies:
        for copy in copies:
            copy.start()

    def rounded(value):
        return jnp.maximum(value, 0.0).astype(jnp.bfloat16)

    samples = dots_ref.shape[1]
    width = units.shape[2]
    value = jnp.zeros((samples, H), jnp.float32)
    for b in range(GROUPS):
        first_copies[b].wait()
        value = value + jnp.dot(
            dots_ref[b], first[pl.ds(b * size, size), :], preferred_element_type=jnp.float32
        )
    for depth in range(layers):
        state = rounded(value)
        for n in range(GROUPS):
            units[n] = state[:, n * width : (n + 1) * width]
        value = jnp.zeros((samples, H), jnp.float32)
        for n in range(GROUPS):
            hidden_copies[depth][n].wait()
            value = value + jnp.dot(
                units[order_ref[n]], hidden[depth, n], preferred_element_type=jnp.float32
            )
    state = rounded(value)
    product = state.astype(jnp.float32) * out_weights_ref[...].astype(jnp.float32)
    total = jnp.sum(product, axis=1, keepdims=True)
    out_ref[...] = jnp.broadcast_to(total, out_ref.shape)


def network(order, dots, first, out_weights, arrays):
    layers, width, _ = arrays[0].shape
    return pl.pallas_call(
        network_kernel,
        out_shape=jax.ShapeDtypeStruct((dots.shape[1], 128), jnp.float32),
        grid_spec=pltpu.PrefetchScalarGridSpec(
            num_scalar_prefetch=1,
            grid=(),
            in_specs=[
                pl.BlockSpec(memory_space=pltpu.VMEM),
                pl.BlockSpec(memory_space=pltpu.HBM),
                pl.BlockSpec(memory_space=pltpu.VMEM),
            ]
            + [pl.BlockSpec(memory_space=pl.ANY)] * len(arrays),
            out_specs=pl.BlockSpec(memory_space=pltpu.VMEM),
            scratch_shapes=[
                pltpu.VMEM(first.shape, first.dtype),
                pltpu.VMEM((layers, GROUPS, width, H), arrays[0].dtype),
                pltpu.VMEM((GROUPS, dots.shape[1], width), jnp.bfloat16),
                pltpu.SemaphoreType.DMA((layers + 1, GROUPS)),
            ],
        ),
        compiler_params=pltpu.CompilerParams(vmem_limit_bytes=26 << 20),
        name="network",
    )(
        order,
        dots,
        pltpu.with_memory_space_constraint(first, pltpu.HBM),
        out_weights,
        *arrays,
    )


def body(row_owner, row_slot, feature_table, w_first, w_hidden, w_out):
    samples = row_slot.shape[0]
    rows = feature_table.shape[0]
    me = lax.axis_index("field")
    mine = lax.axis_index("row")

    source = jnp.arange(2 * 128, dtype=jnp.int32)
    wanted = (source % 128) // 32 * K + source // 128 * 32 + source % 32
    reorder = (source[:, None] == wanted[None, :]).astype(jnp.bfloat16)
    packed = jnp.dot(feature_table, reorder, preferred_element_type=jnp.float32)
    packed = packed.astype(jnp.bfloat16).reshape(rows, 2, 128)
    weights = Weights(w_hidden)
    table, late_slots, late = spread_shard(packed, weights)
    parts, order = weights.parts()

    owner = row_owner[:, :, 0]
    piece = (mine // NY - owner // NY) % NZ * NY + (mine % NY - owner % NY) % NY
    ids = (piece * rows + row_slot).T.reshape(GROUPS, PER, 2, HALF)
    early = (me <= jnp.arange(GROUPS, dtype=jnp.int32))[:, None, None]
    send_ids = jnp.where(early, ids[:, :, 0], ids[:, :, 1]).reshape(-1)
    local_ids = jnp.where(early, ids[:, :, 1], ids[:, :, 0]).reshape(-1)

    sent = gather_rows(send_ids, table, late_slots, late, "gather_sent")
    other = lax.all_to_all(
        sent.reshape(GROUPS, PER * HALF, 2, 128), "field", split_axis=0, concat_axis=0, tiled=True
    )
    local = gather_rows(local_ids, table, late_slots, late, "gather_local")
    local, w_pairs = lax.optimization_barrier((local, w_first))

    col = jnp.arange(F * F, dtype=jnp.int32)
    b, a, i, j = col // 128, col // 16 % 8, col // 4 % 4, col % 4
    forward = (a * PER + i) * F + b * PER + j
    backward = (b * PER + j) * F + a * PER + i
    rows_of = jnp.where(me < GROUPS // 2, forward, backward)
    first_order = (rows_of[:, None] == col[None, :]).astype(jnp.bfloat16)
    first = jnp.dot(
        first_order, w_pairs.reshape(F * F, H), preferred_element_type=jnp.float32
    ).astype(jnp.bfloat16)
    local, first = lax.optimization_barrier((local, first))
    dots = pair_products(
        me.reshape(1),
        local.reshape(GROUPS, PER, 2 * HALF, 128),
        other.reshape(GROUPS, PER, 2 * HALF, 128),
    )
    block = samples // GROUPS
    own_dots = lax.all_to_all(
        dots.reshape(GROUPS, block, 128), "field", split_axis=0, concat_axis=0, tiled=True
    )
    logits = network(order, own_dots, first, w_out.reshape(1, H), parts)[:, 0]
    everyone = lax.all_to_all(
        jnp.broadcast_to(logits[None], (GROUPS, block)),
        "field",
        split_axis=0,
        concat_axis=0,
        tiled=True,
    )
    return everyone.reshape(samples)


def solution(mesh):
    placed = (
        P("row", None, None),
        P("row", None),
        P("row", "field"),
        P(),
        P(None, "field", None),
        P(),
    )
    return jax.shard_map(body, mesh=mesh, in_specs=placed, out_specs=P("row"), check_vma=False)
```

```python
import functools

import jax
import jax.numpy as jnp
from jax import lax
from jax.experimental import pallas as pl
from jax.experimental.pallas import tpu as pltpu
from jax.sharding import PartitionSpec as P

F = 32
K = 64
H = 2048
NZ = 8
NY = 4
GROUPS = 8
PER = 4
HALF = 128
LAG = 2
CHUNK = 128

DIRECTIONS = ((1, 0), (-1, 0), (0, 1), (0, -1))
SPREAD = (
    ((0, (0, 0), (1, 0)), (1, (0, 0), (7, 0)), (2, (0, 0), (0, 1)), (3, (0, 0), (0, 3))),
    ((0, (1, 0), (2, 0)), (1, (0, 1), (7, 1)), (2, (1, 0), (1, 1)), (3, (1, 0), (1, 3))),
    ((0, (2, 0), (3, 0)), (1, (7, 0), (6, 0)), (2, (0, 1), (0, 2)), (3, (7, 0), (7, 3))),
    ((0, (1, 3), (2, 3)), (1, (7, 1), (6, 1)), (2, (7, 1), (7, 2)), (3, (1, 3), (1, 2))),
    ((0, (3, 0), (4, 0)), (1, (6, 0), (5, 0)), (2, (3, 0), (3, 1)), (3, (6, 0), (6, 3))),
    ((0, (2, 3), (3, 3)), (1, (6, 1), (5, 1)), (2, (6, 1), (6, 2)), (3, (2, 3), (2, 2))),
    ((0, (3, 1), (4, 1)), (1, (3, 1), (2, 1)), (2, (3, 1), (3, 2)), (3, (4, 0), (4, 3))),
    ((0, (3, 2), (4, 2)), (2, (5, 1), (5, 2)), (3, (5, 0), (5, 3))),
)


def step_pairs(direction):
    dz, dy = direction
    return [
        (z * NY + y, ((z + dz) % NZ) * NY + (y + dy) % NY) for z in range(NZ) for y in range(NY)
    ]


def place_kernel(slots, rows, *refs):
    pieces, table, sems = refs[: len(slots)], refs[-2], refs[-1]
    copies = [
        pltpu.make_async_copy(piece, table.at[pl.ds(slot * rows, rows)], sems.at[n])
        for n, (slot, piece) in enumerate(zip(slots, pieces))
    ]
    for copy in copies:
        copy.start()
    for copy in copies:
        copy.wait()


def place_pieces(table, slots, pieces):
    rows = pieces[0].shape[0]
    shape = (NZ * NY * rows,) + pieces[0].shape[1:]
    held = [] if table is None else [table]
    count = len(pieces)
    return pl.pallas_call(
        functools.partial(place_kernel, slots, rows),
        out_shape=pltpu.HBM(shape, pieces[0].dtype),
        in_specs=[pl.BlockSpec(memory_space=pltpu.VMEM)] * count
        + [pl.BlockSpec(memory_space=pltpu.HBM)] * len(held),
        out_specs=pl.BlockSpec(memory_space=pltpu.HBM),
        scratch_shapes=[pltpu.SemaphoreType.DMA((count,))],
        input_output_aliases={count: 0} if held else {},
        compiler_params=pltpu.CompilerParams(vmem_limit_bytes=8 << 20),
        cost_estimate=pl.CostEstimate(
            flops=0, bytes_accessed=2 * count * rows * 512, transcendentals=0
        ),
        name="place",
    )(*pieces, *held)


def slot_of(name):
    return name[0] * NY + name[1]


def spread_shard(own):
    pieces = {(0, 0): own}
    table = place_pieces(None, [0], [own])
    waiting = []
    for step in SPREAD:
        sources = sorted({source for _, source, _ in step})
        kept = lax.optimization_barrier(([pieces[source] for source in sources], table))
        ready, table = dict(zip(sources, kept[0])), kept[1]
        for way, source, target in step:
            pieces[target] = lax.ppermute(ready[source], "row", step_pairs(DIRECTIONS[way]))
        waiting.append([target for _, _, target in step])
        if len(waiting) >= LAG and step is not SPREAD[-1]:
            names = waiting.pop(0)
            table = place_pieces(table, [slot_of(n) for n in names], [pieces[n] for n in names])
    late = waiting[0] + waiting[1]
    return table, [slot_of(n) for n in late], [pieces[n] for n in late]


def gather_kernel(count, parts, late_slots, hand_on, index, table_hbm, *refs):
    number = len(late_slots) if hand_on else 1
    late, outs, (found, table, load_sems, sems, late_sems) = refs[:number], refs[number:-5], refs[-5:]
    out = outs[0]
    rows = table.shape[0] // (NZ * NY)
    loads = []
    for slot in range(NZ * NY):
        span = pl.ds(slot * rows, rows)
        source = table_hbm.at[span]
        if slot in late_slots:
            n = late_slots.index(slot)
            source = late[n] if hand_on else late[0].at[n]
        loads.append(pltpu.make_async_copy(source, table.at[span], load_sems.at[slot]))
    for copy in loads:
        copy.start()
    for copy in loads:
        copy.wait()
    leaving = []
    if hand_on:
        for n, slot in enumerate(late_slots):
            source = table.at[pl.ds(slot * rows, rows)]
            leaving.append(pltpu.make_async_copy(source, outs[1].at[n], late_sems.at[n]))
    for copy in leaving:
        copy.start()
    unroll = 32
    size = count // parts
    for part in range(parts):

        def some(i, carry):
            first = part * size + i * unroll
            for u in range(unroll):
                found[first + u] = table[index[first + u]]
            return carry

        lax.fori_loop(0, size // unroll, some, 0)
        span = pl.ds(part * size, size)
        leaving.append(pltpu.make_async_copy(found.at[span], out.at[span], sems.at[part]))
        leaving[-1].start()
    for copy in leaving:
        copy.wait()


def gather_rows(index, table, late_slots, late, name, hand_on=False):
    count = index.shape[0]
    parts = 8
    rows = table.shape[0] // (NZ * NY)
    shapes = [pltpu.HBM((count, 2, 128), jnp.bfloat16)]
    if hand_on:
        shapes.append(pltpu.HBM((len(late_slots), rows, 2, 128), jnp.bfloat16))
    place = pl.ANY if hand_on else pltpu.HBM
    return pl.pallas_call(
        functools.partial(gather_kernel, count, parts, late_slots, hand_on),
        out_shape=shapes,
        grid_spec=pltpu.PrefetchScalarGridSpec(
            num_scalar_prefetch=1,
            grid=(),
            in_specs=[pl.BlockSpec(memory_space=pltpu.HBM)]
            + [pl.BlockSpec(memory_space=place)] * len(late),
            out_specs=[pl.BlockSpec(memory_space=pltpu.HBM)] * len(shapes),
            scratch_shapes=[
                pltpu.VMEM((count, 2, 128), jnp.bfloat16),
                pltpu.VMEM(table.shape, table.dtype),
                pltpu.SemaphoreType.DMA((NZ * NY,)),
                pltpu.SemaphoreType.DMA((parts,)),
                pltpu.SemaphoreType.DMA((len(late_slots),)),
            ],
        ),
        compiler_params=pltpu.CompilerParams(vmem_limit_bytes=24 << 20),
        cost_estimate=pl.CostEstimate(
            flops=0, bytes_accessed=4 * count * 512, transcendentals=0
        ),
        name=name,
    )(index, pltpu.with_memory_space_constraint(table, pltpu.HBM), *late)


def pair_kernel(
    me_ref, local_hbm, other_hbm, out_ref, local_ref, other_ref, total_ref, sums_ref, sems
):
    me = me_ref[0]
    copies = [
        [
            pltpu.make_async_copy(source.at[a], target.at[a], sems.at[n, a])
            for n, (source, target) in enumerate(((local_hbm, local_ref), (other_hbm, other_ref)))
        ]
        for a in range(GROUPS)
    ]
    for pair in copies:
        for copy in pair:
            copy.start()
    rows = 2 * HALF
    lane = lax.broadcasted_iota(jnp.int32, (CHUNK, 128), 1)
    block = lane // 32
    unit = lane // 16
    inner = lane % 16
    i, j = inner // PER, inner % PER
    depth = lax.broadcasted_iota(jnp.int32, (512, 128), 0)
    column = lax.broadcasted_iota(jnp.int32, (512, 128), 1)
    turn = depth // 128
    second = (depth % 128) // 32
    place = ((second + turn) % PER) * PER + second
    collect = jnp.where(column % 16 == place, 1.0, 0.0).astype(jnp.bfloat16)
    odd = block % 2 == 1
    upper = block >= 2
    outer = (block == 0) | (block == 3)

    def turned(tiles):
        even_low = jnp.where(odd, tiles[1], tiles[0])
        even_high = jnp.where(odd, tiles[3], tiles[2])
        odd_low = jnp.where(odd, tiles[0], tiles[1])
        odd_high = jnp.where(odd, tiles[2], tiles[3])
        return (
            jnp.where(upper, even_high, even_low),
            jnp.where(outer, odd_low, odd_high),
            jnp.where(upper, even_low, even_high),
            jnp.where(outer, odd_high, odd_low),
        )

    def products(first, second):
        high, low = [], []
        lefts, rights = turned(first), turned(second)
        for d in range(PER):
            right = rights[-d % PER]
            if d:
                right = pltpu.roll(right, 128 - 32 * d, 1)
            value = lefts[d] * right
            rounded = value.astype(jnp.bfloat16)
            high.append(rounded)
            low.append((value - rounded.astype(jnp.float32)).astype(jnp.bfloat16))
        high = jnp.concatenate(high, axis=1)
        low = jnp.concatenate(low, axis=1)
        return jnp.dot(high, collect, preferred_element_type=jnp.float32) + jnp.dot(
            low, collect, preferred_element_type=jnp.float32
        )

    def tiles(ref, a, span):
        return [ref[a, n, span, :].astype(jnp.float32) for n in range(PER)]

    for a in range(GROUPS):
        for copy in copies[a]:
            copy.wait()

        for r in range(rows // CHUNK):
            span = pl.ds(r * CHUNK, CHUNK)
            dots = products(tiles(local_ref, a, span), tiles(other_ref, a, span))
            total_ref[span, :] = jnp.where(unit == a, dots, total_ref[span, :])

    for r in range(rows // CHUNK):
        span = pl.ds(r * CHUNK, CHUNK)
        own_first = tiles(other_ref, me, span)
        own_second = tiles(local_ref, me, span)
        first_dots = products(own_first, own_first)
        second_dots = products(own_second, own_second)
        total = total_ref[span, :]
        sums_ref[0, span, :] = jnp.where(
            unit < me, total, jnp.where((unit == me) & (i < j), first_dots, 0.0)
        )
        sums_ref[1, span, :] = jnp.where(
            unit > me, total, jnp.where((unit == me) & (i > j), second_dots, 0.0)
        )
    for half in range(2):
        value = sums_ref[half, pl.ds(0, HALF, stride=2), :] + sums_ref[
            half, pl.ds(1, HALF, stride=2), :
        ]
        out_ref[pl.ds(half * HALF, HALF), :] = value.astype(jnp.bfloat16)


def pair_products(me, local, other):
    return pl.pallas_call(
        pair_kernel,
        out_shape=jax.ShapeDtypeStruct((2 * HALF, 128), jnp.bfloat16),
        grid_spec=pltpu.PrefetchScalarGridSpec(
            num_scalar_prefetch=1,
            grid=(),
            in_specs=[
                pl.BlockSpec(memory_space=pltpu.HBM),
                pl.BlockSpec(memory_space=pl.ANY),
            ],
            out_specs=pl.BlockSpec(memory_space=pltpu.VMEM),
            scratch_shapes=[
                pltpu.VMEM((GROUPS, PER, 2 * HALF, 128), jnp.bfloat16),
                pltpu.VMEM((GROUPS, PER, 2 * HALF, 128), jnp.bfloat16),
                pltpu.VMEM((2 * HALF, 128), jnp.float32),
                pltpu.VMEM((2, 2 * HALF, 128), jnp.float32),
                pltpu.SemaphoreType.DMA((2, GROUPS)),
            ],
        ),
        compiler_params=pltpu.CompilerParams(vmem_limit_bytes=16 << 20),
        name="pair_products",
    )(
        me,
        pltpu.with_memory_space_constraint(local, pltpu.HBM),
        other,
    )


def network_kernel(dots_ref, first_hbm, hidden_hbm, out_weights_ref, out_ref, first, hidden, sems):
    layers = hidden.shape[0]
    size = hidden.shape[1] // GROUPS
    first_size = first.shape[0] // GROUPS
    first_copies = [
        pltpu.make_async_copy(
            first_hbm.at[pl.ds(b * first_size, first_size)],
            first.at[pl.ds(b * first_size, first_size)],
            sems.at[layers, b],
        )
        for b in range(GROUPS)
    ]
    hidden_copies = [
        [
            pltpu.make_async_copy(
                hidden_hbm.at[depth, pl.ds(b * size, size)],
                hidden.at[depth, pl.ds(b * size, size)],
                sems.at[depth, b],
            )
            for b in range(GROUPS)
        ]
        for depth in range(layers)
    ]
    for copies in [first_copies] + hidden_copies:
        for copy in copies:
            copy.start()

    def rounded(value):
        return jnp.maximum(value, 0.0).astype(jnp.bfloat16)

    samples = dots_ref.shape[1]
    value = jnp.zeros((samples, H), jnp.float32)
    for b in range(GROUPS):
        first_copies[b].wait()
        value = value + jnp.dot(
            dots_ref[b],
            first[pl.ds(b * first_size, first_size), :],
            preferred_element_type=jnp.float32,
        )
    units = rounded(value)
    for depth in range(layers):
        value = jnp.zeros((samples, H), jnp.float32)
        for b in range(GROUPS):
            hidden_copies[depth][b].wait()
            value = value + jnp.dot(
                units[:, b * size : (b + 1) * size],
                hidden[depth, pl.ds(b * size, size), :],
                preferred_element_type=jnp.float32,
            )
        units = rounded(value)
    product = units.astype(jnp.float32) * out_weights_ref[...].astype(jnp.float32)
    total = jnp.sum(product, axis=1, keepdims=True)
    out_ref[...] = jnp.broadcast_to(total, out_ref.shape)


def network(dots, first, hidden, out_weights):
    return pl.pallas_call(
        network_kernel,
        out_shape=jax.ShapeDtypeStruct((dots.shape[1], 128), jnp.float32),
        in_specs=[
            pl.BlockSpec(memory_space=pltpu.VMEM),
            pl.BlockSpec(memory_space=pltpu.HBM),
            pl.BlockSpec(memory_space=pltpu.HBM),
            pl.BlockSpec(memory_space=pltpu.VMEM),
        ],
        out_specs=pl.BlockSpec(memory_space=pltpu.VMEM),
        scratch_shapes=[
            pltpu.VMEM(first.shape, first.dtype),
            pltpu.VMEM(hidden.shape, hidden.dtype),
            pltpu.SemaphoreType.DMA((hidden.shape[0] + 1, GROUPS)),
        ],
        compiler_params=pltpu.CompilerParams(vmem_limit_bytes=26 << 20),
        name="network",
    )(
        dots,
        pltpu.with_memory_space_constraint(first, pltpu.HBM),
        pltpu.with_memory_space_constraint(hidden, pltpu.HBM),
        out_weights,
    )


def body(row_owner, row_slot, feature_table, w_first, w_hidden, w_out):
    samples = row_slot.shape[0]
    rows = feature_table.shape[0]
    me = lax.axis_index("field")
    mine = lax.axis_index("row")

    source = jnp.arange(2 * 128, dtype=jnp.int32)
    wanted = (source % 128) // 32 * K + source // 128 * 32 + source % 32
    reorder = (source[:, None] == wanted[None, :]).astype(jnp.bfloat16)
    packed = jnp.dot(feature_table, reorder, preferred_element_type=jnp.float32)
    packed = packed.astype(jnp.bfloat16).reshape(rows, 2, 128)
    table, late_slots, late = spread_shard(packed)

    full_hidden = lax.all_gather(w_hidden, "field", axis=1, tiled=True)

    owner = row_owner[:, :, 0]
    piece = (mine // NY - owner // NY) % NZ * NY + (mine % NY - owner % NY) % NY
    ids = (piece * rows + row_slot).T.reshape(GROUPS, PER, 2, HALF)
    early = (me <= jnp.arange(GROUPS, dtype=jnp.int32))[:, None, None]
    send_ids = jnp.where(early, ids[:, :, 0], ids[:, :, 1]).reshape(-1)
    local_ids = jnp.where(early, ids[:, :, 1], ids[:, :, 0]).reshape(-1)

    table, full_hidden = lax.optimization_barrier((table, full_hidden))

    sent, late = gather_rows(send_ids, table, late_slots, late, "gather_sent", hand_on=True)
    other = lax.all_to_all(
        sent.reshape(GROUPS, PER * HALF, 2, 128), "field", split_axis=0, concat_axis=0, tiled=True
    )
    (local,) = gather_rows(
        local_ids,
        table,
        late_slots,
        [pltpu.with_memory_space_constraint(late, pltpu.HBM)],
        "gather_local",
    )
    local, w_pairs = lax.optimization_barrier((local, w_first))

    col = jnp.arange(F * F, dtype=jnp.int32)
    b, a, i, j = col // 128, col // 16 % 8, col // 4 % 4, col % 4
    forward = (a * PER + i) * F + b * PER + j
    backward = (b * PER + j) * F + a * PER + i
    rows_of = jnp.where(me < GROUPS // 2, forward, backward)
    first_order = (rows_of[:, None] == col[None, :]).astype(jnp.bfloat16)
    first = jnp.dot(
        first_order, w_pairs.reshape(F * F, H), preferred_element_type=jnp.float32
    ).astype(jnp.bfloat16)
    local, first = lax.optimization_barrier((local, first))
    dots = pair_products(
        me.reshape(1),
        local.reshape(GROUPS, PER, 2 * HALF, 128),
        other.reshape(GROUPS, PER, 2 * HALF, 128),
    )
    block = samples // GROUPS
    own_dots = lax.all_to_all(
        dots.reshape(GROUPS, block, 128), "field", split_axis=0, concat_axis=0, tiled=True
    )
    logits = network(own_dots, first, full_hidden, w_out.reshape(1, H))[:, 0]
    everyone = lax.all_to_all(
        jnp.broadcast_to(logits[None], (GROUPS, block)),
        "field",
        split_axis=0,
        concat_axis=0,
        tiled=True,
    )
    return everyone.reshape(samples)


def solution(mesh):
    placed = (
        P("row", None, None),
        P("row", None),
        P("row", "field"),
        P(),
        P(None, "field", None),
        P(),
    )
    return jax.shard_map(body, mesh=mesh, in_specs=placed, out_specs=P("row"), check_vma=False)
```

```python
import functools

import jax
import jax.numpy as jnp
from jax import lax
from jax.experimental import pallas as pl
from jax.experimental.pallas import tpu as pltpu
from jax.sharding import PartitionSpec as P

F = 32
K = 64
H = 2048
NZ = 8
NY = 4
GROUPS = 8
PER = 4
HALF = 128
LAG = 2
CHUNK = 128

DIRECTIONS = ((1, 0), (-1, 0), (0, 1), (0, -1))
SPREAD = (
    ((0, (0, 0), (1, 0)), (1, (0, 0), (7, 0)), (2, (0, 0), (0, 1)), (3, (0, 0), (0, 3))),
    ((0, (1, 0), (2, 0)), (1, (0, 1), (7, 1)), (2, (1, 0), (1, 1)), (3, (1, 0), (1, 3))),
    ((0, (2, 0), (3, 0)), (1, (7, 0), (6, 0)), (2, (0, 1), (0, 2)), (3, (7, 0), (7, 3))),
    ((0, (1, 3), (2, 3)), (1, (7, 1), (6, 1)), (2, (7, 1), (7, 2)), (3, (1, 3), (1, 2))),
    ((0, (3, 0), (4, 0)), (1, (6, 0), (5, 0)), (2, (3, 0), (3, 1)), (3, (6, 0), (6, 3))),
    ((0, (2, 3), (3, 3)), (1, (6, 1), (5, 1)), (2, (6, 1), (6, 2)), (3, (2, 3), (2, 2))),
    ((0, (3, 1), (4, 1)), (1, (3, 1), (2, 1)), (2, (3, 1), (3, 2)), (3, (4, 0), (4, 3))),
    ((0, (3, 2), (4, 2)), (2, (5, 1), (5, 2)), (3, (5, 0), (5, 3))),
)


def step_pairs(direction):
    dz, dy = direction
    return [
        (z * NY + y, ((z + dz) % NZ) * NY + (y + dy) % NY) for z in range(NZ) for y in range(NY)
    ]


def place_kernel(slots, rows, *refs):
    pieces, table, sems = refs[: len(slots)], refs[-2], refs[-1]
    copies = [
        pltpu.make_async_copy(piece, table.at[pl.ds(slot * rows, rows)], sems.at[n])
        for n, (slot, piece) in enumerate(zip(slots, pieces))
    ]
    for copy in copies:
        copy.start()
    for copy in copies:
        copy.wait()


def place_pieces(table, slots, pieces):
    rows = pieces[0].shape[0]
    shape = (NZ * NY * rows,) + pieces[0].shape[1:]
    held = [] if table is None else [table]
    count = len(pieces)
    return pl.pallas_call(
        functools.partial(place_kernel, slots, rows),
        out_shape=pltpu.HBM(shape, pieces[0].dtype),
        in_specs=[pl.BlockSpec(memory_space=pltpu.VMEM)] * count
        + [pl.BlockSpec(memory_space=pltpu.HBM)] * len(held),
        out_specs=pl.BlockSpec(memory_space=pltpu.HBM),
        scratch_shapes=[pltpu.SemaphoreType.DMA((count,))],
        input_output_aliases={count: 0} if held else {},
        compiler_params=pltpu.CompilerParams(vmem_limit_bytes=8 << 20),
        cost_estimate=pl.CostEstimate(
            flops=0, bytes_accessed=2 * count * rows * 512, transcendentals=0
        ),
        name="place",
    )(*pieces, *held)


def slot_of(name):
    return name[0] * NY + name[1]


def spread_shard(own):
    pieces = {(0, 0): own}
    table = place_pieces(None, [0], [own])
    waiting = []
    for step in SPREAD:
        sources = sorted({source for _, source, _ in step})
        kept = lax.optimization_barrier(([pieces[source] for source in sources], table))
        ready, table = dict(zip(sources, kept[0])), kept[1]
        for way, source, target in step:
            pieces[target] = lax.ppermute(ready[source], "row", step_pairs(DIRECTIONS[way]))
        waiting.append([target for _, _, target in step])
        if len(waiting) >= LAG and step is not SPREAD[-1]:
            names = waiting.pop(0)
            table = place_pieces(table, [slot_of(n) for n in names], [pieces[n] for n in names])
    late = waiting[0] + waiting[1]
    return table, [slot_of(n) for n in late], [pieces[n] for n in late]


def gather_kernel(count, parts, copies, hand_on, index, *refs):
    outs = 2 if hand_on else 1
    found, table, load_sems, sems, on_sem = refs[-5:]
    out = refs[-5 - outs]

    loads = [
        pltpu.make_async_copy(
            refs[operand].at[pl.ds(start, rows)], table.at[pl.ds(to, rows)], load_sems.at[n]
        )
        for n, (operand, start, rows, to) in enumerate(copies)
    ]
    for copy in loads:
        copy.start()
    for copy in loads:
        copy.wait()
    leaving = []
    if hand_on:
        leaving.append(pltpu.make_async_copy(table.at[pl.ds(0, hand_on)], refs[-6], on_sem))
        leaving[0].start()
    unroll = 32
    size = count // parts
    for part in range(parts):

        def some(i, carry):
            first = part * size + i * unroll
            for u in range(unroll):
                found[first + u] = table[index[first + u]]
            return carry

        lax.fori_loop(0, size // unroll, some, 0)
        span = pl.ds(part * size, size)
        leaving.append(pltpu.make_async_copy(found.at[span], out.at[span], sems.at[part]))
        leaving[-1].start()
    for copy in leaving:
        copy.wait()


def gather_rows(index, operands, spaces, copies, name, hand_on=0):
    count = index.shape[0]
    parts = 8
    total = max(to + rows for _, _, rows, to in copies)
    shapes = [pltpu.HBM((count, 2, 128), jnp.bfloat16)]
    if hand_on:
        shapes.append(pltpu.HBM((hand_on, 2, 128), jnp.bfloat16))
    return pl.pallas_call(
        functools.partial(gather_kernel, count, parts, copies, hand_on),
        out_shape=shapes,
        grid_spec=pltpu.PrefetchScalarGridSpec(
            num_scalar_prefetch=1,
            grid=(),
            in_specs=[pl.BlockSpec(memory_space=space) for space in spaces],
            out_specs=[pl.BlockSpec(memory_space=pltpu.HBM)] * len(shapes),
            scratch_shapes=[
                pltpu.VMEM((count, 2, 128), jnp.bfloat16),
                pltpu.VMEM((total, 2, 128), jnp.bfloat16),
                pltpu.SemaphoreType.DMA((len(copies),)),
                pltpu.SemaphoreType.DMA((parts,)),
                pltpu.SemaphoreType.DMA,
            ],
        ),
        compiler_params=pltpu.CompilerParams(vmem_limit_bytes=24 << 20),
        cost_estimate=pl.CostEstimate(
            flops=0, bytes_accessed=2 * (total + count) * 512, transcendentals=0
        ),
        name=name,
    )(
        index,
        *[
            pltpu.with_memory_space_constraint(operand, pltpu.HBM) if space == pltpu.HBM else operand
            for operand, space in zip(operands, spaces)
        ],
    )


def pair_kernel(
    me_ref, local_hbm, other_hbm, out_ref, local_ref, other_ref, total_ref, sums_ref, sems
):
    me = me_ref[0]
    copies = [
        [
            pltpu.make_async_copy(source.at[a], target.at[a], sems.at[n, a])
            for n, (source, target) in enumerate(((local_hbm, local_ref), (other_hbm, other_ref)))
        ]
        for a in range(GROUPS)
    ]
    for pair in copies:
        for copy in pair:
            copy.start()
    rows = 2 * HALF
    lane = lax.broadcasted_iota(jnp.int32, (CHUNK, 128), 1)
    block = lane // 32
    unit = lane // 16
    inner = lane % 16
    i, j = inner // PER, inner % PER
    depth = lax.broadcasted_iota(jnp.int32, (512, 128), 0)
    column = lax.broadcasted_iota(jnp.int32, (512, 128), 1)
    turn = depth // 128
    second = (depth % 128) // 32
    place = ((second + turn) % PER) * PER + second
    collect = jnp.where(column % 16 == place, 1.0, 0.0).astype(jnp.bfloat16)
    odd = block % 2 == 1
    upper = block >= 2
    outer = (block == 0) | (block == 3)

    def turned(tiles):
        even_low = jnp.where(odd, tiles[1], tiles[0])
        even_high = jnp.where(odd, tiles[3], tiles[2])
        odd_low = jnp.where(odd, tiles[0], tiles[1])
        odd_high = jnp.where(odd, tiles[2], tiles[3])
        return (
            jnp.where(upper, even_high, even_low),
            jnp.where(outer, odd_low, odd_high),
            jnp.where(upper, even_low, even_high),
            jnp.where(outer, odd_high, odd_low),
        )

    def products(first, second):
        high, low = [], []
        lefts, rights = turned(first), turned(second)
        for d in range(PER):
            right = rights[-d % PER]
            if d:
                right = pltpu.roll(right, 128 - 32 * d, 1)
            value = lefts[d] * right
            rounded = value.astype(jnp.bfloat16)
            high.append(rounded)
            low.append((value - rounded.astype(jnp.float32)).astype(jnp.bfloat16))
        high = jnp.concatenate(high, axis=1)
        low = jnp.concatenate(low, axis=1)
        return jnp.dot(high, collect, preferred_element_type=jnp.float32) + jnp.dot(
            low, collect, preferred_element_type=jnp.float32
        )

    def tiles(ref, a, span):
        return [ref[a, n, span, :].astype(jnp.float32) for n in range(PER)]

    for a in range(GROUPS):
        for copy in copies[a]:
            copy.wait()

        for r in range(rows // CHUNK):
            span = pl.ds(r * CHUNK, CHUNK)
            dots = products(tiles(local_ref, a, span), tiles(other_ref, a, span))
            total_ref[span, :] = jnp.where(unit == a, dots, total_ref[span, :])

    for r in range(rows // CHUNK):
        span = pl.ds(r * CHUNK, CHUNK)
        own_first = tiles(other_ref, me, span)
        own_second = tiles(local_ref, me, span)
        first_dots = products(own_first, own_first)
        second_dots = products(own_second, own_second)
        total = total_ref[span, :]
        sums_ref[0, span, :] = jnp.where(
            unit < me, total, jnp.where((unit == me) & (i < j), first_dots, 0.0)
        )
        sums_ref[1, span, :] = jnp.where(
            unit > me, total, jnp.where((unit == me) & (i > j), second_dots, 0.0)
        )
    for half in range(2):
        value = sums_ref[half, pl.ds(0, HALF, stride=2), :] + sums_ref[
            half, pl.ds(1, HALF, stride=2), :
        ]
        out_ref[pl.ds(half * HALF, HALF), :] = value.astype(jnp.bfloat16)


def pair_products(me, local, other):
    return pl.pallas_call(
        pair_kernel,
        out_shape=jax.ShapeDtypeStruct((2 * HALF, 128), jnp.bfloat16),
        grid_spec=pltpu.PrefetchScalarGridSpec(
            num_scalar_prefetch=1,
            grid=(),
            in_specs=[
                pl.BlockSpec(memory_space=pltpu.HBM),
                pl.BlockSpec(memory_space=pl.ANY),
            ],
            out_specs=pl.BlockSpec(memory_space=pltpu.VMEM),
            scratch_shapes=[
                pltpu.VMEM((GROUPS, PER, 2 * HALF, 128), jnp.bfloat16),
                pltpu.VMEM((GROUPS, PER, 2 * HALF, 128), jnp.bfloat16),
                pltpu.VMEM((2 * HALF, 128), jnp.float32),
                pltpu.VMEM((2, 2 * HALF, 128), jnp.float32),
                pltpu.SemaphoreType.DMA((2, GROUPS)),
            ],
        ),
        compiler_params=pltpu.CompilerParams(vmem_limit_bytes=16 << 20),
        name="pair_products",
    )(
        me,
        pltpu.with_memory_space_constraint(local, pltpu.HBM),
        other,
    )


def network_kernel(dots_ref, first_hbm, hidden_hbm, out_weights_ref, out_ref, first, hidden, sems):
    layers = hidden.shape[0]
    size = hidden.shape[1] // GROUPS
    first_size = first.shape[0] // GROUPS
    first_copies = [
        pltpu.make_async_copy(
            first_hbm.at[pl.ds(b * first_size, first_size)],
            first.at[pl.ds(b * first_size, first_size)],
            sems.at[layers, b],
        )
        for b in range(GROUPS)
    ]
    hidden_copies = [
        [
            pltpu.make_async_copy(
                hidden_hbm.at[depth, pl.ds(b * size, size)],
                hidden.at[depth, pl.ds(b * size, size)],
                sems.at[depth, b],
            )
            for b in range(GROUPS)
        ]
        for depth in range(layers)
    ]
    for copies in [first_copies] + hidden_copies:
        for copy in copies:
            copy.start()

    def rounded(value):
        return jnp.maximum(value, 0.0).astype(jnp.bfloat16)

    samples = dots_ref.shape[1]
    value = jnp.zeros((samples, H), jnp.float32)
    for b in range(GROUPS):
        first_copies[b].wait()
        value = value + jnp.dot(
            dots_ref[b],
            first[pl.ds(b * first_size, first_size), :],
            preferred_element_type=jnp.float32,
        )
    units = rounded(value)
    for depth in range(layers):
        value = jnp.zeros((samples, H), jnp.float32)
        for b in range(GROUPS):
            hidden_copies[depth][b].wait()
            value = value + jnp.dot(
                units[:, b * size : (b + 1) * size],
                hidden[depth, pl.ds(b * size, size), :],
                preferred_element_type=jnp.float32,
            )
        units = rounded(value)
    product = units.astype(jnp.float32) * out_weights_ref[...].astype(jnp.float32)
    total = jnp.sum(product, axis=1, keepdims=True)
    lane = lax.broadcasted_iota(jnp.int32, (samples, 128), 1)
    sample = lax.broadcasted_iota(jnp.int32, (samples, 128), 0)
    logits = jnp.sum(jnp.where(lane == sample, total, 0.0), axis=0, keepdims=True)
    out_ref[...] = jnp.broadcast_to(logits, out_ref.shape)


def network(dots, first, hidden, out_weights):
    return pl.pallas_call(
        network_kernel,
        out_shape=jax.ShapeDtypeStruct((GROUPS, 128), jnp.float32),
        in_specs=[
            pl.BlockSpec(memory_space=pltpu.VMEM),
            pl.BlockSpec(memory_space=pltpu.HBM),
            pl.BlockSpec(memory_space=pltpu.HBM),
            pl.BlockSpec(memory_space=pltpu.VMEM),
        ],
        out_specs=pl.BlockSpec(memory_space=pltpu.VMEM),
        scratch_shapes=[
            pltpu.VMEM(first.shape, first.dtype),
            pltpu.VMEM(hidden.shape, hidden.dtype),
            pltpu.SemaphoreType.DMA((hidden.shape[0] + 1, GROUPS)),
        ],
        compiler_params=pltpu.CompilerParams(vmem_limit_bytes=26 << 20),
        name="network",
    )(
        dots,
        pltpu.with_memory_space_constraint(first, pltpu.HBM),
        pltpu.with_memory_space_constraint(hidden, pltpu.HBM),
        out_weights,
    )


def body(row_owner, row_slot, feature_table, w_first, w_hidden, w_out):
    samples = row_slot.shape[0]
    rows = feature_table.shape[0]
    me = lax.axis_index("field")
    mine = lax.axis_index("row")

    source = jnp.arange(2 * 128, dtype=jnp.int32)
    wanted = (source % 128) // 32 * K + source // 128 * 32 + source % 32
    reorder = (source[:, None] == wanted[None, :]).astype(jnp.bfloat16)
    packed = jnp.dot(feature_table, reorder, preferred_element_type=jnp.float32)
    packed = packed.astype(jnp.bfloat16).reshape(rows, 2, 128)
    table, late_slots, late = spread_shard(packed)

    full_hidden = lax.all_gather(w_hidden, "field", axis=1, tiled=True)

    owner = row_owner[:, :, 0]
    piece = (mine // NY - owner // NY) % NZ * NY + (mine % NY - owner % NY) % NY
    late_rows = len(late) * rows
    place = jnp.full_like(piece, -1)
    for n, slot in enumerate(late_slots):
        place = jnp.where(piece == slot, n, place)

    early = (me <= jnp.arange(GROUPS, dtype=jnp.int32))[:, None, None]

    def in_order(values, sent):
        halves = values.T.reshape(GROUPS, PER, 2, HALF)
        one, two = (halves[:, :, 0], halves[:, :, 1]) if sent else (halves[:, :, 1], halves[:, :, 0])
        return jnp.where(early, one, two).reshape(-1)

    ids = piece * rows + row_slot
    early_ids = in_order(jnp.where(place < 0, ids, 0), True)
    late_ids = in_order(jnp.where(place < 0, -1, place * rows + row_slot), True)
    number = late_ids.shape[0]
    late_ids = jnp.where(
        late_ids < 0, late_rows + jnp.arange(number, dtype=jnp.int32), late_ids
    )
    local_ids = in_order(ids, False)

    table, full_hidden = lax.optimization_barrier((table, full_hidden))

    early_slots = [slot for slot in range(NZ * NY) if slot not in late_slots]
    (partly,) = gather_rows(
        early_ids,
        [table],
        [pltpu.HBM],
        [(0, slot * rows, rows, slot * rows) for slot in early_slots],
        "gather_early",
    )
    quarter = number // 4
    sent, late_table = gather_rows(
        late_ids,
        list(late) + [partly],
        [pl.ANY] * len(late) + [pltpu.HBM],
        [(n, 0, rows, n * rows) for n in range(len(late))]
        + [
            (len(late), n * quarter, quarter, late_rows + n * quarter) for n in range(4)
        ],
        "gather_sent",
        hand_on=late_rows,
    )
    other = lax.all_to_all(
        sent.reshape(GROUPS, PER * HALF, 2, 128), "field", split_axis=0, concat_axis=0, tiled=True
    )
    (local,) = gather_rows(
        local_ids,
        [table, late_table],
        [pltpu.HBM] * 2,
        [(0, slot * rows, rows, slot * rows) for slot in early_slots]
        + [(1, n * rows, rows, slot * rows) for n, slot in enumerate(late_slots)],
        "gather_local",
    )
    local, w_pairs = lax.optimization_barrier((local, w_first))

    col = jnp.arange(F * F, dtype=jnp.int32)
    b, a, i, j = col // 128, col // 16 % 8, col // 4 % 4, col % 4
    forward = (a * PER + i) * F + b * PER + j
    backward = (b * PER + j) * F + a * PER + i
    rows_of = jnp.where(me < GROUPS // 2, forward, backward)
    first_order = (rows_of[:, None] == col[None, :]).astype(jnp.bfloat16)
    first = jnp.dot(
        first_order, w_pairs.reshape(F * F, H), preferred_element_type=jnp.float32
    ).astype(jnp.bfloat16)
    local, first = lax.optimization_barrier((local, first))
    dots = pair_products(
        me.reshape(1),
        local.reshape(GROUPS, PER, 2 * HALF, 128),
        other.reshape(GROUPS, PER, 2 * HALF, 128),
    )
    block = samples // GROUPS
    own_dots = lax.all_to_all(
        dots.reshape(GROUPS, block, 128), "field", split_axis=0, concat_axis=0, tiled=True
    )
    logits = network(own_dots, first, full_hidden, w_out.reshape(1, H))
    everyone = lax.all_to_all(logits, "field", split_axis=0, concat_axis=0, tiled=True)
    return everyone[:, :block].reshape(samples)


def solution(mesh):
    placed = (
        P("row", None, None),
        P("row", None),
        P("row", "field"),
        P(),
        P(None, "field", None),
        P(),
    )
    return jax.shard_map(body, mesh=mesh, in_specs=placed, out_specs=P("row"), check_vma=False)
```

```python
import functools

import jax
import jax.numpy as jnp
from jax import lax
from jax.experimental import pallas as pl
from jax.experimental.pallas import tpu as pltpu
from jax.sharding import PartitionSpec as P

F = 32
K = 64
H = 2048
NZ = 8
NY = 4
NX = 4
GROUPS = 8
PER = 4
HALF = 128
LAG = 2
CHUNK = 128

DIRECTIONS = ((1, 0), (-1, 0), (0, 1), (0, -1))
SPREAD = (
    ((0, (0, 0), (1, 0)), (1, (0, 0), (7, 0)), (2, (0, 0), (0, 1)), (3, (0, 0), (0, 3))),
    ((0, (1, 0), (2, 0)), (1, (0, 1), (7, 1)), (2, (1, 0), (1, 1)), (3, (1, 0), (1, 3))),
    ((0, (2, 0), (3, 0)), (1, (7, 0), (6, 0)), (2, (0, 1), (0, 2)), (3, (7, 0), (7, 3))),
    ((0, (1, 3), (2, 3)), (1, (7, 1), (6, 1)), (2, (7, 1), (7, 2)), (3, (1, 3), (1, 2))),
    ((0, (3, 0), (4, 0)), (1, (6, 0), (5, 0)), (2, (3, 0), (3, 1)), (3, (6, 0), (6, 3))),
    ((0, (2, 3), (3, 3)), (1, (6, 1), (5, 1)), (2, (6, 1), (6, 2)), (3, (2, 3), (2, 2))),
    ((0, (3, 1), (4, 1)), (1, (3, 1), (2, 1)), (2, (3, 1), (3, 2)), (3, (4, 0), (4, 3))),
    ((0, (3, 2), (4, 2)), (2, (5, 1), (5, 2)), (3, (5, 0), (5, 3))),
)


def step_pairs(direction):
    dz, dy = direction
    return [
        (z * NY + y, ((z + dz) % NZ) * NY + (y + dy) % NY) for z in range(NZ) for y in range(NY)
    ]


def place_kernel(slots, rows, *refs):
    pieces, table, sems = refs[: len(slots)], refs[-2], refs[-1]
    copies = [
        pltpu.make_async_copy(piece, table.at[pl.ds(slot * rows, rows)], sems.at[n])
        for n, (slot, piece) in enumerate(zip(slots, pieces))
    ]
    for copy in copies:
        copy.start()
    for copy in copies:
        copy.wait()


def place_pieces(table, slots, pieces):
    rows = pieces[0].shape[0]
    shape = (NZ * NY * rows,) + pieces[0].shape[1:]
    held = [] if table is None else [table]
    count = len(pieces)
    return pl.pallas_call(
        functools.partial(place_kernel, slots, rows),
        out_shape=pltpu.HBM(shape, pieces[0].dtype),
        in_specs=[pl.BlockSpec(memory_space=pltpu.VMEM)] * count
        + [pl.BlockSpec(memory_space=pltpu.HBM)] * len(held),
        out_specs=pl.BlockSpec(memory_space=pltpu.HBM),
        scratch_shapes=[pltpu.SemaphoreType.DMA((count,))],
        input_output_aliases={count: 0} if held else {},
        compiler_params=pltpu.CompilerParams(vmem_limit_bytes=8 << 20),
        cost_estimate=pl.CostEstimate(
            flops=0, bytes_accessed=2 * count * rows * 512, transcendentals=0
        ),
        name="place",
    )(*pieces, *held)


def slot_of(name):
    return name[0] * NY + name[1]


def spread_shard(own):
    pieces = {(0, 0): own}
    table = place_pieces(None, [0], [own])
    waiting = []
    for step in SPREAD:
        sources = sorted({source for _, source, _ in step})
        kept = lax.optimization_barrier(([pieces[source] for source in sources], table))
        ready, table = dict(zip(sources, kept[0])), kept[1]
        for way, source, target in step:
            pieces[target] = lax.ppermute(ready[source], "row", step_pairs(DIRECTIONS[way]))
        waiting.append([target for _, _, target in step])
        if len(waiting) >= LAG and step is not SPREAD[-1]:
            names = waiting.pop(0)
            table = place_pieces(table, [slot_of(n) for n in names], [pieces[n] for n in names])
    late = waiting[0] + waiting[1]
    return table, [slot_of(n) for n in late], [pieces[n] for n in late]


def gather_kernel(count, parts, copies, hand_on, index, *refs):
    outs = 2 if hand_on else 1
    found, table, load_sems, sems, on_sem = refs[-5:]
    out = refs[-5 - outs]

    loads = [
        pltpu.make_async_copy(
            refs[operand].at[pl.ds(start, rows)], table.at[pl.ds(to, rows)], load_sems.at[n]
        )
        for n, (operand, start, rows, to) in enumerate(copies)
    ]
    for copy in loads:
        copy.start()
    for copy in loads:
        copy.wait()
    leaving = []
    if hand_on:
        leaving.append(pltpu.make_async_copy(table.at[pl.ds(0, hand_on)], refs[-6], on_sem))
        leaving[0].start()
    unroll = 32
    size = count // parts
    for part in range(parts):

        def some(i, carry):
            first = part * size + i * unroll
            for u in range(unroll):
                found[first + u] = table[index[first + u]]
            return carry

        lax.fori_loop(0, size // unroll, some, 0)
        span = pl.ds(part * size, size)
        leaving.append(pltpu.make_async_copy(found.at[span], out.at[span], sems.at[part]))
        leaving[-1].start()
    for copy in leaving:
        copy.wait()


def gather_rows(index, operands, spaces, copies, name, hand_on=0):
    count = index.shape[0]
    parts = 8
    total = max(to + rows for _, _, rows, to in copies)
    shapes = [pltpu.HBM((count, 2, 128), jnp.bfloat16)]
    if hand_on:
        shapes.append(pltpu.HBM((hand_on, 2, 128), jnp.bfloat16))
    return pl.pallas_call(
        functools.partial(gather_kernel, count, parts, copies, hand_on),
        out_shape=shapes,
        grid_spec=pltpu.PrefetchScalarGridSpec(
            num_scalar_prefetch=1,
            grid=(),
            in_specs=[pl.BlockSpec(memory_space=space) for space in spaces],
            out_specs=[pl.BlockSpec(memory_space=pltpu.HBM)] * len(shapes),
            scratch_shapes=[
                pltpu.VMEM((count, 2, 128), jnp.bfloat16),
                pltpu.VMEM((total, 2, 128), jnp.bfloat16),
                pltpu.SemaphoreType.DMA((len(copies),)),
                pltpu.SemaphoreType.DMA((parts,)),
                pltpu.SemaphoreType.DMA,
            ],
        ),
        compiler_params=pltpu.CompilerParams(vmem_limit_bytes=24 << 20),
        cost_estimate=pl.CostEstimate(
            flops=0, bytes_accessed=2 * (total + count) * 512, transcendentals=0
        ),
        name=name,
    )(
        index,
        *[
            pltpu.with_memory_space_constraint(operand, pltpu.HBM) if space == pltpu.HBM else operand
            for operand, space in zip(operands, spaces)
        ],
    )


def pair_kernel(
    me_ref, local_hbm, other_hbm, out_ref, local_ref, other_ref, total_ref, sums_ref, sems
):
    me = me_ref[0]
    copies = [
        [
            pltpu.make_async_copy(source.at[a], target.at[a], sems.at[n, a])
            for n, (source, target) in enumerate(((local_hbm, local_ref), (other_hbm, other_ref)))
        ]
        for a in range(GROUPS)
    ]
    for pair in copies:
        for copy in pair:
            copy.start()
    rows = 2 * HALF
    lane = lax.broadcasted_iota(jnp.int32, (CHUNK, 128), 1)
    block = lane // 32
    unit = lane // 16
    inner = lane % 16
    i, j = inner // PER, inner % PER
    depth = lax.broadcasted_iota(jnp.int32, (512, 128), 0)
    column = lax.broadcasted_iota(jnp.int32, (512, 128), 1)
    turn = depth // 128
    second = (depth % 128) // 32
    place = ((second + turn) % PER) * PER + second
    collect = jnp.where(column % 16 == place, 1.0, 0.0).astype(jnp.bfloat16)
    odd = block % 2 == 1
    upper = block >= 2
    outer = (block == 0) | (block == 3)

    def turned(tiles):
        even_low = jnp.where(odd, tiles[1], tiles[0])
        even_high = jnp.where(odd, tiles[3], tiles[2])
        odd_low = jnp.where(odd, tiles[0], tiles[1])
        odd_high = jnp.where(odd, tiles[2], tiles[3])
        return (
            jnp.where(upper, even_high, even_low),
            jnp.where(outer, odd_low, odd_high),
            jnp.where(upper, even_low, even_high),
            jnp.where(outer, odd_high, odd_low),
        )

    def products(first, second):
        high, low = [], []
        lefts, rights = turned(first), turned(second)
        for d in range(PER):
            right = rights[-d % PER]
            if d:
                right = pltpu.roll(right, 128 - 32 * d, 1)
            value = lefts[d] * right
            rounded = value.astype(jnp.bfloat16)
            high.append(rounded)
            low.append((value - rounded.astype(jnp.float32)).astype(jnp.bfloat16))
        high = jnp.concatenate(high, axis=1)
        low = jnp.concatenate(low, axis=1)
        return jnp.dot(high, collect, preferred_element_type=jnp.float32) + jnp.dot(
            low, collect, preferred_element_type=jnp.float32
        )

    def tiles(ref, a, span):
        return [ref[a, n, span, :].astype(jnp.float32) for n in range(PER)]

    for a in range(GROUPS):
        for copy in copies[a]:
            copy.wait()

        for r in range(rows // CHUNK):
            span = pl.ds(r * CHUNK, CHUNK)
            dots = products(tiles(local_ref, a, span), tiles(other_ref, a, span))
            total_ref[span, :] = jnp.where(unit == a, dots, total_ref[span, :])

    for r in range(rows // CHUNK):
        span = pl.ds(r * CHUNK, CHUNK)
        own_first = tiles(other_ref, me, span)
        own_second = tiles(local_ref, me, span)
        first_dots = products(own_first, own_first)
        second_dots = products(own_second, own_second)
        total = total_ref[span, :]
        sums_ref[0, span, :] = jnp.where(
            unit < me, total, jnp.where((unit == me) & (i < j), first_dots, 0.0)
        )
        sums_ref[1, span, :] = jnp.where(
            unit > me, total, jnp.where((unit == me) & (i > j), second_dots, 0.0)
        )
    for half in range(2):
        value = sums_ref[half, pl.ds(0, HALF, stride=2), :] + sums_ref[
            half, pl.ds(1, HALF, stride=2), :
        ]
        out_ref[pl.ds(half * HALF, HALF), :] = value.astype(jnp.bfloat16)


def pair_products(me, local, other):
    return pl.pallas_call(
        pair_kernel,
        out_shape=jax.ShapeDtypeStruct((2 * HALF, 128), jnp.bfloat16),
        grid_spec=pltpu.PrefetchScalarGridSpec(
            num_scalar_prefetch=1,
            grid=(),
            in_specs=[
                pl.BlockSpec(memory_space=pltpu.HBM),
                pl.BlockSpec(memory_space=pl.ANY),
            ],
            out_specs=pl.BlockSpec(memory_space=pltpu.VMEM),
            scratch_shapes=[
                pltpu.VMEM((GROUPS, PER, 2 * HALF, 128), jnp.bfloat16),
                pltpu.VMEM((GROUPS, PER, 2 * HALF, 128), jnp.bfloat16),
                pltpu.VMEM((2 * HALF, 128), jnp.float32),
                pltpu.VMEM((2, 2 * HALF, 128), jnp.float32),
                pltpu.SemaphoreType.DMA((2, GROUPS)),
            ],
        ),
        compiler_params=pltpu.CompilerParams(vmem_limit_bytes=16 << 20),
        name="pair_products",
    )(
        me,
        pltpu.with_memory_space_constraint(local, pltpu.HBM),
        other,
    )


def network_kernel(order_ref, dots_ref, first_hbm, out_weights_ref, *refs):
    near, twin, out_ref, first, hidden, units, sems = refs
    layers = hidden.shape[0]
    size = first.shape[0] // GROUPS
    first_copies = [
        pltpu.make_async_copy(
            first_hbm.at[pl.ds(b * size, size)], first.at[pl.ds(b * size, size)], sems.at[layers, b]
        )
        for b in range(GROUPS)
    ]
    hidden_copies = []
    for depth in range(layers):
        sources = [part.at[x, depth] for part in (near, twin) for x in range(NX)]
        hidden_copies.append(
            [
                pltpu.make_async_copy(source, hidden.at[depth, n], sems.at[depth, n])
                for n, source in enumerate(sources)
            ]
        )
    for copies in [first_copies] + hidden_copies:
        for copy in copies:
            copy.start()

    def rounded(value):
        return jnp.maximum(value, 0.0).astype(jnp.bfloat16)

    samples = dots_ref.shape[1]
    width = units.shape[2]
    value = jnp.zeros((samples, H), jnp.float32)
    for b in range(GROUPS):
        first_copies[b].wait()
        value = value + jnp.dot(
            dots_ref[b], first[pl.ds(b * size, size), :], preferred_element_type=jnp.float32
        )
    for depth in range(layers):
        state = rounded(value)
        for n in range(GROUPS):
            units[n] = state[:, n * width : (n + 1) * width]
        value = jnp.zeros((samples, H), jnp.float32)
        for n in range(GROUPS):
            hidden_copies[depth][n].wait()
            value = value + jnp.dot(
                units[order_ref[n]], hidden[depth, n], preferred_element_type=jnp.float32
            )
    state = rounded(value)
    product = state.astype(jnp.float32) * out_weights_ref[...].astype(jnp.float32)
    total = jnp.sum(product, axis=1, keepdims=True)
    lane = lax.broadcasted_iota(jnp.int32, (samples, 128), 1)
    sample = lax.broadcasted_iota(jnp.int32, (samples, 128), 0)
    logits = jnp.sum(jnp.where(lane == sample, total, 0.0), axis=0, keepdims=True)
    out_ref[...] = jnp.broadcast_to(logits, out_ref.shape)


def network(order, dots, first, out_weights, near, twin):
    _, layers, width, _ = near.shape
    return pl.pallas_call(
        network_kernel,
        out_shape=jax.ShapeDtypeStruct((GROUPS, 128), jnp.float32),
        grid_spec=pltpu.PrefetchScalarGridSpec(
            num_scalar_prefetch=1,
            grid=(),
            in_specs=[
                pl.BlockSpec(memory_space=pltpu.VMEM),
                pl.BlockSpec(memory_space=pltpu.HBM),
                pl.BlockSpec(memory_space=pltpu.VMEM),
            ]
            + [pl.BlockSpec(memory_space=pltpu.HBM)] * 2,
            out_specs=pl.BlockSpec(memory_space=pltpu.VMEM),
            scratch_shapes=[
                pltpu.VMEM(first.shape, first.dtype),
                pltpu.VMEM((layers, GROUPS, width, H), near.dtype),
                pltpu.VMEM((GROUPS, dots.shape[1], width), jnp.bfloat16),
                pltpu.SemaphoreType.DMA((layers + 1, GROUPS)),
            ],
        ),
        compiler_params=pltpu.CompilerParams(vmem_limit_bytes=26 << 20),
        name="network",
    )(
        order,
        dots,
        pltpu.with_memory_space_constraint(first, pltpu.HBM),
        out_weights,
        pltpu.with_memory_space_constraint(near, pltpu.HBM),
        pltpu.with_memory_space_constraint(twin, pltpu.HBM),
    )


def body(row_owner, row_slot, feature_table, w_first, w_hidden, w_out):
    samples = row_slot.shape[0]
    rows = feature_table.shape[0]
    me = lax.axis_index("field")
    mine = lax.axis_index("row")

    source = jnp.arange(2 * 128, dtype=jnp.int32)
    wanted = (source % 128) // 32 * K + source // 128 * 32 + source % 32
    reorder = (source[:, None] == wanted[None, :]).astype(jnp.bfloat16)
    packed = jnp.dot(feature_table, reorder, preferred_element_type=jnp.float32)
    packed = packed.astype(jnp.bfloat16).reshape(rows, 2, 128)
    table, late_slots, late = spread_shard(packed)

    near = lax.all_to_all(
        jnp.broadcast_to(w_hidden[None], (NX,) + w_hidden.shape),
        "field",
        split_axis=0,
        concat_axis=0,
        axis_index_groups=[[x * 2 + core for x in range(NX)] for core in range(2)],
        tiled=True,
    )
    chips, core = 2 * jnp.arange(NX, dtype=jnp.int32), me % 2
    order = jnp.concatenate([chips + core, chips + 1 - core])

    owner = row_owner[:, :, 0]
    piece = (mine // NY - owner // NY) % NZ * NY + (mine % NY - owner % NY) % NY
    late_rows = len(late) * rows
    place = jnp.full_like(piece, -1)
    for n, slot in enumerate(late_slots):
        place = jnp.where(piece == slot, n, place)

    early = (me <= jnp.arange(GROUPS, dtype=jnp.int32))[:, None, None]

    def in_order(values, sent):
        halves = values.T.reshape(GROUPS, PER, 2, HALF)
        one, two = (halves[:, :, 0], halves[:, :, 1]) if sent else (halves[:, :, 1], halves[:, :, 0])
        return jnp.where(early, one, two).reshape(-1)

    ids = piece * rows + row_slot
    early_ids = in_order(jnp.where(place < 0, ids, 0), True)
    late_ids = in_order(jnp.where(place < 0, -1, place * rows + row_slot), True)
    number = late_ids.shape[0]
    late_ids = jnp.where(
        late_ids < 0, late_rows + jnp.arange(number, dtype=jnp.int32), late_ids
    )
    local_ids = in_order(ids, False)

    early_slots = [slot for slot in range(NZ * NY) if slot not in late_slots]
    (partly,) = gather_rows(
        early_ids,
        [table],
        [pltpu.HBM],
        [(0, slot * rows, rows, slot * rows) for slot in early_slots],
        "gather_early",
    )
    quarter = number // 4
    sent, late_table = gather_rows(
        late_ids,
        list(late) + [partly],
        [pl.ANY] * len(late) + [pltpu.HBM],
        [(n, 0, rows, n * rows) for n in range(len(late))]
        + [
            (len(late), n * quarter, quarter, late_rows + n * quarter) for n in range(4)
        ],
        "gather_sent",
        hand_on=late_rows,
    )
    other = lax.all_to_all(
        sent.reshape(GROUPS, PER * HALF, 2, 128), "field", split_axis=0, concat_axis=0, tiled=True
    )
    near, sent = lax.optimization_barrier((near, sent))
    twin = lax.ppermute(near, "field", [(index, index ^ 1) for index in range(2 * NX)])
    (local,) = gather_rows(
        local_ids,
        [table, late_table],
        [pltpu.HBM] * 2,
        [(0, slot * rows, rows, slot * rows) for slot in early_slots]
        + [(1, n * rows, rows, slot * rows) for n, slot in enumerate(late_slots)],
        "gather_local",
    )
    local, w_pairs = lax.optimization_barrier((local, w_first))

    col = jnp.arange(F * F, dtype=jnp.int32)
    b, a, i, j = col // 128, col // 16 % 8, col // 4 % 4, col % 4
    forward = (a * PER + i) * F + b * PER + j
    backward = (b * PER + j) * F + a * PER + i
    rows_of = jnp.where(me < GROUPS // 2, forward, backward)
    first_order = (rows_of[:, None] == col[None, :]).astype(jnp.bfloat16)
    first = jnp.dot(
        first_order, w_pairs.reshape(F * F, H), preferred_element_type=jnp.float32
    ).astype(jnp.bfloat16)
    local, first = lax.optimization_barrier((local, first))
    dots = pair_products(
        me.reshape(1),
        local.reshape(GROUPS, PER, 2 * HALF, 128),
        other.reshape(GROUPS, PER, 2 * HALF, 128),
    )
    block = samples // GROUPS
    own_dots = lax.all_to_all(
        dots.reshape(GROUPS, block, 128), "field", split_axis=0, concat_axis=0, tiled=True
    )
    logits = network(order, own_dots, first, w_out.reshape(1, H), near, twin)
    everyone = lax.all_to_all(logits, "field", split_axis=0, concat_axis=0, tiled=True)
    return everyone[:, :block].reshape(samples)


def solution(mesh):
    placed = (
        P("row", None, None),
        P("row", None),
        P("row", "field"),
        P(),
        P(None, "field", None),
        P(),
    )
    return jax.shard_map(body, mesh=mesh, in_specs=placed, out_specs=P("row"), check_vma=False)
```

```python
import functools

import jax
import jax.numpy as jnp
from jax import lax
from jax.experimental import pallas as pl
from jax.experimental.pallas import tpu as pltpu
from jax.sharding import PartitionSpec as P

F = 32
K = 64
H = 2048
NZ = 8
NY = 4
GROUPS = 8
PER = 4
HALF = 128
LAG = 2
CHUNK = 128

DIRECTIONS = ((1, 0), (-1, 0), (0, 1), (0, -1))
SPREAD = (
    ((0, (0, 0), (1, 0)), (1, (0, 0), (7, 0)), (2, (0, 0), (0, 1)), (3, (0, 0), (0, 3))),
    ((0, (1, 0), (2, 0)), (1, (0, 1), (7, 1)), (2, (1, 0), (1, 1)), (3, (1, 0), (1, 3))),
    ((0, (2, 0), (3, 0)), (1, (7, 0), (6, 0)), (2, (0, 1), (0, 2)), (3, (7, 0), (7, 3))),
    ((0, (1, 3), (2, 3)), (1, (7, 1), (6, 1)), (2, (7, 1), (7, 2)), (3, (1, 3), (1, 2))),
    ((0, (3, 0), (4, 0)), (1, (6, 0), (5, 0)), (2, (3, 0), (3, 1)), (3, (6, 0), (6, 3))),
    ((0, (2, 3), (3, 3)), (1, (6, 1), (5, 1)), (2, (6, 1), (6, 2)), (3, (2, 3), (2, 2))),
    ((0, (3, 1), (4, 1)), (1, (3, 1), (2, 1)), (2, (3, 1), (3, 2)), (3, (4, 0), (4, 3))),
    ((0, (3, 2), (4, 2)), (2, (5, 1), (5, 2)), (3, (5, 0), (5, 3))),
)


def step_pairs(direction):
    dz, dy = direction
    return [
        (z * NY + y, ((z + dz) % NZ) * NY + (y + dy) % NY) for z in range(NZ) for y in range(NY)
    ]


def place_kernel(slots, rows, *refs):
    pieces, table, sems = refs[: len(slots)], refs[-2], refs[-1]
    copies = [
        pltpu.make_async_copy(piece, table.at[pl.ds(slot * rows, rows)], sems.at[n])
        for n, (slot, piece) in enumerate(zip(slots, pieces))
    ]
    for copy in copies:
        copy.start()
    for copy in copies:
        copy.wait()


def place_pieces(table, slots, pieces):
    rows = pieces[0].shape[0]
    shape = (NZ * NY * rows,) + pieces[0].shape[1:]
    held = [] if table is None else [table]
    count = len(pieces)
    return pl.pallas_call(
        functools.partial(place_kernel, slots, rows),
        out_shape=pltpu.HBM(shape, pieces[0].dtype),
        in_specs=[pl.BlockSpec(memory_space=pltpu.VMEM)] * count
        + [pl.BlockSpec(memory_space=pltpu.HBM)] * len(held),
        out_specs=pl.BlockSpec(memory_space=pltpu.HBM),
        scratch_shapes=[pltpu.SemaphoreType.DMA((count,))],
        input_output_aliases={count: 0} if held else {},
        compiler_params=pltpu.CompilerParams(vmem_limit_bytes=8 << 20),
        cost_estimate=pl.CostEstimate(
            flops=0, bytes_accessed=2 * count * rows * 512, transcendentals=0
        ),
        name="place",
    )(*pieces, *held)


def slot_of(name):
    return name[0] * NY + name[1]


def spread_shard(own):
    pieces = {(0, 0): own}
    table = place_pieces(None, [0], [own])
    waiting = []
    for step in SPREAD:
        sources = sorted({source for _, source, _ in step})
        kept = lax.optimization_barrier(([pieces[source] for source in sources], table))
        ready, table = dict(zip(sources, kept[0])), kept[1]
        for way, source, target in step:
            pieces[target] = lax.ppermute(ready[source], "row", step_pairs(DIRECTIONS[way]))
        waiting.append([target for _, _, target in step])
        if len(waiting) >= LAG and step is not SPREAD[-1]:
            names = waiting.pop(0)
            table = place_pieces(table, [slot_of(n) for n in names], [pieces[n] for n in names])
    late = waiting[0] + waiting[1]
    return table, [slot_of(n) for n in late], [pieces[n] for n in late]


def gather_kernel(count, parts, copies, hand_on, index, *refs):
    outs = 2 if hand_on else 1
    found, table, load_sems, sems, on_sem = refs[-5:]
    out = refs[-5 - outs]

    loads = [
        pltpu.make_async_copy(
            refs[operand].at[pl.ds(start, rows)], table.at[pl.ds(to, rows)], load_sems.at[n]
        )
        for n, (operand, start, rows, to) in enumerate(copies)
    ]
    for copy in loads:
        copy.start()
    for copy in loads:
        copy.wait()
    leaving = []
    if hand_on:
        leaving.append(pltpu.make_async_copy(table.at[pl.ds(0, hand_on)], refs[-6], on_sem))
        leaving[0].start()
    unroll = 64
    size = count // parts
    for part in range(parts):

        def some(i, carry):
            first = part * size + i * unroll
            for u in range(unroll):
                found[first + u] = table[index[first + u]]
            return carry

        lax.fori_loop(0, size // unroll, some, 0)
        span = pl.ds(part * size, size)
        leaving.append(pltpu.make_async_copy(found.at[span], out.at[span], sems.at[part]))
        leaving[-1].start()
    for copy in leaving:
        copy.wait()


def gather_rows(index, operands, spaces, copies, name, hand_on=0):
    count = index.shape[0]
    parts = 8
    total = max(to + rows for _, _, rows, to in copies)
    shapes = [pltpu.HBM((count, 2, 128), jnp.bfloat16)]
    if hand_on:
        shapes.append(pltpu.HBM((hand_on, 2, 128), jnp.bfloat16))
    return pl.pallas_call(
        functools.partial(gather_kernel, count, parts, copies, hand_on),
        out_shape=shapes,
        grid_spec=pltpu.PrefetchScalarGridSpec(
            num_scalar_prefetch=1,
            grid=(),
            in_specs=[pl.BlockSpec(memory_space=space) for space in spaces],
            out_specs=[pl.BlockSpec(memory_space=pltpu.HBM)] * len(shapes),
            scratch_shapes=[
                pltpu.VMEM((count, 2, 128), jnp.bfloat16),
                pltpu.VMEM((total, 2, 128), jnp.bfloat16),
                pltpu.SemaphoreType.DMA((len(copies),)),
                pltpu.SemaphoreType.DMA((parts,)),
                pltpu.SemaphoreType.DMA,
            ],
        ),
        compiler_params=pltpu.CompilerParams(vmem_limit_bytes=24 << 20),
        cost_estimate=pl.CostEstimate(
            flops=0, bytes_accessed=2 * (total + count) * 512, transcendentals=0
        ),
        name=name,
    )(
        index,
        *[
            pltpu.with_memory_space_constraint(operand, pltpu.HBM) if space == pltpu.HBM else operand
            for operand, space in zip(operands, spaces)
        ],
    )


def pair_kernel(
    me_ref, local_hbm, other_hbm, out_ref, local_ref, other_ref, total_ref, sums_ref, sems
):
    me = me_ref[0]
    copies = [
        [
            pltpu.make_async_copy(source.at[a], target.at[a], sems.at[n, a])
            for n, (source, target) in enumerate(((local_hbm, local_ref), (other_hbm, other_ref)))
        ]
        for a in range(GROUPS)
    ]
    for pair in copies:
        for copy in pair:
            copy.start()
    rows = 2 * HALF
    lane = lax.broadcasted_iota(jnp.int32, (CHUNK, 128), 1)
    block = lane // 32
    unit = lane // 16
    inner = lane % 16
    i, j = inner // PER, inner % PER
    depth = lax.broadcasted_iota(jnp.int32, (512, 128), 0)
    column = lax.broadcasted_iota(jnp.int32, (512, 128), 1)
    turn = depth // 128
    second = (depth % 128) // 32
    place = ((second + turn) % PER) * PER + second
    collect = jnp.where(column % 16 == place, 1.0, 0.0).astype(jnp.bfloat16)
    odd = block % 2 == 1
    upper = block >= 2
    outer = (block == 0) | (block == 3)

    def turned(tiles):
        even_low = jnp.where(odd, tiles[1], tiles[0])
        even_high = jnp.where(odd, tiles[3], tiles[2])
        odd_low = jnp.where(odd, tiles[0], tiles[1])
        odd_high = jnp.where(odd, tiles[2], tiles[3])
        return (
            jnp.where(upper, even_high, even_low),
            jnp.where(outer, odd_low, odd_high),
            jnp.where(upper, even_low, even_high),
            jnp.where(outer, odd_high, odd_low),
        )

    def products(first, second):
        high, low = [], []
        lefts, rights = turned(first), turned(second)
        for d in range(PER):
            right = rights[-d % PER]
            if d:
                right = pltpu.roll(right, 128 - 32 * d, 1)
            value = lefts[d] * right
            rounded = value.astype(jnp.bfloat16)
            high.append(rounded)
            low.append((value - rounded.astype(jnp.float32)).astype(jnp.bfloat16))
        high = jnp.concatenate(high, axis=1)
        low = jnp.concatenate(low, axis=1)
        return jnp.dot(high, collect, preferred_element_type=jnp.float32) + jnp.dot(
            low, collect, preferred_element_type=jnp.float32
        )

    def tiles(ref, a, span):
        return [ref[a, n, span, :].astype(jnp.float32) for n in range(PER)]

    for a in range(GROUPS):
        for copy in copies[a]:
            copy.wait()

        for r in range(rows // CHUNK):
            span = pl.ds(r * CHUNK, CHUNK)
            dots = products(tiles(local_ref, a, span), tiles(other_ref, a, span))
            total_ref[span, :] = jnp.where(unit == a, dots, total_ref[span, :])

    for r in range(rows // CHUNK):
        span = pl.ds(r * CHUNK, CHUNK)
        own_first = tiles(other_ref, me, span)
        own_second = tiles(local_ref, me, span)
        first_dots = products(own_first, own_first)
        second_dots = products(own_second, own_second)
        total = total_ref[span, :]
        sums_ref[0, span, :] = jnp.where(
            unit < me, total, jnp.where((unit == me) & (i < j), first_dots, 0.0)
        )
        sums_ref[1, span, :] = jnp.where(
            unit > me, total, jnp.where((unit == me) & (i > j), second_dots, 0.0)
        )
    for half in range(2):
        value = sums_ref[half, pl.ds(0, HALF, stride=2), :] + sums_ref[
            half, pl.ds(1, HALF, stride=2), :
        ]
        out_ref[pl.ds(half * HALF, HALF), :] = value.astype(jnp.bfloat16)


def pair_products(me, local, other):
    return pl.pallas_call(
        pair_kernel,
        out_shape=jax.ShapeDtypeStruct((2 * HALF, 128), jnp.bfloat16),
        grid_spec=pltpu.PrefetchScalarGridSpec(
            num_scalar_prefetch=1,
            grid=(),
            in_specs=[
                pl.BlockSpec(memory_space=pltpu.HBM),
                pl.BlockSpec(memory_space=pl.ANY),
            ],
            out_specs=pl.BlockSpec(memory_space=pltpu.VMEM),
            scratch_shapes=[
                pltpu.VMEM((GROUPS, PER, 2 * HALF, 128), jnp.bfloat16),
                pltpu.VMEM((GROUPS, PER, 2 * HALF, 128), jnp.bfloat16),
                pltpu.VMEM((2 * HALF, 128), jnp.float32),
                pltpu.VMEM((2, 2 * HALF, 128), jnp.float32),
                pltpu.SemaphoreType.DMA((2, GROUPS)),
            ],
        ),
        compiler_params=pltpu.CompilerParams(vmem_limit_bytes=16 << 20),
        name="pair_products",
    )(
        me,
        pltpu.with_memory_space_constraint(local, pltpu.HBM),
        other,
    )


def network_kernel(dots_ref, first_hbm, hidden_hbm, out_weights_ref, out_ref, first, hidden, sems):
    layers = hidden.shape[0]
    size = hidden.shape[1] // GROUPS
    first_size = first.shape[0] // GROUPS
    first_copies = [
        pltpu.make_async_copy(
            first_hbm.at[pl.ds(b * first_size, first_size)],
            first.at[pl.ds(b * first_size, first_size)],
            sems.at[layers, b],
        )
        for b in range(GROUPS)
    ]
    hidden_copies = [
        [
            pltpu.make_async_copy(
                hidden_hbm.at[depth, pl.ds(b * size, size)],
                hidden.at[depth, pl.ds(b * size, size)],
                sems.at[depth, b],
            )
            for b in range(GROUPS)
        ]
        for depth in range(layers)
    ]
    for copies in [first_copies] + hidden_copies:
        for copy in copies:
            copy.start()

    def rounded(value):
        return jnp.maximum(value, 0.0).astype(jnp.bfloat16)

    samples = dots_ref.shape[1]
    value = jnp.zeros((samples, H), jnp.float32)
    for b in range(GROUPS):
        first_copies[b].wait()
        value = value + jnp.dot(
            dots_ref[b],
            first[pl.ds(b * first_size, first_size), :],
            preferred_element_type=jnp.float32,
        )
    units = rounded(value)
    for depth in range(layers):
        value = jnp.zeros((samples, H), jnp.float32)
        for b in range(GROUPS):
            hidden_copies[depth][b].wait()
            value = value + jnp.dot(
                units[:, b * size : (b + 1) * size],
                hidden[depth, pl.ds(b * size, size), :],
                preferred_element_type=jnp.float32,
            )
        units = rounded(value)
    product = units.astype(jnp.float32) * out_weights_ref[...].astype(jnp.float32)
    total = jnp.sum(product, axis=1, keepdims=True)
    lane = lax.broadcasted_iota(jnp.int32, (samples, 128), 1)
    sample = lax.broadcasted_iota(jnp.int32, (samples, 128), 0)
    logits = jnp.sum(jnp.where(lane == sample, total, 0.0), axis=0, keepdims=True)
    out_ref[...] = jnp.broadcast_to(logits, out_ref.shape)


def network(dots, first, hidden, out_weights):
    return pl.pallas_call(
        network_kernel,
        out_shape=jax.ShapeDtypeStruct((GROUPS, 128), jnp.float32),
        in_specs=[
            pl.BlockSpec(memory_space=pltpu.VMEM),
            pl.BlockSpec(memory_space=pltpu.HBM),
            pl.BlockSpec(memory_space=pltpu.HBM),
            pl.BlockSpec(memory_space=pltpu.VMEM),
        ],
        out_specs=pl.BlockSpec(memory_space=pltpu.VMEM),
        scratch_shapes=[
            pltpu.VMEM(first.shape, first.dtype),
            pltpu.VMEM(hidden.shape, hidden.dtype),
            pltpu.SemaphoreType.DMA((hidden.shape[0] + 1, GROUPS)),
        ],
        compiler_params=pltpu.CompilerParams(vmem_limit_bytes=26 << 20),
        name="network",
    )(
        dots,
        pltpu.with_memory_space_constraint(first, pltpu.HBM),
        pltpu.with_memory_space_constraint(hidden, pltpu.HBM),
        out_weights,
    )


def body(row_owner, row_slot, feature_table, w_first, w_hidden, w_out):
    samples = row_slot.shape[0]
    rows = feature_table.shape[0]
    me = lax.axis_index("field")
    mine = lax.axis_index("row")

    source = jnp.arange(2 * 128, dtype=jnp.int32)
    wanted = (source % 128) // 32 * K + source // 128 * 32 + source % 32
    reorder = (source[:, None] == wanted[None, :]).astype(jnp.bfloat16)
    packed = jnp.dot(feature_table, reorder, preferred_element_type=jnp.float32)
    packed = packed.astype(jnp.bfloat16).reshape(rows, 2, 128)
    table, late_slots, late = spread_shard(packed)

    full_hidden = lax.all_gather(w_hidden, "field", axis=1, tiled=True)

    owner = row_owner[:, :, 0]
    piece = (mine // NY - owner // NY) % NZ * NY + (mine % NY - owner % NY) % NY
    late_rows = len(late) * rows
    place = jnp.full_like(piece, -1)
    for n, slot in enumerate(late_slots):
        place = jnp.where(piece == slot, n, place)

    early = (me <= jnp.arange(GROUPS, dtype=jnp.int32))[:, None, None]

    def in_order(values, sent):
        halves = values.T.reshape(GROUPS, PER, 2, HALF)
        one, two = (halves[:, :, 0], halves[:, :, 1]) if sent else (halves[:, :, 1], halves[:, :, 0])
        return jnp.where(early, one, two).reshape(-1)

    ids = piece * rows + row_slot
    early_ids = in_order(jnp.where(place < 0, ids, 0), True)
    late_ids = in_order(jnp.where(place < 0, -1, place * rows + row_slot), True)
    number = late_ids.shape[0]
    late_ids = jnp.where(
        late_ids < 0, late_rows + jnp.arange(number, dtype=jnp.int32), late_ids
    )
    local_ids = in_order(ids, False)

    table, full_hidden = lax.optimization_barrier((table, full_hidden))

    early_slots = [slot for slot in range(NZ * NY) if slot not in late_slots]
    (partly,) = gather_rows(
        early_ids,
        [table],
        [pltpu.HBM],
        [(0, slot * rows, rows, slot * rows) for slot in early_slots],
        "gather_early",
    )
    quarter = number // 4
    sent, late_table = gather_rows(
        late_ids,
        list(late) + [partly],
        [pl.ANY] * len(late) + [pltpu.HBM],
        [(n, 0, rows, n * rows) for n in range(len(late))]
        + [
            (len(late), n * quarter, quarter, late_rows + n * quarter) for n in range(4)
        ],
        "gather_sent",
        hand_on=late_rows,
    )
    other = lax.all_to_all(
        sent.reshape(GROUPS, PER * HALF, 2, 128), "field", split_axis=0, concat_axis=0, tiled=True
    )
    (local,) = gather_rows(
        local_ids,
        [table, late_table],
        [pltpu.HBM] * 2,
        [(0, slot * rows, rows, slot * rows) for slot in early_slots]
        + [(1, n * rows, rows, slot * rows) for n, slot in enumerate(late_slots)],
        "gather_local",
    )
    local, w_pairs = lax.optimization_barrier((local, w_first))

    col = jnp.arange(F * F, dtype=jnp.int32)
    b, a, i, j = col // 128, col // 16 % 8, col // 4 % 4, col % 4
    forward = (a * PER + i) * F + b * PER + j
    backward = (b * PER + j) * F + a * PER + i
    rows_of = jnp.where(me < GROUPS // 2, forward, backward)
    first_order = (rows_of[:, None] == col[None, :]).astype(jnp.bfloat16)
    first = jnp.dot(
        first_order, w_pairs.reshape(F * F, H), preferred_element_type=jnp.float32
    ).astype(jnp.bfloat16)
    local, first = lax.optimization_barrier((local, first))
    dots = pair_products(
        me.reshape(1),
        local.reshape(GROUPS, PER, 2 * HALF, 128),
        other.reshape(GROUPS, PER, 2 * HALF, 128),
    )
    block = samples // GROUPS
    own_dots = lax.all_to_all(
        dots.reshape(GROUPS, block, 128), "field", split_axis=0, concat_axis=0, tiled=True
    )
    logits = network(own_dots, first, full_hidden, w_out.reshape(1, H))
    everyone = lax.all_to_all(logits, "field", split_axis=0, concat_axis=0, tiled=True)
    return everyone[:, :block].reshape(samples)


def solution(mesh):
    placed = (
        P("row", None, None),
        P("row", None),
        P("row", "field"),
        P(),
        P(None, "field", None),
        P(),
    )
    return jax.shard_map(body, mesh=mesh, in_specs=placed, out_specs=P("row"), check_vma=False)
```

```python
import functools

import jax
import jax.numpy as jnp
from jax import lax
from jax.experimental import pallas as pl
from jax.experimental.pallas import tpu as pltpu
from jax.sharding import PartitionSpec as P

F = 32
K = 64
H = 2048
NZ = 8
NY = 4
GROUPS = 8
PER = 4
HALF = 128
LAG = 2
CHUNK = 128

DIRECTIONS = ((1, 0), (-1, 0), (0, 1), (0, -1))
SPREAD = (
    ((0, (0, 0), (1, 0)), (1, (0, 0), (7, 0)), (2, (0, 0), (0, 1)), (3, (0, 0), (0, 3))),
    ((0, (1, 0), (2, 0)), (1, (0, 1), (7, 1)), (2, (1, 0), (1, 1)), (3, (1, 0), (1, 3))),
    ((0, (2, 0), (3, 0)), (1, (7, 0), (6, 0)), (2, (0, 1), (0, 2)), (3, (7, 0), (7, 3))),
    ((0, (1, 3), (2, 3)), (1, (7, 1), (6, 1)), (2, (7, 1), (7, 2)), (3, (1, 3), (1, 2))),
    ((0, (3, 0), (4, 0)), (1, (6, 0), (5, 0)), (2, (3, 0), (3, 1)), (3, (6, 0), (6, 3))),
    ((0, (2, 3), (3, 3)), (1, (6, 1), (5, 1)), (2, (6, 1), (6, 2)), (3, (2, 3), (2, 2))),
    ((0, (3, 1), (4, 1)), (1, (3, 1), (2, 1)), (2, (3, 1), (3, 2)), (3, (4, 0), (4, 3))),
    ((0, (3, 2), (4, 2)), (2, (5, 1), (5, 2)), (3, (5, 0), (5, 3))),
)


def step_pairs(direction):
    dz, dy = direction
    return [
        (z * NY + y, ((z + dz) % NZ) * NY + (y + dy) % NY) for z in range(NZ) for y in range(NY)
    ]


def place_kernel(slots, rows, *refs):
    pieces, table, sems = refs[: len(slots)], refs[-2], refs[-1]
    copies = [
        pltpu.make_async_copy(piece, table.at[pl.ds(slot * rows, rows)], sems.at[n])
        for n, (slot, piece) in enumerate(zip(slots, pieces))
    ]
    for copy in copies:
        copy.start()
    for copy in copies:
        copy.wait()


def place_pieces(table, slots, pieces):
    rows = pieces[0].shape[0]
    shape = (NZ * NY * rows,) + pieces[0].shape[1:]
    held = [] if table is None else [table]
    count = len(pieces)
    return pl.pallas_call(
        functools.partial(place_kernel, slots, rows),
        out_shape=pltpu.HBM(shape, pieces[0].dtype),
        in_specs=[pl.BlockSpec(memory_space=pltpu.VMEM)] * count
        + [pl.BlockSpec(memory_space=pltpu.HBM)] * len(held),
        out_specs=pl.BlockSpec(memory_space=pltpu.HBM),
        scratch_shapes=[pltpu.SemaphoreType.DMA((count,))],
        input_output_aliases={count: 0} if held else {},
        compiler_params=pltpu.CompilerParams(vmem_limit_bytes=8 << 20),
        cost_estimate=pl.CostEstimate(
            flops=0, bytes_accessed=2 * count * rows * 512, transcendentals=0
        ),
        name="place",
    )(*pieces, *held)


def slot_of(name):
    return name[0] * NY + name[1]


def spread_shard(own):
    pieces = {(0, 0): own}
    table = None
    waiting = []
    for step in SPREAD:
        sources = sorted({source for _, source, _ in step})
        ready = {source: pieces[source] for source in sources}
        if table is not None:
            kept = lax.optimization_barrier(([ready[source] for source in sources], table))
            ready, table = dict(zip(sources, kept[0])), kept[1]
        for way, source, target in step:
            pieces[target] = lax.ppermute(ready[source], "row", step_pairs(DIRECTIONS[way]))
        waiting.append([target for _, _, target in step])
        if len(waiting) >= LAG and step is not SPREAD[-1]:
            names = waiting.pop(0) + ([(0, 0)] if table is None else [])
            table = place_pieces(table, [slot_of(n) for n in names], [pieces[n] for n in names])
    late = waiting[0] + waiting[1]
    return table, [slot_of(n) for n in late], [pieces[n] for n in late]


def gather_kernel(count, parts, copies, hand_on, index, *refs):
    outs = 2 if hand_on else 1
    found, table, load_sems, sems, on_sem = refs[-5:]
    out = refs[-5 - outs]

    loads = [
        pltpu.make_async_copy(
            refs[operand].at[pl.ds(start, rows)], table.at[pl.ds(to, rows)], load_sems.at[n]
        )
        for n, (operand, start, rows, to) in enumerate(copies)
    ]
    for copy in loads:
        copy.start()
    for copy in loads:
        copy.wait()
    leaving = []
    if hand_on:
        leaving.append(pltpu.make_async_copy(table.at[pl.ds(0, hand_on)], refs[-6], on_sem))
        leaving[0].start()
    unroll = 64
    size = count // parts
    for part in range(parts):

        def some(i, carry):
            first = part * size + i * unroll
            for u in range(unroll):
                found[first + u] = table[index[first + u]]
            return carry

        lax.fori_loop(0, size // unroll, some, 0)
        span = pl.ds(part * size, size)
        leaving.append(pltpu.make_async_copy(found.at[span], out.at[span], sems.at[part]))
        leaving[-1].start()
    for copy in leaving:
        copy.wait()


def gather_rows(index, operands, spaces, copies, name, hand_on=0):
    count = index.shape[0]
    parts = 8
    total = max(to + rows for _, _, rows, to in copies)
    shapes = [pltpu.HBM((count, 2, 128), jnp.bfloat16)]
    if hand_on:
        shapes.append(pltpu.HBM((hand_on, 2, 128), jnp.bfloat16))
    return pl.pallas_call(
        functools.partial(gather_kernel, count, parts, copies, hand_on),
        out_shape=shapes,
        grid_spec=pltpu.PrefetchScalarGridSpec(
            num_scalar_prefetch=1,
            grid=(),
            in_specs=[pl.BlockSpec(memory_space=space) for space in spaces],
            out_specs=[pl.BlockSpec(memory_space=pltpu.HBM)] * len(shapes),
            scratch_shapes=[
                pltpu.VMEM((count, 2, 128), jnp.bfloat16),
                pltpu.VMEM((total, 2, 128), jnp.bfloat16),
                pltpu.SemaphoreType.DMA((len(copies),)),
                pltpu.SemaphoreType.DMA((parts,)),
                pltpu.SemaphoreType.DMA,
            ],
        ),
        compiler_params=pltpu.CompilerParams(vmem_limit_bytes=24 << 20),
        cost_estimate=pl.CostEstimate(
            flops=0, bytes_accessed=2 * (total + count) * 512, transcendentals=0
        ),
        name=name,
    )(
        index,
        *[
            pltpu.with_memory_space_constraint(operand, pltpu.HBM) if space == pltpu.HBM else operand
            for operand, space in zip(operands, spaces)
        ],
    )


def pair_kernel(
    me_ref, local_hbm, other_hbm, out_ref, local_ref, other_ref, total_ref, sums_ref, sems
):
    me = me_ref[0]
    copies = [
        [
            pltpu.make_async_copy(source.at[a], target.at[a], sems.at[n, a])
            for n, (source, target) in enumerate(((local_hbm, local_ref), (other_hbm, other_ref)))
        ]
        for a in range(GROUPS)
    ]
    for pair in copies:
        for copy in pair:
            copy.start()
    rows = 2 * HALF
    lane = lax.broadcasted_iota(jnp.int32, (CHUNK, 128), 1)
    block = lane // 32
    unit = lane // 16
    inner = lane % 16
    i, j = inner // PER, inner % PER
    depth = lax.broadcasted_iota(jnp.int32, (512, 128), 0)
    column = lax.broadcasted_iota(jnp.int32, (512, 128), 1)
    turn = depth // 128
    second = (depth % 128) // 32
    place = ((second + turn) % PER) * PER + second
    collect = jnp.where(column % 16 == place, 1.0, 0.0).astype(jnp.bfloat16)
    odd = block % 2 == 1
    upper = block >= 2
    outer = (block == 0) | (block == 3)

    def turned(tiles):
        even_low = jnp.where(odd, tiles[1], tiles[0])
        even_high = jnp.where(odd, tiles[3], tiles[2])
        odd_low = jnp.where(odd, tiles[0], tiles[1])
        odd_high = jnp.where(odd, tiles[2], tiles[3])
        return (
            jnp.where(upper, even_high, even_low),
            jnp.where(outer, odd_low, odd_high),
            jnp.where(upper, even_low, even_high),
            jnp.where(outer, odd_high, odd_low),
        )

    def products(first, second):
        high, low = [], []
        lefts, rights = turned(first), turned(second)
        for d in range(PER):
            right = rights[-d % PER]
            if d:
                right = pltpu.roll(right, 128 - 32 * d, 1)
            value = lefts[d] * right
            rounded = value.astype(jnp.bfloat16)
            high.append(rounded)
            low.append((value - rounded.astype(jnp.float32)).astype(jnp.bfloat16))
        high = jnp.concatenate(high, axis=1)
        low = jnp.concatenate(low, axis=1)
        return jnp.dot(high, collect, preferred_element_type=jnp.float32) + jnp.dot(
            low, collect, preferred_element_type=jnp.float32
        )

    def tiles(ref, a, span):
        return [ref[a, n, span, :].astype(jnp.float32) for n in range(PER)]

    for a in range(GROUPS):
        for copy in copies[a]:
            copy.wait()

        for r in range(rows // CHUNK):
            span = pl.ds(r * CHUNK, CHUNK)
            dots = products(tiles(local_ref, a, span), tiles(other_ref, a, span))
            total_ref[span, :] = jnp.where(unit == a, dots, total_ref[span, :])

    for r in range(rows // CHUNK):
        span = pl.ds(r * CHUNK, CHUNK)
        own_first = tiles(other_ref, me, span)
        own_second = tiles(local_ref, me, span)
        first_dots = products(own_first, own_first)
        second_dots = products(own_second, own_second)
        total = total_ref[span, :]
        sums_ref[0, span, :] = jnp.where(
            unit < me, total, jnp.where((unit == me) & (i < j), first_dots, 0.0)
        )
        sums_ref[1, span, :] = jnp.where(
            unit > me, total, jnp.where((unit == me) & (i > j), second_dots, 0.0)
        )
    for half in range(2):
        value = sums_ref[half, pl.ds(0, HALF, stride=2), :] + sums_ref[
            half, pl.ds(1, HALF, stride=2), :
        ]
        out_ref[pl.ds(half * HALF, HALF), :] = value.astype(jnp.bfloat16)


def pair_products(me, local, other):
    return pl.pallas_call(
        pair_kernel,
        out_shape=jax.ShapeDtypeStruct((2 * HALF, 128), jnp.bfloat16),
        grid_spec=pltpu.PrefetchScalarGridSpec(
            num_scalar_prefetch=1,
            grid=(),
            in_specs=[
                pl.BlockSpec(memory_space=pltpu.HBM),
                pl.BlockSpec(memory_space=pl.ANY),
            ],
            out_specs=pl.BlockSpec(memory_space=pltpu.VMEM),
            scratch_shapes=[
                pltpu.VMEM((GROUPS, PER, 2 * HALF, 128), jnp.bfloat16),
                pltpu.VMEM((GROUPS, PER, 2 * HALF, 128), jnp.bfloat16),
                pltpu.VMEM((2 * HALF, 128), jnp.float32),
                pltpu.VMEM((2, 2 * HALF, 128), jnp.float32),
                pltpu.SemaphoreType.DMA((2, GROUPS)),
            ],
        ),
        compiler_params=pltpu.CompilerParams(vmem_limit_bytes=16 << 20),
        name="pair_products",
    )(
        me,
        pltpu.with_memory_space_constraint(local, pltpu.HBM),
        other,
    )


def network_kernel(dots_ref, first_hbm, hidden_hbm, out_weights_ref, out_ref, first, hidden, sems):
    layers = hidden.shape[0]
    size = hidden.shape[1] // GROUPS
    first_size = first.shape[0] // GROUPS
    first_copies = [
        pltpu.make_async_copy(
            first_hbm.at[pl.ds(b * first_size, first_size)],
            first.at[pl.ds(b * first_size, first_size)],
            sems.at[layers, b],
        )
        for b in range(GROUPS)
    ]
    hidden_copies = [
        [
            pltpu.make_async_copy(
                hidden_hbm.at[depth, pl.ds(b * size, size)],
                hidden.at[depth, pl.ds(b * size, size)],
                sems.at[depth, b],
            )
            for b in range(GROUPS)
        ]
        for depth in range(layers)
    ]
    for copies in [first_copies] + hidden_copies:
        for copy in copies:
            copy.start()

    def rounded(value):
        return jnp.maximum(value, 0.0).astype(jnp.bfloat16)

    samples = dots_ref.shape[1]
    value = jnp.zeros((samples, H), jnp.float32)
    for b in range(GROUPS):
        first_copies[b].wait()
        value = value + jnp.dot(
            dots_ref[b],
            first[pl.ds(b * first_size, first_size), :],
            preferred_element_type=jnp.float32,
        )
    units = rounded(value)
    for depth in range(layers):
        value = jnp.zeros((samples, H), jnp.float32)
        for b in range(GROUPS):
            hidden_copies[depth][b].wait()
            value = value + jnp.dot(
                units[:, b * size : (b + 1) * size],
                hidden[depth, pl.ds(b * size, size), :],
                preferred_element_type=jnp.float32,
            )
        units = rounded(value)
    product = units.astype(jnp.float32) * out_weights_ref[...].astype(jnp.float32)
    total = jnp.sum(product, axis=1, keepdims=True)
    lane = lax.broadcasted_iota(jnp.int32, (samples, 128), 1)
    sample = lax.broadcasted_iota(jnp.int32, (samples, 128), 0)
    logits = jnp.sum(jnp.where(lane == sample, total, 0.0), axis=0, keepdims=True)
    out_ref[...] = jnp.broadcast_to(logits, out_ref.shape)


def network(dots, first, hidden, out_weights):
    return pl.pallas_call(
        network_kernel,
        out_shape=jax.ShapeDtypeStruct((GROUPS, 128), jnp.float32),
        in_specs=[
            pl.BlockSpec(memory_space=pltpu.VMEM),
            pl.BlockSpec(memory_space=pltpu.HBM),
            pl.BlockSpec(memory_space=pltpu.HBM),
            pl.BlockSpec(memory_space=pltpu.VMEM),
        ],
        out_specs=pl.BlockSpec(memory_space=pltpu.VMEM),
        scratch_shapes=[
            pltpu.VMEM(first.shape, first.dtype),
            pltpu.VMEM(hidden.shape, hidden.dtype),
            pltpu.SemaphoreType.DMA((hidden.shape[0] + 1, GROUPS)),
        ],
        compiler_params=pltpu.CompilerParams(vmem_limit_bytes=26 << 20),
        name="network",
    )(
        dots,
        pltpu.with_memory_space_constraint(first, pltpu.HBM),
        pltpu.with_memory_space_constraint(hidden, pltpu.HBM),
        out_weights,
    )


def body(row_owner, row_slot, feature_table, w_first, w_hidden, w_out):
    samples = row_slot.shape[0]
    rows = feature_table.shape[0]
    me = lax.axis_index("field")
    mine = lax.axis_index("row")

    source = jnp.arange(2 * 128, dtype=jnp.int32)
    wanted = (source % 128) // 32 * K + source // 128 * 32 + source % 32
    reorder = (source[:, None] == wanted[None, :]).astype(jnp.bfloat16)
    packed = jnp.dot(feature_table, reorder, preferred_element_type=jnp.float32)
    packed = packed.astype(jnp.bfloat16).reshape(rows, 2, 128)
    table, late_slots, late = spread_shard(packed)

    full_hidden = lax.all_gather(w_hidden, "field", axis=1, tiled=True)

    owner = row_owner[:, :, 0]
    piece = (mine // NY - owner // NY) % NZ * NY + (mine % NY - owner % NY) % NY
    late_rows = len(late) * rows
    place = jnp.full_like(piece, -1)
    for n, slot in enumerate(late_slots):
        place = jnp.where(piece == slot, n, place)

    early = (me <= jnp.arange(GROUPS, dtype=jnp.int32))[:, None, None]

    def in_order(values, sent):
        halves = values.T.reshape(GROUPS, PER, 2, HALF)
        one, two = (halves[:, :, 0], halves[:, :, 1]) if sent else (halves[:, :, 1], halves[:, :, 0])
        return jnp.where(early, one, two).reshape(-1)

    ids = piece * rows + row_slot
    early_ids = in_order(jnp.where(place < 0, ids, 0), True)
    late_ids = in_order(jnp.where(place < 0, -1, place * rows + row_slot), True)
    number = late_ids.shape[0]
    late_ids = jnp.where(
        late_ids < 0, late_rows + jnp.arange(number, dtype=jnp.int32), late_ids
    )
    local_ids = in_order(ids, False)

    table, full_hidden = lax.optimization_barrier((table, full_hidden))

    early_slots = [slot for slot in range(NZ * NY) if slot not in late_slots]
    (partly,) = gather_rows(
        early_ids,
        [table],
        [pltpu.HBM],
        [(0, slot * rows, rows, slot * rows) for slot in early_slots],
        "gather_early",
    )
    quarter = number // 4
    sent, late_table = gather_rows(
        late_ids,
        list(late) + [partly],
        [pl.ANY] * len(late) + [pltpu.HBM],
        [(n, 0, rows, n * rows) for n in range(len(late))]
        + [
            (len(late), n * quarter, quarter, late_rows + n * quarter) for n in range(4)
        ],
        "gather_sent",
        hand_on=late_rows,
    )
    other = lax.all_to_all(
        sent.reshape(GROUPS, PER * HALF, 2, 128), "field", split_axis=0, concat_axis=0, tiled=True
    )
    (local,) = gather_rows(
        local_ids,
        [table, late_table],
        [pltpu.HBM] * 2,
        [(0, slot * rows, rows, slot * rows) for slot in early_slots]
        + [(1, n * rows, rows, slot * rows) for n, slot in enumerate(late_slots)],
        "gather_local",
    )
    local, w_pairs = lax.optimization_barrier((local, w_first))

    col = jnp.arange(F * F, dtype=jnp.int32)
    b, a, i, j = col // 128, col // 16 % 8, col // 4 % 4, col % 4
    forward = (a * PER + i) * F + b * PER + j
    backward = (b * PER + j) * F + a * PER + i
    rows_of = jnp.where(me < GROUPS // 2, forward, backward)
    first_order = (rows_of[:, None] == col[None, :]).astype(jnp.bfloat16)
    first = jnp.dot(
        first_order, w_pairs.reshape(F * F, H), preferred_element_type=jnp.float32
    ).astype(jnp.bfloat16)
    local, first = lax.optimization_barrier((local, first))
    dots = pair_products(
        me.reshape(1),
        local.reshape(GROUPS, PER, 2 * HALF, 128),
        other.reshape(GROUPS, PER, 2 * HALF, 128),
    )
    block = samples // GROUPS
    own_dots = lax.all_to_all(
        dots.reshape(GROUPS, block, 128), "field", split_axis=0, concat_axis=0, tiled=True
    )
    logits = network(own_dots, first, full_hidden, w_out.reshape(1, H))
    everyone = lax.all_to_all(logits, "field", split_axis=0, concat_axis=0, tiled=True)
    return everyone[:, :block].reshape(samples)


def solution(mesh):
    placed = (
        P("row", None, None),
        P("row", None),
        P("row", "field"),
        P(),
        P(None, "field", None),
        P(),
    )
    return jax.shard_map(body, mesh=mesh, in_specs=placed, out_specs=P("row"), check_vma=False)
```
